32 devices in a mesh: blk: 8 (over z, y), grp: 4 (over x, core).
Axes of the slice: x: 2, y: 2, z: 4, core: 2. Of those that a mesh axis runs over, the one named last changes fastest.
Arguments:
- embeddings: bfloat16 [4, 4096, 1024], P('grp', 'blk'), may hold values from -12 to 12
- strata: int32 [4, 4096], P('grp', 'blk'), may hold values from 0 to 127, as said below
- centroids: bfloat16 [4, 128, 1024], P('grp', 'blk'), may hold values from -12 to 12
Outputs:
- probs: float32 [4, 4096], P('grp', 'blk')
The draws below stay inside these ranges and needn't reach their ends.
Inputs may be any that keep to these rules, and one draw needn't show every extreme that they name: `strata`: within each aligned run of 512 rows of a collection the stratum ids never fall; within each range of 16 consecutive ids the smallest are about four times as common as the largest. `strata`: in each aligned run of 512 rows, at most 128 rows have ids in one range k * 16 to (k + 1) * 16 - 1, and exactly 128 in some range.
All inputs are finite; a program needn't handle non-finite values.
Results may differ from the reference program's by a relative error of at most 0.0014.
Values may be sent and summed in bfloat16 or wider, within the bound.
No kernel may reach another device: no remote copies, remote signals or barrier semaphores. Data moves between devices by JAX's collectives and lax.ppermute only.
A program may use at most 64 MiB of HBM per device.

```python
import math
import jax
import jax.numpy as jnp
from jax import lax

D = 1024
ROW_DEV = 512
STR_DEV = 16
COLS = 4
COLROWS = 4096
STRATA = 128


def sample_strata(key):
    owners_count = COLROWS // ROW_DEV
    blocks = COLS * owners_count
    mean_count = ROW_DEV // owners_count
    half = owners_count // 2
    block_key_rows = jax.random.split(jax.random.fold_in(key, 11), blocks)
    order = jax.vmap(lambda one_key: jax.random.permutation(one_key, owners_count))(block_key_rows).astype(jnp.int32)
    spread = jax.random.randint(jax.random.fold_in(key, 12), (blocks, half), 0, mean_count + 1)
    spread = spread.at[:, 0].set(mean_count)
    counts = jnp.stack([mean_count + spread, mean_count - spread], axis=-1).reshape(blocks, owners_count)
    ends = jnp.cumsum(counts, axis=-1)
    positions = jnp.arange(ROW_DEV, dtype=jnp.int32)
    place = jnp.sum((positions[None, :, None] >= ends[:, None, :]).astype(jnp.int32), axis=-1)
    owner = jnp.take_along_axis(order, place, axis=-1)
    first = jax.random.randint(jax.random.fold_in(key, 13), (blocks, ROW_DEV), 0, STR_DEV)
    second = jax.random.randint(jax.random.fold_in(key, 14), (blocks, ROW_DEV), 0, STR_DEV)
    third = jax.random.randint(jax.random.fold_in(key, 15), (blocks, ROW_DEV), 0, STR_DEV)
    coin = jax.random.randint(jax.random.fold_in(key, 16), (blocks, ROW_DEV), 0, 2)
    smallest = jnp.minimum(jnp.minimum(first, second), third)
    local = jnp.where(coin == 0, first, smallest)
    ids = owner * STR_DEV + local
    ordered = jnp.sort(ids, axis=-1)
    return ordered.reshape(COLS, COLROWS).astype(jnp.int32)


def stratum_directions(key):
    return jax.random.normal(jax.random.fold_in(key, 21), (COLS, STRATA, D), jnp.float32)


def draw_strata(key, part):
    return sample_strata(key)


def draw_centroids(key, part):
    unit_directions = stratum_directions(key)
    noise = jax.random.normal(jax.random.fold_in(key, 22), (COLS, STRATA, D), jnp.float32)
    return jnp.clip(unit_directions + 0.5 * noise, -12.0, 12.0).astype(jnp.bfloat16)


def draw_embeddings(key, part):
    entry_number_sequence = sample_strata(key)
    unit_directions = stratum_directions(key)
    chosen = jax.vmap(lambda table, index: table[index])(unit_directions, entry_number_sequence)
    position = jnp.arange(COLROWS, dtype=jnp.float32) / COLROWS
    jitter = jax.random.uniform(jax.random.fold_in(key, 23), (COLS, COLROWS), jnp.float32, 0.8, 1.25)
    amplitude = (0.6 + 1.4 * position)[None, :] * jitter
    noise = jax.random.normal(jax.random.fold_in(key, 24), (COLS, COLROWS, D), jnp.float32)
    return jnp.clip(amplitude[:, :, None] * chosen + noise, -12.0, 12.0).astype(jnp.bfloat16)


def setup_inputs(seed: int = 0) -> dict:
    key_of = jax.random.split(jax.random.key(seed), 4)
    embeddings = draw_embeddings(jax.random.fold_in(key_of[3], 71), 0)
    strata = draw_strata(jax.random.fold_in(key_of[3], 71), 0)
    centroids = draw_centroids(jax.random.fold_in(key_of[3], 71), 0)
    return dict(embeddings=embeddings, strata=strata, centroids=centroids)


sharpness_divisor = 0.25
base_term = 0.05
epsilon = 1e-06

def unit_rows(matrix):
    values = matrix.astype(jnp.float32)
    scaling = lax.rsqrt(lax.optimization_barrier(jnp.mean(values * values, axis=-1, keepdims=True)) + epsilon) / math.sqrt(matrix.shape[-1])
    return (values * scaling).astype(jnp.bfloat16)

def one_collection(inputs):
    emb_rows, entry_number_sequence, cent_rows = inputs
    units = unit_rows(emb_rows)
    cent_units = unit_rows(cent_rows)
    picked = cent_units[entry_number_sequence].astype(jnp.float32)
    distance = 1.0 - lax.optimization_barrier(jnp.sum(units.astype(jnp.float32) * picked, axis=-1))
    block_count = COLROWS // ROW_DEV
    query_blocks = units.reshape(block_count, ROW_DEV, D)
    query_ids = entry_number_sequence.reshape(block_count, ROW_DEV)

    def block_density(pair):
        block_rows, tile_number_sequence = pair
        logit_entries = lax.dot_general(block_rows, units, (((1,), (1,)), ((), ())), preferred_element_type=jnp.float32)
        similarity_grid = jnp.where(tile_number_sequence[:, None] == entry_number_sequence[None, :], jnp.exp((logit_entries - 1.0) / sharpness_divisor), jnp.zeros_like(logit_entries))
        return lax.optimization_barrier(jnp.sum(similarity_grid, axis=1))
    density = lax.map(block_density, (query_blocks, query_ids)).reshape(COLROWS)
    return (distance + base_term) / density

def reference(embeddings, strata, centroids):
    weights = lax.map(one_collection, (embeddings, strata, centroids))
    total = jnp.sum(weights)
    return weights * (float(COLS * COLROWS) / total)
```

```python
import functools
import math

import jax
import jax.numpy as jnp
from jax import lax
from jax.experimental import pallas as pl
from jax.experimental.pallas import tpu as pltpu
from jax.sharding import PartitionSpec as P

base_term = 0.05
epsilon = 1e-06
LANES = 128
TAIL = 16

VMEM = pl.BlockSpec(memory_space=pltpu.VMEM)
SMEM = pl.BlockSpec(memory_space=pltpu.SMEM)


def unit_values(rows):
    values = rows.astype(jnp.float32)
    mean = jnp.mean(values * values, axis=-1, keepdims=True)
    scaling = lax.rsqrt(mean + epsilon) / math.sqrt(rows.shape[-1])
    return (values * scaling).astype(jnp.bfloat16)


def first_row(ids, owner, strata_dev, last):
    return jnp.minimum(jnp.sum((ids < owner * strata_dev).astype(jnp.int32)), last)


def pack_kernel(peers, cap, strata_dev, place_ref, ids_ref, rows_ref, *rest):
    outs, held = rest[:peers], rest[peers]
    rows, width = rows_ref.shape
    step, window = 32, 2 * LANES

    def normalize(i, carry):
        at = pl.ds(pl.multiple_of(i * step, step), step)
        held[at, :] = unit_values(rows_ref[at, :])
        return carry

    lax.fori_loop(0, rows // step, normalize, 0, unroll=2)
    ids = ids_ref[...]
    ids_wide = jnp.broadcast_to(ids.astype(jnp.float32), (8, rows))
    for k, out in enumerate(outs):
        start = first_row(ids, place_ref[0] ^ k, strata_dev, rows - cap)
        base = jnp.minimum(start // LANES * LANES, rows - window)
        pick = lax.broadcasted_iota(jnp.int32, (cap, window), 1) == lax.broadcasted_iota(
            jnp.int32, (cap, window), 0
        ) + (start - base)
        run = jnp.dot(
            pick.astype(jnp.bfloat16),
            held[pl.ds(pl.multiple_of(base, LANES), window), :],
            preferred_element_type=jnp.float32,
        ).astype(jnp.bfloat16)
        for c in range(width // LANES):
            out[c * cap : (c + 1) * cap, :] = run[:, c * LANES : (c + 1) * LANES]
        turned = pltpu.roll(ids_wide, rows - start, axis=1)[:, :LANES]
        out[width // LANES * cap :, :] = jnp.concatenate([turned, turned], axis=0).astype(
            jnp.bfloat16
        )


def own_kernel(peers, cap, groups, place_ref, cent_ref, *rest):
    blocks, (out_ref, units, id_col) = rest[:peers], rest[peers:]
    slots, width = units.shape
    strata_dev = cent_ref.shape[0]
    me, group = place_ref[0], place_ref[1]
    low = (me * strata_dev).astype(jnp.float32)

    id_rows = []
    for k, block in enumerate(blocks):
        for c in range(width // LANES):
            units[k * cap : (k + 1) * cap, c * LANES : (c + 1) * LANES] = block[
                c * cap : (c + 1) * cap, :
            ]
        ids = block[width // LANES * cap :, :].astype(jnp.float32)[:1, :]
        ids = ids - low
        ids = jnp.where((ids >= 0) & (ids < strata_dev), ids, -1.0)
        id_rows.append(ids[:, :cap])
        wide = jnp.broadcast_to(ids, (LANES, LANES)).T
        id_col[k * cap : (k + 1) * cap, :] = wide[:cap, :]
    id_row = jnp.concatenate(id_rows, axis=1)
    real = id_row >= 0.0
    id_key = jnp.where(real, id_row, -2.0)

    tile = 256
    sums = jnp.zeros((8, slots), jnp.float32)
    everything = units[...]
    for t in range(slots // tile):
        scores = lax.dot_general(
            units[t * tile : (t + 1) * tile, :],
            everything,
            (((1,), (1,)), ((), ())),
            preferred_element_type=jnp.float32,
        )
        kernel = jnp.exp((scores - 1.0) * 4.0)
        same = jnp.concatenate([id_col[t * tile : (t + 1) * tile, :]] * (slots // LANES), axis=1) == id_key
        kernel = jnp.where(same, kernel, 0.0)
        sums = sums + jnp.sum(kernel.reshape(tile // 8, 8, slots), axis=0)
    density = jnp.sum(sums, axis=0, keepdims=True)

    cent_units = unit_values(cent_ref[...])
    near = lax.dot_general(
        cent_units, everything, (((1,), (1,)), ((), ())), preferred_element_type=jnp.float32
    )
    which = lax.broadcasted_iota(jnp.int32, near.shape, 0).astype(jnp.float32)
    picked = jnp.sum(jnp.where(which == id_row, near, 0.0), axis=0, keepdims=True)
    weight = jnp.where(
        real, ((1.0 - picked) + base_term) / jnp.where(real, density, 1.0), 0.0
    )
    out_ref[...] = jnp.broadcast_to(jnp.sum(weight, axis=1, keepdims=True), out_ref.shape)
    for k in range(peers):
        row = 2 * ((me ^ k) * groups + group)
        out_ref[pl.ds(row, 1), :cap] = weight[:, k * cap : (k + 1) * cap]


def finish_kernel(peers, cap, groups, strata_dev, place_ref, ids_ref, got_ref, out_ref):
    rows = ids_ref.shape[1]
    group = place_ref[1]
    got = got_ref[...]
    odd = lax.broadcasted_iota(jnp.int32, got.shape, 0) % 2
    total = jnp.sum(jnp.where(odd == 1, got, 0.0), axis=0, keepdims=True)[:, :1]
    ids = ids_ref[...]
    weight = jnp.zeros((1, rows), jnp.float32)
    for owner in range(peers):
        start = first_row(ids, owner, strata_dev, rows - cap)
        part = got_ref[pl.ds(2 * (owner * groups + group), 1), :]
        part = jnp.broadcast_to(jnp.concatenate([part] * (rows // LANES), axis=1), (8, rows))
        part = pltpu.roll(part, start, axis=1)[:1, :]
        mine = (ids >= owner * strata_dev) & (ids < (owner + 1) * strata_dev)
        weight = jnp.where(mine, part, weight)
    out_ref[...] = weight * (float(rows * peers * groups) / total)


def body(embeddings, strata, centroids):
    peers, groups = lax.axis_size("blk"), lax.axis_size("grp")
    rows, width = embeddings.shape[1:]
    strata_dev = centroids.shape[1]
    cap = 2 * rows // peers
    depth = width // LANES * cap + TAIL
    place = jnp.stack([lax.axis_index("blk"), lax.axis_index("grp")]).astype(jnp.int32)

    message = jax.ShapeDtypeStruct((depth, LANES), jnp.bfloat16)
    blocks = pl.pallas_call(
        functools.partial(pack_kernel, peers, cap, strata_dev),
        out_shape=[message] * peers,
        in_specs=[SMEM, VMEM, VMEM],
        out_specs=[VMEM] * peers,
        scratch_shapes=[pltpu.VMEM((rows, width), jnp.bfloat16)],
        name="pack",
    )(place, strata, embeddings[0])
    blocks = [blocks[0]] + [
        lax.ppermute(blocks[k], "blk", [(i, i ^ k) for i in range(peers)])
        for k in range(1, peers)
    ]
    sent = pl.pallas_call(
        functools.partial(own_kernel, peers, cap, groups),
        out_shape=jax.ShapeDtypeStruct((peers * groups * 2, LANES), jnp.float32),
        in_specs=[SMEM] + [VMEM] * (peers + 1),
        out_specs=VMEM,
        scratch_shapes=[
            pltpu.VMEM((peers * cap, width), jnp.bfloat16),
            pltpu.VMEM((peers * cap, LANES), jnp.float32),
        ],
        name="own",
    )(place, centroids[0], *blocks)
    got = lax.all_to_all(
        sent.reshape(peers * groups, 2, LANES), ("blk", "grp"), 0, 0, tiled=True
    ).reshape(peers * groups * 2, LANES)
    return pl.pallas_call(
        functools.partial(finish_kernel, peers, cap, groups, strata_dev),
        out_shape=jax.ShapeDtypeStruct((1, rows), jnp.float32),
        in_specs=[SMEM, VMEM, VMEM],
        out_specs=VMEM,
        name="finish",
    )(place, strata, got)


def solution(mesh):
    placed = (P("grp", "blk", None), P("grp", "blk"), P("grp", "blk", None))
    return jax.shard_map(
        body, mesh=mesh, in_specs=placed, out_specs=P("grp", "blk"), check_vma=False
    )
```

```python
import functools
import math

import jax
import jax.numpy as jnp
from jax import lax
from jax.experimental import pallas as pl
from jax.experimental.pallas import tpu as pltpu
from jax.sharding import PartitionSpec as P


base_term = 0.05
epsilon = 1e-06
LANES = 128
TAIL = 16
AXES = ("blk", "grp")

VMEM = pl.BlockSpec(memory_space=pltpu.VMEM)
SMEM = pl.BlockSpec(memory_space=pltpu.SMEM)


def unit_values(rows):
    values = rows.astype(jnp.float32)
    mean = jnp.mean(values * values, axis=-1, keepdims=True)
    scaling = lax.rsqrt(mean + epsilon) / math.sqrt(rows.shape[-1])
    return (values * scaling).astype(jnp.bfloat16)


def across(left, right):
    return lax.dot_general(
        left, right, (((1,), (1,)), ((), ())), preferred_element_type=jnp.float32
    )


def first_row(ids, shard, strata_dev, last):
    return jnp.minimum(jnp.sum((ids < shard * strata_dev).astype(jnp.int32)), last)


def pack_kernel(chips, cap, strata_dev, ids_ref, rows_ref, *rest):
    outs, held = rest[:chips], rest[chips]
    rows, width = rows_ref.shape
    step, window = 32, 2 * LANES
    chip = lax.axis_index("blk") % chips

    def normalize(i, carry):
        at = pl.ds(pl.multiple_of(i * step, step), step)
        held[at, :] = unit_values(rows_ref[at, :])
        return carry

    lax.fori_loop(0, rows // step, normalize, 0, unroll=2)
    ids = ids_ref[...]
    ids_wide = jnp.broadcast_to(ids.astype(jnp.float32), (8, rows))
    for d, out in enumerate(outs):
        tails = []
        for r in range(2):
            start = first_row(ids, (chip ^ d) * 2 + r, strata_dev, rows - cap)
            base = jnp.minimum(start // LANES * LANES, rows - window)
            pick = lax.broadcasted_iota(jnp.int32, (cap, window), 1) == lax.broadcasted_iota(
                jnp.int32, (cap, window), 0
            ) + (start - base)
            run = jnp.dot(
                pick.astype(jnp.bfloat16),
                held[pl.ds(pl.multiple_of(base, LANES), window), :],
                preferred_element_type=jnp.float32,
            ).astype(jnp.bfloat16)
            for c in range(width // LANES):
                at = (2 * c + r) * cap
                out[at : at + cap, :] = run[:, c * LANES : (c + 1) * LANES]
            tails.append(pltpu.roll(ids_wide, rows - start, axis=1)[:, :LANES])
        out[width // LANES * 2 * cap :, :] = jnp.concatenate(tails, axis=0).astype(jnp.bfloat16)


def unpack(blocks, cap, strata_dev, units, id_col):
    chip = lax.axis_index("blk") % len(blocks)
    each = len(blocks) * cap
    width = units.shape[1]
    id_rows = [[], []]
    for d, block in enumerate(blocks):
        tail = block[width // LANES * 2 * cap :, :].astype(jnp.float32)
        for r in range(2):
            at = r * each + d * cap
            for c in range(width // LANES):
                units[at : at + cap, c * LANES : (c + 1) * LANES] = block[
                    (2 * c + r) * cap : (2 * c + r + 1) * cap, :
                ]
            ids = tail[8 * r : 8 * r + 1, :] - ((2 * chip + r) * strata_dev).astype(jnp.float32)
            ids = jnp.where((ids >= 0) & (ids < strata_dev), ids, -1.0)
            id_rows[r].append(ids[:, :cap])
            id_col[at : at + cap, :] = jnp.broadcast_to(ids, (LANES, LANES)).T[:cap, :]
    return [jnp.concatenate(rows, axis=1) for rows in id_rows]


def masked_exp(scores, id_col, id_key):
    same = jnp.concatenate([id_col] * (scores.shape[1] // LANES), axis=1) == id_key
    return jnp.where(same, jnp.exp((scores - 1.0) * 4.0), 0.0)


def fold(kernel):
    rows, lanes = kernel.shape
    return jnp.sum(kernel.reshape(rows // 8, 8, lanes), axis=0)


def key_of(id_row):
    return jnp.where(id_row >= 0.0, id_row, -2.0)


def picked_by(cent_units, units, id_row):
    near = across(cent_units, units)
    which = lax.broadcasted_iota(jnp.int32, near.shape, 0).astype(jnp.float32)
    return jnp.sum(jnp.where(which == id_row, near, 0.0), axis=0, keepdims=True)


def early_kernel(chips, cap, cent0_ref, cent1_ref, *rest):
    blocks = rest[:chips]
    units, id_col, cents, facts = rest[chips:]
    strata_dev = cent0_ref.shape[0]
    each = chips * cap
    id_rows = unpack(blocks, cap, strata_dev, units, id_col)
    cents[:strata_dev, :] = unit_values(cent0_ref[...])
    cents[strata_dev:, :] = unit_values(cent1_ref[...])
    for r in range(2):
        mine = units[r * each : (r + 1) * each, :]
        sums = jnp.zeros((8, each), jnp.float32)
        for t in range(each // LANES):
            at = r * each + t * LANES
            kernel = masked_exp(
                across(units[at : at + LANES, :], mine), id_col[at : at + LANES, :], key_of(id_rows[r])
            )
            sums = sums + fold(kernel)
        picked = picked_by(cents[r * strata_dev : (r + 1) * strata_dev, :], mine, id_rows[r])
        facts[r : r + 1, :] = jnp.sum(sums, axis=0, keepdims=True)
        facts[2 + r : 3 + r, :] = picked
        facts[4 + r : 5 + r, :] = id_rows[r]


def late_kernel(chips, cap, groups, units_a, col_a, cents, facts, *rest):
    blocks, (out_ref, units_b, col_b) = rest[:chips], rest[chips:]
    strata_dev = cents.shape[0] // 2
    each = chips * cap
    me, group = lax.axis_index("blk"), lax.axis_index("grp")
    at_work = (me // chips) != (group % 2)
    rows_b = unpack(blocks, cap, strata_dev, units_b, col_b)
    total = jnp.zeros((1, 1), jnp.float32)
    weights = []
    for r in range(2):
        row_a, row_b = facts[4 + r : 5 + r, :], rows_b[r]
        key_b = key_of(row_b)
        mine = units_b[r * each : (r + 1) * each, :]
        sums = jnp.zeros((8, each), jnp.float32)
        more_a = []
        for t in range(each // LANES):
            at = r * each + t * LANES
            kernel = masked_exp(
                across(units_a[at : at + LANES, :], mine), col_a[at : at + LANES, :], key_b
            )
            sums = sums + fold(kernel)
            part = sum(
                kernel[:, c * LANES : (c + 1) * LANES] for c in range(1, each // LANES)
            ) + kernel[:, :LANES]
            more_a.append(jnp.sum(part.T, axis=0, keepdims=True))
            kernel = masked_exp(
                across(units_b[at : at + LANES, :], mine), col_b[at : at + LANES, :], key_b
            )
            sums = sums + fold(kernel)
        density_a = facts[r : r + 1, :] + jnp.concatenate(more_a, axis=1)
        density_b = jnp.sum(sums, axis=0, keepdims=True)
        picked_a = facts[2 + r : 3 + r, :]
        picked_b = picked_by(cents[r * strata_dev : (r + 1) * strata_dev, :], mine, row_b)
        both = []
        for row, picked, density in ((row_a, picked_a, density_a), (row_b, picked_b, density_b)):
            real = row >= 0.0
            weight = jnp.where(
                real, ((1.0 - picked) + base_term) / jnp.where(real, density, 1.0), 0.0
            )
            total = total + jnp.sum(weight, axis=1, keepdims=True)
            both.append(weight)
        weights.append(both)
    out_ref[...] = jnp.broadcast_to(jnp.where(at_work, total, 0.0), out_ref.shape)
    for r in range(2):
        for side in range(2):
            for d in range(chips):
                source = me ^ (d + side * chips)
                row = 4 * (source * groups + (group ^ 1)) + r
                out_ref[pl.ds(row, 1), :cap] = weights[r][side][:, d * cap : (d + 1) * cap]


def finish_kernel(chips, cap, groups, strata_dev, ids_ref, got_ref, out_ref):
    rows = ids_ref.shape[1]
    group = lax.axis_index("grp")
    got = got_ref[...]
    row_of = lax.broadcasted_iota(jnp.int32, got.shape, 0) % 4
    total = jnp.sum(jnp.where(row_of == 2, got, 0.0), axis=0, keepdims=True)[:, :1]
    ids = ids_ref[...]
    weight = jnp.zeros((1, rows), jnp.float32)
    for i in range(chips):
        owner = ((group % 2) * chips + i) * groups + (group ^ 1)
        for r in range(2):
            shard = 2 * i + r
            start = first_row(ids, shard, strata_dev, rows - cap)
            part = got_ref[pl.ds(4 * owner + r, 1), :]
            part = jnp.broadcast_to(jnp.concatenate([part] * (rows // LANES), axis=1), (8, rows))
            part = pltpu.roll(part, start, axis=1)[:1, :]
            mine = (ids >= shard * strata_dev) & (ids < (shard + 1) * strata_dev)
            weight = jnp.where(mine, part, weight)
    out_ref[...] = weight * (float(rows * 2 * chips * groups) / total)


def body(embeddings, strata, centroids):
    shards, groups = lax.axis_size("blk"), lax.axis_size("grp")
    chips = shards // 2
    rows, width = embeddings.shape[1:]
    strata_dev = centroids.shape[1]
    cap = 2 * rows // shards
    depth = width // LANES * 2 * cap + TAIL
    each = chips * cap
    every = [(b, g) for b in range(shards) for g in range(groups)]
    kind_a = [(b, g) for b, g in every if b // chips == g % 2]
    kind_b = [(b, g) for b, g in every if b // chips != g % 2]

    def send(array, pairs):
        return lax.ppermute(
            array, AXES, [(b * groups + g, to_b * groups + to_g) for (b, g), (to_b, to_g) in pairs]
        )

    def pack(ids, rows_in):
        return pl.pallas_call(
            functools.partial(pack_kernel, chips, cap, strata_dev),
            out_shape=[jax.ShapeDtypeStruct((depth, LANES), jnp.bfloat16)] * chips,
            in_specs=[VMEM, VMEM],
            out_specs=[VMEM] * chips,
            scratch_shapes=[pltpu.VMEM((rows, width), jnp.bfloat16)],
            name="pack",
        )(ids, rows_in)

    own_rows = embeddings[0]
    swap = [((b, g), (b ^ chips, g ^ 1)) for b, g in kind_b]
    far_rows, far_ids = send(own_rows, swap), send(strata, swap)
    cents = [
        send(
            centroids[0],
            [((b, g), ((g % 2) * chips + b // 2, g ^ 1)) for b, g in every if b % 2 == parity],
        )
        for parity in range(2)
    ]
    blocks_a = [
        send(block, [((b, g), (b ^ d, g ^ 1)) for b, g in kind_a])
        for d, block in enumerate(pack(strata, own_rows))
    ]
    held = pl.pallas_call(
        functools.partial(early_kernel, chips, cap),
        out_shape=[
            jax.ShapeDtypeStruct((2 * each, width), jnp.bfloat16),
            jax.ShapeDtypeStruct((2 * each, LANES), jnp.float32),
            jax.ShapeDtypeStruct((2 * strata_dev, width), jnp.bfloat16),
            jax.ShapeDtypeStruct((8, each), jnp.float32),
        ],
        in_specs=[VMEM] * (chips + 2),
        out_specs=[VMEM] * 4,
        name="early",
    )(*cents, *blocks_a)
    blocks_b = [
        block if d == 0 else send(block, [((b, g), (b ^ d, g)) for b, g in kind_b])
        for d, block in enumerate(pack(far_ids, far_rows))
    ]
    sent = pl.pallas_call(
        functools.partial(late_kernel, chips, cap, groups),
        out_shape=jax.ShapeDtypeStruct((shards * groups * 4, LANES), jnp.float32),
        in_specs=[VMEM] * (chips + 4),
        out_specs=VMEM,
        scratch_shapes=[
            pltpu.VMEM((2 * each, width), jnp.bfloat16),
            pltpu.VMEM((2 * each, LANES), jnp.float32),
        ],
        name="late",
    )(*held, *blocks_b)
    got = lax.all_to_all(
        sent.reshape(shards * groups, 4, LANES), AXES, 0, 0, tiled=True
    ).reshape(shards * groups * 4, LANES)
    return pl.pallas_call(
        functools.partial(finish_kernel, chips, cap, groups, strata_dev),
        out_shape=jax.ShapeDtypeStruct((1, rows), jnp.float32),
        in_specs=[VMEM, VMEM],
        out_specs=VMEM,
        name="finish",
    )(strata, got)


def solution(mesh):
    placed = (P("grp", "blk", None), P("grp", "blk"), P("grp", "blk", None))
    return jax.shard_map(
        body, mesh=mesh, in_specs=placed, out_specs=P("grp", "blk"), check_vma=False
    )
```

```python
import functools
import math

import jax
import jax.numpy as jnp
from jax import lax
from jax.experimental import pallas as pl
from jax.experimental.pallas import tpu as pltpu
from jax.sharding import PartitionSpec as P


base_term = 0.05
epsilon = 1e-06
LANES = 128
TAIL = 16
AXES = ("blk", "grp")

VMEM = pl.BlockSpec(memory_space=pltpu.VMEM)
ANY = pl.BlockSpec(memory_space=pl.ANY)


def params(mib):
    return pltpu.CompilerParams(vmem_limit_bytes=mib << 20)


def unit_values(rows):
    values = rows.astype(jnp.float32)
    mean = jnp.mean(values * values, axis=-1, keepdims=True)
    scaling = lax.rsqrt(mean + epsilon) / math.sqrt(rows.shape[-1])
    return (values * scaling).astype(jnp.bfloat16)


def across(left, right):
    return lax.dot_general(
        left, right, (((1,), (1,)), ((), ())), preferred_element_type=jnp.float32
    )


def pack_kernel(peers, cap, strata_dev, ids_any, rows_any, *rest):
    outs, (rows_ref, ids_ref, held, pick, sems) = rest[:peers], rest[peers:]
    rows, width = rows_ref.shape
    me = lax.axis_index("blk")
    pieces = 4
    step = rows // pieces
    loads = [pltpu.make_async_copy(ids_any, ids_ref, sems.at[pieces])]
    for i in range(pieces):
        at = pl.ds(i * step, step)
        loads.append(pltpu.make_async_copy(rows_any.at[at, :], rows_ref.at[at, :], sems.at[i]))
    for load in loads:
        load.start()
    loads[0].wait()
    ids = ids_ref[...].astype(jnp.float32)
    number = lax.broadcasted_iota(jnp.int32, (peers, 1), 0)
    lowest = ((me ^ number) * strata_dev).astype(jnp.float32)
    begin = jnp.sum((ids < lowest).astype(jnp.float32), axis=1, keepdims=True)
    start = jnp.minimum(begin, float(rows - cap))
    number = lax.broadcasted_iota(jnp.int32, (peers * strata_dev, 1), 0)
    stratum = (me ^ (number // strata_dev)) * strata_dev + number % strata_dev
    ends = jnp.sum((ids <= stratum.astype(jnp.float32)).astype(jnp.float32), axis=1, keepdims=True)
    slot = lax.broadcasted_iota(jnp.int32, (cap, rows), 0).astype(jnp.float32)
    row = lax.broadcasted_iota(jnp.int32, (cap, rows), 1).astype(jnp.float32)
    ahead = row - slot
    lane = lax.broadcasted_iota(jnp.int32, (1, LANES), 1).astype(jnp.float32)
    for k, out in enumerate(outs):
        first = start[k : k + 1, :]
        pick[k * cap : (k + 1) * cap, :] = (ahead == first).astype(jnp.bfloat16)
        at = lane + first
        passed = (ends[k * strata_dev : (k + 1) * strata_dev, :] <= at).astype(jnp.float32)
        local = jnp.where(
            at >= begin[k : k + 1, :], jnp.sum(passed, axis=0, keepdims=True), float(strata_dev)
        )
        out[width // LANES * cap :, :] = jnp.broadcast_to(local, (TAIL, LANES)).astype(jnp.bfloat16)
    for i in range(pieces):
        loads[1 + i].wait()
        held[i * step : (i + 1) * step, :] = unit_values(rows_ref[i * step : (i + 1) * step, :])
    wide = 2 * LANES
    for c in range(width // wide):
        runs = jnp.dot(
            pick[...], held[:, c * wide : (c + 1) * wide], preferred_element_type=jnp.float32
        ).astype(jnp.bfloat16)
        for k, out in enumerate(outs):
            for part in range(2):
                at = (2 * c + part) * cap
                out[at : at + cap, :] = runs[
                    k * cap : (k + 1) * cap, part * LANES : (part + 1) * LANES
                ]


def own_kernel(order, cap, groups, cent_ref, *rest):
    peers = len(order)
    blocks, (out_ref, units, id_col) = rest[:peers], rest[peers:]
    slots, width = units.shape
    strata_dev = cent_ref.shape[0]
    me, group = lax.axis_index("blk"), lax.axis_index("grp")

    id_rows = []
    for k, block in enumerate(blocks):
        for c in range(width // LANES):
            units[k * cap : (k + 1) * cap, c * LANES : (c + 1) * LANES] = block[
                c * cap : (c + 1) * cap, :
            ]
        ids = block[width // LANES * cap :, :].astype(jnp.float32)[:1, :]
        ids = jnp.where(ids < float(strata_dev), ids, -1.0)
        id_rows.append(ids[:, :cap])
        wide = jnp.broadcast_to(ids, (LANES, LANES)).T
        id_col[k * cap : (k + 1) * cap, :] = wide[:cap, :]
    id_row = jnp.concatenate(id_rows, axis=1)
    real = id_row >= 0.0
    id_key = jnp.where(real, id_row, -2.0)

    tile = 512
    sums = jnp.zeros((8, slots), jnp.float32)
    everything = units[...]
    for t in range(slots // tile):
        scores = across(units[t * tile : (t + 1) * tile, :], everything)
        kernel = jnp.exp((scores - 1.0) * 4.0)
        same = (
            jnp.concatenate([id_col[t * tile : (t + 1) * tile, :]] * (slots // LANES), axis=1)
            == id_key
        )
        kernel = jnp.where(same, kernel, 0.0)
        sums = sums + jnp.sum(kernel.reshape(tile // 8, 8, slots), axis=0)
    density = jnp.sum(sums, axis=0, keepdims=True)

    near = across(unit_values(cent_ref[...]), everything)
    which = lax.broadcasted_iota(jnp.int32, near.shape, 0).astype(jnp.float32)
    picked = jnp.sum(jnp.where(which == id_row, near, 0.0), axis=0, keepdims=True)
    weight = jnp.where(
        real, ((1.0 - picked) + base_term) / jnp.where(real, density, 1.0), 0.0
    )
    out_ref[...] = jnp.broadcast_to(jnp.sum(weight, axis=1, keepdims=True), out_ref.shape)
    for i, k in enumerate(order):
        row = 2 * ((me ^ k) * groups + group)
        out_ref[pl.ds(row, 1), :cap] = weight[:, i * cap : (i + 1) * cap]


def finish_kernel(peers, cap, groups, strata_dev, ids_ref, got_ref, out_ref):
    rows = ids_ref.shape[1]
    group = lax.axis_index("grp")
    got = got_ref[...]
    odd = lax.broadcasted_iota(jnp.int32, got.shape, 0) % 2
    total = jnp.sum(jnp.where(odd == 1, got, 0.0), axis=0, keepdims=True)[:, :1]
    ids = ids_ref[...]
    weight = jnp.zeros((1, rows), jnp.float32)
    for owner in range(peers):
        begin = jnp.sum((ids < owner * strata_dev).astype(jnp.int32))
        start = jnp.minimum(begin, rows - cap)
        part = got_ref[pl.ds(2 * (owner * groups + group), 1), :]
        part = jnp.broadcast_to(jnp.concatenate([part] * (rows // LANES), axis=1), (8, rows))
        part = pltpu.roll(part, start, axis=1)[:1, :]
        mine = (ids >= owner * strata_dev) & (ids < (owner + 1) * strata_dev)
        weight = jnp.where(mine, part, weight)
    out_ref[...] = weight * (float(rows * peers * groups) / total)


def body(embeddings, strata, centroids):
    peers, groups = lax.axis_size("blk"), lax.axis_size("grp")
    rows, width = embeddings.shape[1:]
    strata_dev = centroids.shape[1]
    cap = 2 * rows // peers
    depth = width // LANES * cap + TAIL

    blocks = [*pl.pallas_call(
        functools.partial(pack_kernel, peers, cap, strata_dev),
        out_shape=[pltpu.VMEM((depth, LANES), jnp.bfloat16)] * peers,
        in_specs=[ANY, ANY],
        out_specs=[VMEM] * peers,
        scratch_shapes=[
            pltpu.VMEM((rows, width), jnp.bfloat16),
            pltpu.VMEM((1, rows), jnp.int32),
            pltpu.VMEM((rows, width), jnp.bfloat16),
            pltpu.VMEM((peers * cap, rows), jnp.bfloat16),
            pltpu.SemaphoreType.DMA((5,)),
        ],
        compiler_params=params(58),
        name="pack",
    )(strata, embeddings[0])]
    far = range(peers // 2, peers)
    order = [0, 1, 2, *far, *range(3, peers // 2)]
    blocks = [
        blocks[k] if k == 0 else lax.ppermute(blocks[k], "blk", [(i, i ^ k) for i in range(peers)])
        for k in order
    ]
    sent = pl.pallas_call(
        functools.partial(own_kernel, order, cap, groups),
        out_shape=jax.ShapeDtypeStruct((peers * groups * 2, LANES), jnp.float32),
        in_specs=[VMEM] * (peers + 1),
        out_specs=VMEM,
        scratch_shapes=[
            pltpu.VMEM((peers * cap, width), jnp.bfloat16),
            pltpu.VMEM((peers * cap, LANES), jnp.float32),
        ],
        compiler_params=params(24),
        name="own",
    )(centroids[0], *blocks)
    got = lax.all_to_all(
        sent.reshape(peers * groups, 2, LANES), AXES, 0, 0, tiled=True
    ).reshape(peers * groups * 2, LANES)
    return pl.pallas_call(
        functools.partial(finish_kernel, peers, cap, groups, strata_dev),
        out_shape=jax.ShapeDtypeStruct((1, rows), jnp.float32),
        in_specs=[VMEM, VMEM],
        out_specs=VMEM,
        compiler_params=params(8),
        name="finish",
    )(strata, got)


def solution(mesh):
    placed = (P("grp", "blk", None), P("grp", "blk"), P("grp", "blk", None))
    return jax.shard_map(
        body, mesh=mesh, in_specs=placed, out_specs=P("grp", "blk"), check_vma=False
    )
```

```python
import functools
import math

import jax
import jax.numpy as jnp
from jax import lax
from jax.experimental import pallas as pl
from jax.experimental.pallas import tpu as pltpu
from jax.sharding import PartitionSpec as P


base_term = 0.05
epsilon = 1e-06
LANES = 128
TAIL = 16
AXES = ("blk", "grp")

VMEM = pl.BlockSpec(memory_space=pltpu.VMEM)
ANY = pl.BlockSpec(memory_space=pl.ANY)


def params(mib):
    return pltpu.CompilerParams(vmem_limit_bytes=mib << 20)


def unit_values(rows):
    values = rows.astype(jnp.float32)
    mean = jnp.mean(values * values, axis=-1, keepdims=True)
    scaling = lax.rsqrt(mean + epsilon) / math.sqrt(rows.shape[-1])
    return (values * scaling).astype(jnp.bfloat16)


def across(left, right):
    return lax.dot_general(
        left, right, (((1,), (1,)), ((), ())), preferred_element_type=jnp.float32
    )


def shard_of(k, chips):
    me = lax.axis_index("blk")
    half, chip = me // chips, me % chips
    return ((half ^ (k % 2)) * chips) + (chip ^ (k // 2))


def pack_into(ids, loads, rows_ref, outs, held, pick, cap, strata_dev):
    rows, width = rows_ref.shape
    chips = len(outs)
    shards = 2 * chips
    number = lax.broadcasted_iota(jnp.int32, (shards, 1), 0)
    lowest = (shard_of(number, chips) * strata_dev).astype(jnp.float32)
    begin = jnp.sum((ids < lowest).astype(jnp.float32), axis=1, keepdims=True)
    start = jnp.minimum(begin, float(rows - cap))
    number = lax.broadcasted_iota(jnp.int32, (shards * strata_dev, 1), 0)
    stratum = shard_of(number // strata_dev, chips) * strata_dev + number % strata_dev
    ends = jnp.sum((ids <= stratum.astype(jnp.float32)).astype(jnp.float32), axis=1, keepdims=True)
    slot = lax.broadcasted_iota(jnp.int32, (cap, rows), 0).astype(jnp.float32)
    row = lax.broadcasted_iota(jnp.int32, (cap, rows), 1).astype(jnp.float32)
    ahead = row - slot
    lane = lax.broadcasted_iota(jnp.int32, (1, LANES), 1).astype(jnp.float32)
    for k in range(shards):
        first = start[k : k + 1, :]
        pick[k * cap : (k + 1) * cap, :] = (ahead == first).astype(jnp.bfloat16)
        at = lane + first
        passed = (ends[k * strata_dev : (k + 1) * strata_dev, :] <= at).astype(jnp.float32)
        local = jnp.where(
            at >= begin[k : k + 1, :], jnp.sum(passed, axis=0, keepdims=True), float(strata_dev)
        )
        tail = width // LANES * 2 * cap + (k % 2) * 8
        outs[k // 2][tail : tail + 8, :] = jnp.broadcast_to(local, (8, LANES)).astype(jnp.bfloat16)
    step = rows // max(len(loads), 1)
    for i, load in enumerate(loads):
        load.wait()
        held[i * step : (i + 1) * step, :] = unit_values(rows_ref[i * step : (i + 1) * step, :])
    if not loads:
        held[...] = unit_values(rows_ref[...])
    wide = 2 * LANES
    for c in range(width // wide):
        runs = jnp.dot(
            pick[...], held[:, c * wide : (c + 1) * wide], preferred_element_type=jnp.float32
        ).astype(jnp.bfloat16)
        for d, out in enumerate(outs):
            for part in range(2):
                at = (2 * c + part) * 2 * cap
                out[at : at + 2 * cap, :] = runs[
                    d * 2 * cap : (d + 1) * 2 * cap, part * LANES : (part + 1) * LANES
                ]


def near_kernel(chips, cap, ids_any, cent_ref, rows_any, *rest):
    outs, (extra, rows_ref, ids_ref, held, pick, sems) = rest[:chips], rest[chips:]
    strata_dev, width = cent_ref.shape
    rows = rows_ref.shape[0]
    pieces = 4
    loads = [pltpu.make_async_copy(ids_any, ids_ref, sems.at[pieces])]
    for i in range(pieces):
        at = pl.ds(i * (rows // pieces), rows // pieces)
        loads.append(pltpu.make_async_copy(rows_any.at[at, :], rows_ref.at[at, :], sems.at[i]))
    for load in loads:
        load.start()
    cent = unit_values(cent_ref[...])
    extra[:strata_dev, :] = cent
    depth = width // LANES * 2 * cap + TAIL
    for c in range(width // LANES):
        at = depth + c * strata_dev
        outs[0][at : at + strata_dev, :] = cent[:, c * LANES : (c + 1) * LANES]
    loads[0].wait()
    ids = ids_ref[...].astype(jnp.float32)
    extra[strata_dev:, :] = jnp.zeros((TAIL, width), jnp.bfloat16)
    extra[strata_dev:, :rows] = jnp.broadcast_to(ids, (TAIL, rows)).astype(jnp.bfloat16)
    pack_into(ids, loads[1:], rows_ref, outs, held, pick, cap, strata_dev)


def far_kernel(chips, cap, strata_dev, extra, rows_ref, *rest):
    outs, (held, pick) = rest[:chips], rest[chips:]
    rows = rows_ref.shape[0]
    ids = extra[strata_dev:, :rows].astype(jnp.float32)[:1, :]
    pack_into(ids, [], rows_ref, outs, held, pick, cap, strata_dev)


def unpack(blocks, cap, strata_dev, units, id_col):
    each = len(blocks) * cap
    width = units.shape[1]
    id_rows = [[], []]
    for i, block in enumerate(blocks):
        depth = width // LANES * 2 * cap
        tail = block[depth : depth + TAIL, :].astype(jnp.float32)
        for r in range(2):
            at = r * each + i * cap
            for c in range(width // LANES):
                units[at : at + cap, c * LANES : (c + 1) * LANES] = block[
                    (2 * c + r) * cap : (2 * c + r + 1) * cap, :
                ]
            ids = tail[8 * r : 8 * r + 1, :]
            ids = jnp.where(ids < float(strata_dev), ids, -1.0)
            id_rows[r].append(ids[:, :cap])
            id_col[at : at + cap, :] = jnp.broadcast_to(ids, (LANES, LANES)).T[:cap, :]
    return [jnp.concatenate(rows, axis=1) for rows in id_rows]


def masked_exp(scores, id_col, id_key):
    same = jnp.concatenate([id_col] * (scores.shape[1] // LANES), axis=1) == id_key
    return jnp.where(same, jnp.exp((scores - 1.0) * 4.0), 0.0)


def fold(kernel):
    rows, lanes = kernel.shape
    return jnp.sum(kernel.reshape(rows // 8, 8, lanes), axis=0)


def key_of(id_row):
    return jnp.where(id_row >= 0.0, id_row, -2.0)


def picked_by(cent_units, units, id_row):
    near = across(cent_units, units)
    which = lax.broadcasted_iota(jnp.int32, near.shape, 0).astype(jnp.float32)
    return jnp.sum(jnp.where(which == id_row, near, 0.0), axis=0, keepdims=True)


def early_kernel(chips, cap, strata_dev, *rest):
    blocks, (units, id_col, facts) = rest[:chips], rest[chips:]
    each = chips * cap
    id_rows = unpack(blocks, cap, strata_dev, units, id_col)
    for r, row in enumerate(id_rows):
        mine = units[r * each : (r + 1) * each, :]
        kernel = masked_exp(across(mine, mine), id_col[r * each : (r + 1) * each, :], key_of(row))
        facts[r : r + 1, :] = jnp.sum(fold(kernel), axis=0, keepdims=True)
        facts[2 + r : 3 + r, :] = row


def late_kernel(order, cap, groups, units_a, col_a, facts, extra, block0, *rest):
    chips = len(order)
    blocks, (out_ref, units_b, col_b, cent0) = rest[:chips], rest[chips:]
    strata_dev, width = cent0.shape
    depth = width // LANES * 2 * cap + TAIL
    for c in range(width // LANES):
        at = depth + c * strata_dev
        cent0[:, c * LANES : (c + 1) * LANES] = block0[at : at + strata_dev, :]
    ids_b = unpack(blocks, cap, strata_dev, units_b, col_b)
    each = chips * cap
    me, group = lax.axis_index("blk"), lax.axis_index("grp")
    at_work = (me // chips) != (group % 2)
    total = jnp.zeros((1, 1), jnp.float32)
    weights = []
    for r in range(2):
        part_of = slice(r * each, (r + 1) * each)
        row_a, row_b = facts[2 + r : 3 + r, :], ids_b[r]
        key_b = key_of(row_b)
        rows_a, rows_b = units_a[part_of, :], units_b[part_of, :]
        kernel = masked_exp(across(rows_a, rows_b), col_a[part_of, :], key_b)
        sums = fold(kernel)
        part = kernel[:, :LANES]
        for c in range(1, each // LANES):
            part = part + kernel[:, c * LANES : (c + 1) * LANES]
        density_a = facts[r : r + 1, :] + jnp.concatenate(
            [
                jnp.sum(part[i * LANES : (i + 1) * LANES, :].T, axis=0, keepdims=True)
                for i in range(each // LANES)
            ],
            axis=1,
        )
        kernel = masked_exp(across(rows_b, rows_b), col_b[part_of, :], key_b)
        density_b = jnp.sum(sums + fold(kernel), axis=0, keepdims=True)
        cents = cent0[...] if r == 0 else extra[:strata_dev, :]
        both = []
        for row, units, density in ((row_a, rows_a, density_a), (row_b, rows_b, density_b)):
            real = row >= 0.0
            weight = jnp.where(
                real,
                ((1.0 - picked_by(cents, units, row)) + base_term)
                / jnp.where(real, density, 1.0),
                0.0,
            )
            total = total + jnp.sum(weight, axis=1, keepdims=True)
            both.append(weight)
        weights.append(both)
    out_ref[...] = jnp.broadcast_to(jnp.where(at_work, total, 0.0), out_ref.shape)
    for r in range(2):
        for side in range(2):
            for i, d in enumerate(order):
                source = me ^ (d + side * chips)
                at = 4 * (source * groups + (group ^ 1)) + r
                out_ref[pl.ds(at, 1), :cap] = weights[r][side][:, i * cap : (i + 1) * cap]


def finish_kernel(chips, cap, groups, strata_dev, ids_ref, got_ref, out_ref):
    rows = ids_ref.shape[1]
    group = lax.axis_index("grp")
    half = group % 2
    got = got_ref[...]
    row_of = lax.broadcasted_iota(jnp.int32, got.shape, 0) % 4
    total = jnp.sum(jnp.where(row_of == 2, got, 0.0), axis=0, keepdims=True)[:, :1]
    ids = ids_ref[...]
    weight = jnp.zeros((1, rows), jnp.float32)
    for i in range(chips):
        owner = (half * chips + i) * groups + (group ^ 1)
        for r in range(2):
            shard = (half ^ r) * chips + i
            begin = jnp.sum((ids < shard * strata_dev).astype(jnp.int32))
            start = jnp.minimum(begin, rows - cap)
            part = got_ref[pl.ds(4 * owner + r, 1), :]
            part = jnp.broadcast_to(jnp.concatenate([part] * (rows // LANES), axis=1), (8, rows))
            part = pltpu.roll(part, start, axis=1)[:1, :]
            mine = (ids >= shard * strata_dev) & (ids < (shard + 1) * strata_dev)
            weight = jnp.where(mine, part, weight)
    out_ref[...] = weight * (float(rows * 2 * chips * groups) / total)


def body(embeddings, strata, centroids):
    shards, groups = lax.axis_size("blk"), lax.axis_size("grp")
    chips = shards // 2
    rows, width = embeddings.shape[1:]
    strata_dev = centroids.shape[1]
    cap = 2 * rows // shards
    chunks = width // LANES
    depth = chunks * 2 * cap + TAIL
    each = chips * cap
    every = [(b, g) for b in range(shards) for g in range(groups)]
    kind_a = [(b, g) for b, g in every if b // chips == g % 2]
    kind_b = [(b, g) for b, g in every if b // chips != g % 2]

    def send(array, pairs):
        return lax.ppermute(
            array, AXES, [(b * groups + g, to_b * groups + to_g) for (b, g), (to_b, to_g) in pairs]
        )

    def shape(*dims, dtype=jnp.bfloat16):
        return pltpu.VMEM(dims, dtype)

    held = [pltpu.VMEM((rows, width), jnp.bfloat16), pltpu.VMEM((shards * cap, rows), jnp.bfloat16)]
    order = [0, *reversed(range(1, chips))]
    swap = [((b, g), (b ^ chips, g ^ 1)) for b, g in kind_b]
    far_rows = send(embeddings[0], swap)
    *near, extra = pl.pallas_call(
        functools.partial(near_kernel, chips, cap),
        out_shape=[
            shape(depth + (chunks * strata_dev if d == 0 else 0), LANES) for d in range(chips)
        ]
        + [shape(strata_dev + TAIL, width)],
        in_specs=[ANY, VMEM, ANY],
        out_specs=[VMEM] * (chips + 1),
        scratch_shapes=[
            pltpu.VMEM((rows, width), jnp.bfloat16),
            pltpu.VMEM((1, rows), jnp.int32),
            *held,
            pltpu.SemaphoreType.DMA((5,)),
        ],
        compiler_params=params(44),
        cost_estimate=pl.CostEstimate(flops=0, transcendentals=0, bytes_accessed=0),
        name="near",
    )(strata, centroids[0], embeddings[0])
    blocks_a = []
    for d in order:
        block = near[d]
        if d == 1:
            block, _ = lax.optimization_barrier((block, blocks_a[0]))
        blocks_a.append(send(block, [((b, g), (b ^ d, g ^ 1)) for b, g in kind_a]))
    extra = send(extra, swap)
    blocks_b = pl.pallas_call(
        functools.partial(far_kernel, chips, cap, strata_dev),
        out_shape=[shape(depth, LANES)] * chips,
        in_specs=[VMEM, VMEM],
        out_specs=[VMEM] * chips,
        scratch_shapes=held,
        compiler_params=params(20),
        name="far",
    )(extra, far_rows)
    blocks_b = [
        blocks_b[d]
        if d == 0
        else send(blocks_b[d], [((b, g), (b ^ d, g)) for b, g in kind_b])
        for d in order
    ]
    units_a, col_a, facts = pl.pallas_call(
        functools.partial(early_kernel, chips, cap, strata_dev),
        out_shape=[
            shape(2 * each, width),
            shape(2 * each, LANES, dtype=jnp.float32),
            shape(8, each, dtype=jnp.float32),
        ],
        in_specs=[VMEM] * chips,
        out_specs=[VMEM] * 3,
        compiler_params=params(20),
        name="early",
    )(*blocks_a)
    sent = pl.pallas_call(
        functools.partial(late_kernel, order, cap, groups),
        out_shape=jax.ShapeDtypeStruct((shards * groups * 4, LANES), jnp.float32),
        in_specs=[VMEM] * (chips + 5),
        out_specs=VMEM,
        scratch_shapes=[
            pltpu.VMEM((2 * each, width), jnp.bfloat16),
            pltpu.VMEM((2 * each, LANES), jnp.float32),
            pltpu.VMEM((strata_dev, width), jnp.bfloat16),
        ],
        compiler_params=params(24),
        name="late",
    )(units_a, col_a, facts, extra, blocks_a[0], *blocks_b)
    got = lax.all_to_all(
        sent.reshape(shards * groups, 4, LANES), AXES, 0, 0, tiled=True
    ).reshape(shards * groups * 4, LANES)
    return pl.pallas_call(
        functools.partial(finish_kernel, chips, cap, groups, strata_dev),
        out_shape=jax.ShapeDtypeStruct((1, rows), jnp.float32),
        in_specs=[VMEM, VMEM],
        out_specs=VMEM,
        compiler_params=params(8),
        name="finish",
    )(strata, got)


def solution(mesh):
    placed = (P("grp", "blk", None), P("grp", "blk"), P("grp", "blk", None))
    return jax.shard_map(
        body, mesh=mesh, in_specs=placed, out_specs=P("grp", "blk"), check_vma=False
    )
```

```python
import functools
import math

import jax
import jax.numpy as jnp
from jax import lax
from jax.experimental import pallas as pl
from jax.experimental.pallas import tpu as pltpu
from jax.sharding import PartitionSpec as P


base_term = 0.05
epsilon = 1e-06
LANES = 128
TAIL = 16
AXES = ("blk", "grp")

VMEM = pl.BlockSpec(memory_space=pltpu.VMEM)
ANY = pl.BlockSpec(memory_space=pl.ANY)


def params(mib):
    return pltpu.CompilerParams(vmem_limit_bytes=mib << 20)


def unit_values(rows):
    values = rows.astype(jnp.float32)
    mean = jnp.mean(values * values, axis=-1, keepdims=True)
    scaling = lax.rsqrt(mean + epsilon) / math.sqrt(rows.shape[-1])
    return (values * scaling).astype(jnp.bfloat16)


def across(left, right):
    return lax.dot_general(
        left, right, (((1,), (1,)), ((), ())), preferred_element_type=jnp.float32
    )


def shard_of(k, chips):
    me = lax.axis_index("blk")
    half, chip = me // chips, me % chips
    return ((half ^ (k % 2)) * chips) + (chip ^ (k // 2))


def pack_into(ids, loads, rows_ref, outs, held, pick, cap, strata_dev):
    rows, width = rows_ref.shape
    chips = len(outs)
    shards = 2 * chips
    number = lax.broadcasted_iota(jnp.int32, (shards, 1), 0)
    lowest = (shard_of(number, chips) * strata_dev).astype(jnp.float32)
    begin = jnp.sum((ids < lowest).astype(jnp.float32), axis=1, keepdims=True)
    start = jnp.minimum(begin, float(rows - cap))
    number = lax.broadcasted_iota(jnp.int32, (shards * strata_dev, 1), 0)
    stratum = shard_of(number // strata_dev, chips) * strata_dev + number % strata_dev
    ends = jnp.sum((ids <= stratum.astype(jnp.float32)).astype(jnp.float32), axis=1, keepdims=True)
    slot = lax.broadcasted_iota(jnp.int32, (cap, rows), 0).astype(jnp.float32)
    row = lax.broadcasted_iota(jnp.int32, (cap, rows), 1).astype(jnp.float32)
    ahead = row - slot
    lane = lax.broadcasted_iota(jnp.int32, (1, LANES), 1).astype(jnp.float32)
    for k in range(shards):
        first = start[k : k + 1, :]
        pick[k * cap : (k + 1) * cap, :] = (ahead == first).astype(jnp.bfloat16)
        at = lane + first
        passed = (ends[k * strata_dev : (k + 1) * strata_dev, :] <= at).astype(jnp.float32)
        local = jnp.where(
            at >= begin[k : k + 1, :], jnp.sum(passed, axis=0, keepdims=True), float(strata_dev)
        )
        tail = width // LANES * 2 * cap + (k % 2) * 8
        outs[k // 2][tail : tail + 8, :] = jnp.broadcast_to(local, (8, LANES)).astype(jnp.bfloat16)
    step = rows // max(len(loads), 1)
    for i, load in enumerate(loads):
        load.wait()
        held[i * step : (i + 1) * step, :] = unit_values(rows_ref[i * step : (i + 1) * step, :])
    if not loads:
        held[...] = unit_values(rows_ref[...])
    wide = 2 * LANES
    for c in range(width // wide):
        runs = jnp.dot(
            pick[...], held[:, c * wide : (c + 1) * wide], preferred_element_type=jnp.float32
        ).astype(jnp.bfloat16)
        for d, out in enumerate(outs):
            for part in range(2):
                at = (2 * c + part) * 2 * cap
                out[at : at + 2 * cap, :] = runs[
                    d * 2 * cap : (d + 1) * 2 * cap, part * LANES : (part + 1) * LANES
                ]


def near_kernel(chips, cap, ids_any, cent_ref, rows_any, *rest):
    outs, (extra, rows_ref, ids_ref, held, pick, sems) = rest[:chips], rest[chips:]
    strata_dev, width = cent_ref.shape
    rows = rows_ref.shape[0]
    pieces = 4
    loads = [pltpu.make_async_copy(ids_any, ids_ref, sems.at[pieces])]
    for i in range(pieces):
        at = pl.ds(i * (rows // pieces), rows // pieces)
        loads.append(pltpu.make_async_copy(rows_any.at[at, :], rows_ref.at[at, :], sems.at[i]))
    for load in loads:
        load.start()
    cent = unit_values(cent_ref[...])
    extra[:strata_dev, :] = cent
    depth = width // LANES * 2 * cap + TAIL
    for c in range(width // LANES):
        at = depth + c * strata_dev
        outs[0][at : at + strata_dev, :] = cent[:, c * LANES : (c + 1) * LANES]
    loads[0].wait()
    ids = ids_ref[...].astype(jnp.float32)
    extra[strata_dev:, :] = jnp.zeros((TAIL, width), jnp.bfloat16)
    extra[strata_dev:, :rows] = jnp.broadcast_to(ids, (TAIL, rows)).astype(jnp.bfloat16)
    pack_into(ids, loads[1:], rows_ref, outs, held, pick, cap, strata_dev)


def far_kernel(chips, cap, strata_dev, extra, rows_ref, *rest):
    outs, (held, pick) = rest[:chips], rest[chips:]
    rows = rows_ref.shape[0]
    ids = extra[strata_dev:, :rows].astype(jnp.float32)[:1, :]
    pack_into(ids, [], rows_ref, outs, held, pick, cap, strata_dev)


def unpack(blocks, cap, strata_dev, units, id_col):
    each = len(blocks) * cap
    width = units.shape[1]
    id_rows = [[], []]
    for i, block in enumerate(blocks):
        depth = width // LANES * 2 * cap
        tail = block[depth : depth + TAIL, :].astype(jnp.float32)
        for r in range(2):
            at = r * each + i * cap
            for c in range(width // LANES):
                units[at : at + cap, c * LANES : (c + 1) * LANES] = block[
                    (2 * c + r) * cap : (2 * c + r + 1) * cap, :
                ]
            ids = tail[8 * r : 8 * r + 1, :]
            ids = jnp.where(ids < float(strata_dev), ids, -1.0)
            id_rows[r].append(ids[:, :cap])
            id_col[at : at + cap, :] = jnp.broadcast_to(ids, (LANES, LANES)).T[:cap, :]
    return [jnp.concatenate(rows, axis=1) for rows in id_rows]


def masked_exp(scores, id_col, id_key):
    same = jnp.concatenate([id_col] * (scores.shape[1] // LANES), axis=1) == id_key
    return jnp.where(same, jnp.exp((scores - 1.0) * 4.0), 0.0)


def fold(kernel):
    rows, lanes = kernel.shape
    return jnp.sum(kernel.reshape(rows // 8, 8, lanes), axis=0)


def key_of(id_row):
    return jnp.where(id_row >= 0.0, id_row, -2.0)


def picked_by(cent_units, units, id_row):
    near = across(cent_units, units)
    which = lax.broadcasted_iota(jnp.int32, near.shape, 0).astype(jnp.float32)
    return jnp.sum(jnp.where(which == id_row, near, 0.0), axis=0, keepdims=True)


def transposed_sum(kernel):
    part = kernel[:, :LANES]
    for c in range(1, kernel.shape[1] // LANES):
        part = part + kernel[:, c * LANES : (c + 1) * LANES]
    return jnp.concatenate(
        [
            jnp.sum(part[i * LANES : (i + 1) * LANES, :].T, axis=0, keepdims=True)
            for i in range(part.shape[0] // LANES)
        ],
        axis=1,
    )


def join(groups, units, id_col, ids):
    earlier, new = [[] for _ in groups], []
    for r, row in enumerate(ids):
        key = key_of(row)
        each = row.shape[1]
        mine = units[r * each : (r + 1) * each, :]
        sums = fold(masked_exp(across(mine, mine), id_col[r * each : (r + 1) * each, :], key))
        for sums_of, (old_units, old_col, old_facts) in zip(earlier, groups):
            size = old_facts.shape[1]
            at = slice(r * size, (r + 1) * size)
            kernel = masked_exp(across(old_units[at, :], mine), old_col[at, :], key)
            sums = sums + fold(kernel)
            sums_of.append(old_facts[r : r + 1, :] + transposed_sum(kernel))
        new.append(jnp.sum(sums, axis=0, keepdims=True))
    return earlier, new


def early_kernel(chips, cap, strata_dev, *rest):
    blocks, (units, id_col, facts) = rest[:chips], rest[chips:]
    ids = unpack(blocks, cap, strata_dev, units, id_col)
    _, density = join([], units, id_col, ids)
    for r, row in enumerate(ids):
        facts[r : r + 1, :] = density[r]
        facts[2 + r : 3 + r, :] = row


def mid_kernel(count, cap, units_a, col_a, facts_a, extra, block0, *rest):
    blocks, (units, id_col, facts, facts_out, cents) = rest[:count], rest[count:]
    strata_dev, width = cents.shape[0] // 2, cents.shape[1]
    depth = width // LANES * 2 * cap + TAIL
    for c in range(width // LANES):
        at = depth + c * strata_dev
        cents[:strata_dev, c * LANES : (c + 1) * LANES] = block0[at : at + strata_dev, :]
    cents[strata_dev:, :] = extra[:strata_dev, :]
    ids = unpack(blocks, cap, strata_dev, units, id_col)
    (old,), density = join([(units_a, col_a, facts_a)], units, id_col, ids)
    for r, row in enumerate(ids):
        near = cents[r * strata_dev : (r + 1) * strata_dev, :]
        facts[r : r + 1, :] = density[r]
        facts[2 + r : 3 + r, :] = row
        each = row.shape[1]
        facts[4 + r : 5 + r, :] = picked_by(near, units[r * each : (r + 1) * each, :], row)
        row = facts_a[2 + r : 3 + r, :]
        facts_out[r : r + 1, :] = old[r]
        facts_out[2 + r : 3 + r, :] = row
        each = row.shape[1]
        facts_out[4 + r : 5 + r, :] = picked_by(near, units_a[r * each : (r + 1) * each, :], row)


def late_kernel(order, cap, groups, units_a, col_a, facts_a, units_m, col_m, facts_m, cents, *rest):
    blocks, (out_ref, units, id_col) = rest[:-3], rest[-3:]
    chips = len(order)
    strata_dev = cents.shape[0] // 2
    me, group = lax.axis_index("blk"), lax.axis_index("grp")
    at_work = (me // chips) != (group % 2)
    ids = unpack(blocks, cap, strata_dev, units, id_col)
    old = [(units_a, col_a, facts_a), (units_m, col_m, facts_m)]
    earlier, density = join(old, units, id_col, ids)
    total = jnp.zeros((1, 1), jnp.float32)
    weights = []
    for r, row in enumerate(ids):
        near = cents[r * strata_dev : (r + 1) * strata_dev, :]
        each = row.shape[1]
        states = [
            (facts_a[2 + r : 3 + r, :], facts_a[4 + r : 5 + r, :], earlier[0][r]),
            (facts_m[2 + r : 3 + r, :], facts_m[4 + r : 5 + r, :], earlier[1][r]),
            (row, picked_by(near, units[r * each : (r + 1) * each, :], row), density[r]),
        ]
        all_of = [jnp.concatenate(parts, axis=1) for parts in zip(*states)]
        row, picked, dense = all_of
        real = row >= 0.0
        weight = jnp.where(
            real, ((1.0 - picked) + base_term) / jnp.where(real, dense, 1.0), 0.0
        )
        total = total + jnp.sum(weight, axis=1, keepdims=True)
        weights.append(weight)
    out_ref[...] = jnp.broadcast_to(jnp.where(at_work, total, 0.0), out_ref.shape)
    for r in range(2):
        for i in range(2 * chips):
            source = me ^ (order[i % chips] + i // chips * chips)
            at = 4 * (source * groups + (group ^ 1)) + r
            out_ref[pl.ds(at, 1), :cap] = weights[r][:, i * cap : (i + 1) * cap]


def finish_kernel(chips, cap, groups, strata_dev, ids_ref, got_ref, out_ref):
    rows = ids_ref.shape[1]
    group = lax.axis_index("grp")
    half = group % 2
    got = got_ref[...]
    row_of = lax.broadcasted_iota(jnp.int32, got.shape, 0) % 4
    total = jnp.sum(jnp.where(row_of == 2, got, 0.0), axis=0, keepdims=True)[:, :1]
    ids = ids_ref[...]
    weight = jnp.zeros((1, rows), jnp.float32)
    for i in range(chips):
        owner = (half * chips + i) * groups + (group ^ 1)
        for r in range(2):
            shard = (half ^ r) * chips + i
            begin = jnp.sum((ids < shard * strata_dev).astype(jnp.int32))
            start = jnp.minimum(begin, rows - cap)
            part = got_ref[pl.ds(4 * owner + r, 1), :]
            part = jnp.broadcast_to(jnp.concatenate([part] * (rows // LANES), axis=1), (8, rows))
            part = pltpu.roll(part, start, axis=1)[:1, :]
            mine = (ids >= shard * strata_dev) & (ids < (shard + 1) * strata_dev)
            weight = jnp.where(mine, part, weight)
    out_ref[...] = weight * (float(rows * 2 * chips * groups) / total)


def body(embeddings, strata, centroids):
    shards, groups = lax.axis_size("blk"), lax.axis_size("grp")
    chips = shards // 2
    rows, width = embeddings.shape[1:]
    strata_dev = centroids.shape[1]
    cap = 2 * rows // shards
    chunks = width // LANES
    depth = chunks * 2 * cap + TAIL
    each = chips * cap
    every = [(b, g) for b in range(shards) for g in range(groups)]
    kind_a = [(b, g) for b, g in every if b // chips == g % 2]
    kind_b = [(b, g) for b, g in every if b // chips != g % 2]

    def send(array, pairs):
        return lax.ppermute(
            array, AXES, [(b * groups + g, to_b * groups + to_g) for (b, g), (to_b, to_g) in pairs]
        )

    def shape(*dims, dtype=jnp.bfloat16):
        return pltpu.VMEM(dims, dtype)

    held = [pltpu.VMEM((rows, width), jnp.bfloat16), pltpu.VMEM((shards * cap, rows), jnp.bfloat16)]
    order = [0, *reversed(range(1, chips))]
    swap = [((b, g), (b ^ chips, g ^ 1)) for b, g in kind_b]
    far_rows = send(embeddings[0], swap)
    *near, extra = pl.pallas_call(
        functools.partial(near_kernel, chips, cap),
        out_shape=[
            shape(depth + (chunks * strata_dev if d == 0 else 0), LANES) for d in range(chips)
        ]
        + [shape(strata_dev + TAIL, width)],
        in_specs=[ANY, VMEM, ANY],
        out_specs=[VMEM] * (chips + 1),
        scratch_shapes=[
            pltpu.VMEM((rows, width), jnp.bfloat16),
            pltpu.VMEM((1, rows), jnp.int32),
            *held,
            pltpu.SemaphoreType.DMA((5,)),
        ],
        compiler_params=params(44),
        cost_estimate=pl.CostEstimate(flops=0, transcendentals=0, bytes_accessed=0),
        name="near",
    )(strata, centroids[0], embeddings[0])
    blocks_a = []
    for d in order:
        block = near[d]
        if d == order[-1]:
            block, _ = lax.optimization_barrier((block, blocks_a[0]))
        blocks_a.append(send(block, [((b, g), (b ^ d, g ^ 1)) for b, g in kind_a]))
    extra = send(extra, swap)
    blocks_b = pl.pallas_call(
        functools.partial(far_kernel, chips, cap, strata_dev),
        out_shape=[shape(depth, LANES)] * chips,
        in_specs=[VMEM, VMEM],
        out_specs=[VMEM] * chips,
        scratch_shapes=held,
        compiler_params=params(20),
        name="far",
    )(extra, far_rows)
    blocks_b = [
        blocks_b[d]
        if d == 0
        else send(blocks_b[d], [((b, g), (b ^ d, g)) for b, g in kind_b])
        for d in order
    ]
    units_a, col_a, facts = pl.pallas_call(
        functools.partial(early_kernel, chips, cap, strata_dev),
        out_shape=[
            shape(2 * each, width),
            shape(2 * each, LANES, dtype=jnp.float32),
            shape(8, each, dtype=jnp.float32),
        ],
        in_specs=[VMEM] * chips,
        out_specs=[VMEM] * 3,
        compiler_params=params(20),
        name="early",
    )(*blocks_a)
    middle = chips // 2
    units_m, col_m, facts_m, facts_a, cents = pl.pallas_call(
        functools.partial(mid_kernel, middle, cap),
        out_shape=[
            shape(2 * middle * cap, width),
            shape(2 * middle * cap, LANES, dtype=jnp.float32),
            shape(8, middle * cap, dtype=jnp.float32),
            shape(8, each, dtype=jnp.float32),
            shape(2 * strata_dev, width),
        ],
        in_specs=[VMEM] * (middle + 5),
        out_specs=[VMEM] * 5,
        compiler_params=params(20),
        name="mid",
    )(units_a, col_a, facts, extra, blocks_a[0], *blocks_b[:middle])
    sent = pl.pallas_call(
        functools.partial(late_kernel, order, cap, groups),
        out_shape=jax.ShapeDtypeStruct((shards * groups * 4, LANES), jnp.float32),
        in_specs=[VMEM] * (7 + chips - middle),
        out_specs=VMEM,
        scratch_shapes=[
            pltpu.VMEM((2 * (chips - middle) * cap, width), jnp.bfloat16),
            pltpu.VMEM((2 * (chips - middle) * cap, LANES), jnp.float32),
        ],
        compiler_params=params(20),
        name="late",
    )(units_a, col_a, facts_a, units_m, col_m, facts_m, cents, *blocks_b[middle:])
    got = lax.all_to_all(
        sent.reshape(shards * groups, 4, LANES), AXES, 0, 0, tiled=True
    ).reshape(shards * groups * 4, LANES)
    return pl.pallas_call(
        functools.partial(finish_kernel, chips, cap, groups, strata_dev),
        out_shape=jax.ShapeDtypeStruct((1, rows), jnp.float32),
        in_specs=[VMEM, VMEM],
        out_specs=VMEM,
        compiler_params=params(8),
        name="finish",
    )(strata, got)


def solution(mesh):
    placed = (P("grp", "blk", None), P("grp", "blk"), P("grp", "blk", None))
    return jax.shard_map(
        body, mesh=mesh, in_specs=placed, out_specs=P("grp", "blk"), check_vma=False
    )
```

```python
import functools
import math

import jax
import jax.numpy as jnp
from jax import lax
from jax.experimental import pallas as pl
from jax.experimental.pallas import tpu as pltpu
from jax.sharding import PartitionSpec as P


base_term = 0.05
epsilon = 1e-06
LANES = 128
TAIL = 16
AXES = ("blk", "grp")

VMEM = pl.BlockSpec(memory_space=pltpu.VMEM)
ANY = pl.BlockSpec(memory_space=pl.ANY)


def params(mib):
    return pltpu.CompilerParams(vmem_limit_bytes=mib << 20)


def unit_values(rows):
    values = rows.astype(jnp.float32)
    mean = jnp.mean(values * values, axis=-1, keepdims=True)
    scaling = lax.rsqrt(mean + epsilon) / math.sqrt(rows.shape[-1])
    return (values * scaling).astype(jnp.bfloat16)


def across(left, right):
    return lax.dot_general(
        left, right, (((1,), (1,)), ((), ())), preferred_element_type=jnp.float32
    )


def shard_of(k, chips):
    me = lax.axis_index("blk")
    half, chip = me // chips, me % chips
    return ((half ^ (k % 2)) * chips) + (chip ^ (k // 2))


def pack_into(ids, loads, rows_ref, outs, held, pick, cap, strata_dev):
    rows, width = rows_ref.shape
    chips = len(outs)
    shards = 2 * chips
    number = lax.broadcasted_iota(jnp.int32, (shards, 1), 0)
    lowest = (shard_of(number, chips) * strata_dev).astype(jnp.float32)
    begin = jnp.sum((ids < lowest).astype(jnp.float32), axis=1, keepdims=True)
    start = jnp.minimum(begin, float(rows - cap))
    number = lax.broadcasted_iota(jnp.int32, (shards * strata_dev, 1), 0)
    stratum = shard_of(number // strata_dev, chips) * strata_dev + number % strata_dev
    ends = jnp.sum((ids <= stratum.astype(jnp.float32)).astype(jnp.float32), axis=1, keepdims=True)
    slot = lax.broadcasted_iota(jnp.int32, (cap, rows), 0).astype(jnp.float32)
    row = lax.broadcasted_iota(jnp.int32, (cap, rows), 1).astype(jnp.float32)
    ahead = row - slot
    lane = lax.broadcasted_iota(jnp.int32, (1, LANES), 1).astype(jnp.float32)
    for k in range(shards):
        first = start[k : k + 1, :]
        pick[k * cap : (k + 1) * cap, :] = (ahead == first).astype(jnp.bfloat16)
        at = lane + first
        passed = (ends[k * strata_dev : (k + 1) * strata_dev, :] <= at).astype(jnp.float32)
        local = jnp.where(
            at >= begin[k : k + 1, :], jnp.sum(passed, axis=0, keepdims=True), float(strata_dev)
        )
        tail = width // LANES * 2 * cap + (k % 2) * 8
        outs[k // 2][tail : tail + 8, :] = jnp.broadcast_to(local, (8, LANES)).astype(jnp.bfloat16)
    step = rows // max(len(loads), 1)
    for i, load in enumerate(loads):
        load.wait()
        held[i * step : (i + 1) * step, :] = unit_values(rows_ref[i * step : (i + 1) * step, :])
    if not loads:
        held[...] = unit_values(rows_ref[...])
    wide = 2 * LANES
    for c in range(width // wide):
        runs = jnp.dot(
            pick[...], held[:, c * wide : (c + 1) * wide], preferred_element_type=jnp.float32
        ).astype(jnp.bfloat16)
        for d, out in enumerate(outs):
            for part in range(2):
                at = (2 * c + part) * 2 * cap
                out[at : at + 2 * cap, :] = runs[
                    d * 2 * cap : (d + 1) * 2 * cap, part * LANES : (part + 1) * LANES
                ]


def near_kernel(chips, cap, ids_any, cent_ref, rows_any, *rest):
    outs, (extra, rows_ref, ids_ref, held, pick, sems) = rest[:chips], rest[chips:]
    strata_dev, width = cent_ref.shape
    rows = rows_ref.shape[0]
    pieces = 4
    loads = [pltpu.make_async_copy(ids_any, ids_ref, sems.at[pieces])]
    for i in range(pieces):
        at = pl.ds(i * (rows // pieces), rows // pieces)
        loads.append(pltpu.make_async_copy(rows_any.at[at, :], rows_ref.at[at, :], sems.at[i]))
    for load in loads:
        load.start()
    cent = unit_values(cent_ref[...])
    depth = width // LANES * 2 * cap + TAIL
    for c in range(width // LANES):
        at = depth + c * strata_dev
        outs[0][at : at + strata_dev, :] = cent[:, c * LANES : (c + 1) * LANES]
    loads[0].wait()
    ids = ids_ref[...].astype(jnp.float32)
    extra[...] = jnp.concatenate(
        [
            jnp.broadcast_to(ids[:, i * LANES : (i + 1) * LANES], (TAIL // 4, LANES))
            for i in range(rows // LANES)
        ],
        axis=0,
    ).astype(jnp.bfloat16)
    pack_into(ids, loads[1:], rows_ref, outs, held, pick, cap, strata_dev)


def far_kernel(chips, cap, strata_dev, extra, rows_ref, *rest):
    outs, (held, pick) = rest[:chips], rest[chips:]
    spread = extra[...].astype(jnp.float32)
    ids = jnp.concatenate([spread[i : i + 1, :] for i in range(0, TAIL, TAIL // 4)], axis=1)
    pack_into(ids, [], rows_ref, outs, held, pick, cap, strata_dev)


def unpack(blocks, cap, strata_dev, units, id_col):
    each = len(blocks) * cap
    width = units.shape[1]
    id_rows = [[], []]
    for i, block in enumerate(blocks):
        depth = width // LANES * 2 * cap
        tail = block[depth : depth + TAIL, :].astype(jnp.float32)
        for r in range(2):
            at = r * each + i * cap
            for c in range(width // LANES):
                units[at : at + cap, c * LANES : (c + 1) * LANES] = block[
                    (2 * c + r) * cap : (2 * c + r + 1) * cap, :
                ]
            ids = tail[8 * r : 8 * r + 1, :]
            ids = jnp.where(ids < float(strata_dev), ids, -1.0)
            id_rows[r].append(ids[:, :cap])
            id_col[at : at + cap, :] = jnp.broadcast_to(ids, (LANES, LANES)).T[:cap, :]
    return [jnp.concatenate(rows, axis=1) for rows in id_rows]


def masked_exp(scores, id_col, id_key):
    same = jnp.concatenate([id_col] * (scores.shape[1] // LANES), axis=1) == id_key
    return jnp.where(same, jnp.exp((scores - 1.0) * 4.0), 0.0)


def fold(kernel):
    rows, lanes = kernel.shape
    return jnp.sum(kernel.reshape(rows // 8, 8, lanes), axis=0)


def key_of(id_row):
    return jnp.where(id_row >= 0.0, id_row, -2.0)


def picked_by(cent_units, units, id_row):
    near = across(cent_units, units)
    which = lax.broadcasted_iota(jnp.int32, near.shape, 0).astype(jnp.float32)
    return jnp.sum(jnp.where(which == id_row, near, 0.0), axis=0, keepdims=True)


def transposed_sum(kernel):
    part = kernel[:, :LANES]
    for c in range(1, kernel.shape[1] // LANES):
        part = part + kernel[:, c * LANES : (c + 1) * LANES]
    return jnp.concatenate(
        [
            jnp.sum(part[i * LANES : (i + 1) * LANES, :].T, axis=0, keepdims=True)
            for i in range(part.shape[0] // LANES)
        ],
        axis=1,
    )


def join(groups, units, id_col, ids):
    earlier, new = [[] for _ in groups], []
    for r, row in enumerate(ids):
        key = key_of(row)
        each = row.shape[1]
        mine = units[r * each : (r + 1) * each, :]
        sums = fold(masked_exp(across(mine, mine), id_col[r * each : (r + 1) * each, :], key))
        for sums_of, (old_units, old_col, old_facts) in zip(earlier, groups):
            size = old_facts.shape[1]
            at = slice(r * size, (r + 1) * size)
            kernel = masked_exp(across(old_units[at, :], mine), old_col[at, :], key)
            sums = sums + fold(kernel)
            sums_of.append(old_facts[r : r + 1, :] + transposed_sum(kernel))
        new.append(jnp.sum(sums, axis=0, keepdims=True))
    return earlier, new


def early_kernel(chips, cap, strata_dev, *rest):
    blocks, (units, id_col, facts) = rest[:chips], rest[chips:]
    ids = unpack(blocks, cap, strata_dev, units, id_col)
    _, density = join([], units, id_col, ids)
    for r, row in enumerate(ids):
        facts[r : r + 1, :] = density[r]
        facts[2 + r : 3 + r, :] = row


def mid_kernel(count, cap, units_a, col_a, facts_a, far_cents, block0, *rest):
    blocks, (units, id_col, facts, facts_out, cents) = rest[:count], rest[count:]
    strata_dev, width = cents.shape[0] // 2, cents.shape[1]
    depth = width // LANES * 2 * cap + TAIL
    for c in range(width // LANES):
        at = depth + c * strata_dev
        cents[:strata_dev, c * LANES : (c + 1) * LANES] = block0[at : at + strata_dev, :]
    cents[strata_dev:, :] = unit_values(far_cents[...])
    ids = unpack(blocks, cap, strata_dev, units, id_col)
    (old,), density = join([(units_a, col_a, facts_a)], units, id_col, ids)
    for r, row in enumerate(ids):
        near = cents[r * strata_dev : (r + 1) * strata_dev, :]
        facts[r : r + 1, :] = density[r]
        facts[2 + r : 3 + r, :] = row
        each = row.shape[1]
        facts[4 + r : 5 + r, :] = picked_by(near, units[r * each : (r + 1) * each, :], row)
        row = facts_a[2 + r : 3 + r, :]
        facts_out[r : r + 1, :] = old[r]
        facts_out[2 + r : 3 + r, :] = row
        each = row.shape[1]
        facts_out[4 + r : 5 + r, :] = picked_by(near, units_a[r * each : (r + 1) * each, :], row)


def late_kernel(order, cap, groups, units_a, col_a, facts_a, units_m, col_m, facts_m, cents, *rest):
    blocks, (out_ref, units, id_col) = rest[:-3], rest[-3:]
    chips = len(order)
    strata_dev = cents.shape[0] // 2
    me, group = lax.axis_index("blk"), lax.axis_index("grp")
    at_work = (me // chips) != (group % 2)
    ids = unpack(blocks, cap, strata_dev, units, id_col)
    old = [(units_a, col_a, facts_a), (units_m, col_m, facts_m)]
    earlier, density = join(old, units, id_col, ids)
    total = jnp.zeros((1, 1), jnp.float32)
    weights = []
    for r, row in enumerate(ids):
        near = cents[r * strata_dev : (r + 1) * strata_dev, :]
        each = row.shape[1]
        states = [
            (facts_a[2 + r : 3 + r, :], facts_a[4 + r : 5 + r, :], earlier[0][r]),
            (facts_m[2 + r : 3 + r, :], facts_m[4 + r : 5 + r, :], earlier[1][r]),
            (row, picked_by(near, units[r * each : (r + 1) * each, :], row), density[r]),
        ]
        all_of = [jnp.concatenate(parts, axis=1) for parts in zip(*states)]
        row, picked, dense = all_of
        real = row >= 0.0
        weight = jnp.where(
            real, ((1.0 - picked) + base_term) / jnp.where(real, dense, 1.0), 0.0
        )
        total = total + jnp.sum(weight, axis=1, keepdims=True)
        weights.append(weight)
    out_ref[...] = jnp.broadcast_to(jnp.where(at_work, total, 0.0), out_ref.shape)
    for r in range(2):
        for i in range(2 * chips):
            source = me ^ (order[i % chips] + i // chips * chips)
            at = 4 * (source * groups + (group ^ 1)) + r
            out_ref[pl.ds(at, 1), :cap] = weights[r][:, i * cap : (i + 1) * cap]


def finish_kernel(chips, cap, groups, strata_dev, ids_ref, got_ref, out_ref):
    rows = ids_ref.shape[1]
    group = lax.axis_index("grp")
    half = group % 2
    got = got_ref[...]
    row_of = lax.broadcasted_iota(jnp.int32, got.shape, 0) % 4
    total = jnp.sum(jnp.where(row_of == 2, got, 0.0), axis=0, keepdims=True)[:, :1]
    ids = ids_ref[...]
    weight = jnp.zeros((1, rows), jnp.float32)
    for i in range(chips):
        owner = (half * chips + i) * groups + (group ^ 1)
        for r in range(2):
            shard = (half ^ r) * chips + i
            begin = jnp.sum((ids < shard * strata_dev).astype(jnp.int32))
            start = jnp.minimum(begin, rows - cap)
            part = got_ref[pl.ds(4 * owner + r, 1), :]
            part = jnp.broadcast_to(jnp.concatenate([part] * (rows // LANES), axis=1), (8, rows))
            part = pltpu.roll(part, start, axis=1)[:1, :]
            mine = (ids >= shard * strata_dev) & (ids < (shard + 1) * strata_dev)
            weight = jnp.where(mine, part, weight)
    out_ref[...] = weight * (float(rows * 2 * chips * groups) / total)


def body(embeddings, strata, centroids):
    shards, groups = lax.axis_size("blk"), lax.axis_size("grp")
    chips = shards // 2
    rows, width = embeddings.shape[1:]
    strata_dev = centroids.shape[1]
    cap = 2 * rows // shards
    chunks = width // LANES
    depth = chunks * 2 * cap + TAIL
    each = chips * cap
    every = [(b, g) for b in range(shards) for g in range(groups)]
    kind_a = [(b, g) for b, g in every if b // chips == g % 2]
    kind_b = [(b, g) for b, g in every if b // chips != g % 2]

    def send(array, pairs):
        return lax.ppermute(
            array, AXES, [(b * groups + g, to_b * groups + to_g) for (b, g), (to_b, to_g) in pairs]
        )

    def shape(*dims, dtype=jnp.bfloat16):
        return pltpu.VMEM(dims, dtype)

    held = [pltpu.VMEM((rows, width), jnp.bfloat16), pltpu.VMEM((shards * cap, rows), jnp.bfloat16)]
    order = [0, *reversed(range(1, chips))]
    swap = [((b, g), (b ^ chips, g ^ 1)) for b, g in kind_b]
    far_rows = send(embeddings[0], swap)
    *near, extra = pl.pallas_call(
        functools.partial(near_kernel, chips, cap),
        out_shape=[
            shape(depth + (chunks * strata_dev if d == 0 else 0), LANES) for d in range(chips)
        ]
        + [shape(TAIL, LANES)],
        in_specs=[ANY, VMEM, ANY],
        out_specs=[VMEM] * (chips + 1),
        scratch_shapes=[
            pltpu.VMEM((rows, width), jnp.bfloat16),
            pltpu.VMEM((1, rows), jnp.int32),
            *held,
            pltpu.SemaphoreType.DMA((5,)),
        ],
        compiler_params=params(44),
        cost_estimate=pl.CostEstimate(flops=0, transcendentals=0, bytes_accessed=0),
        name="near",
    )(strata, centroids[0], embeddings[0])
    blocks_a = []
    for d in order:
        block = near[d]
        if d == order[-1]:
            block, _ = lax.optimization_barrier((block, blocks_a[0]))
        blocks_a.append(send(block, [((b, g), (b ^ d, g ^ 1)) for b, g in kind_a]))
    extra = send(extra, swap)
    blocks_b = pl.pallas_call(
        functools.partial(far_kernel, chips, cap, strata_dev),
        out_shape=[shape(depth, LANES)] * chips,
        in_specs=[VMEM, VMEM],
        out_specs=[VMEM] * chips,
        scratch_shapes=held,
        compiler_params=params(20),
        name="far",
    )(extra, far_rows)
    far_cents, _ = lax.optimization_barrier((centroids[0], blocks_b[0]))
    far_cents = send(far_cents, swap)
    blocks_b = [
        blocks_b[d]
        if d == 0
        else send(blocks_b[d], [((b, g), (b ^ d, g)) for b, g in kind_b])
        for d in order
    ]
    units_a, col_a, facts = pl.pallas_call(
        functools.partial(early_kernel, chips, cap, strata_dev),
        out_shape=[
            shape(2 * each, width),
            shape(2 * each, LANES, dtype=jnp.float32),
            shape(8, each, dtype=jnp.float32),
        ],
        in_specs=[VMEM] * chips,
        out_specs=[VMEM] * 3,
        compiler_params=params(20),
        name="early",
    )(*blocks_a)
    middle = chips // 2
    units_m, col_m, facts_m, facts_a, cents = pl.pallas_call(
        functools.partial(mid_kernel, middle, cap),
        out_shape=[
            shape(2 * middle * cap, width),
            shape(2 * middle * cap, LANES, dtype=jnp.float32),
            shape(8, middle * cap, dtype=jnp.float32),
            shape(8, each, dtype=jnp.float32),
            shape(2 * strata_dev, width),
        ],
        in_specs=[VMEM] * (middle + 5),
        out_specs=[VMEM] * 5,
        compiler_params=params(20),
        name="mid",
    )(units_a, col_a, facts, far_cents, blocks_a[0], *blocks_b[:middle])
    sent = pl.pallas_call(
        functools.partial(late_kernel, order, cap, groups),
        out_shape=jax.ShapeDtypeStruct((shards * groups * 4, LANES), jnp.float32),
        in_specs=[VMEM] * (7 + chips - middle),
        out_specs=VMEM,
        scratch_shapes=[
            pltpu.VMEM((2 * (chips - middle) * cap, width), jnp.bfloat16),
            pltpu.VMEM((2 * (chips - middle) * cap, LANES), jnp.float32),
        ],
        compiler_params=params(20),
        name="late",
    )(units_a, col_a, facts_a, units_m, col_m, facts_m, cents, *blocks_b[middle:])
    got = lax.all_to_all(
        sent.reshape(shards * groups, 4, LANES), AXES, 0, 0, tiled=True
    ).reshape(shards * groups * 4, LANES)
    return pl.pallas_call(
        functools.partial(finish_kernel, chips, cap, groups, strata_dev),
        out_shape=jax.ShapeDtypeStruct((1, rows), jnp.float32),
        in_specs=[VMEM, VMEM],
        out_specs=VMEM,
        compiler_params=params(8),
        name="finish",
    )(strata, got)


def solution(mesh):
    placed = (P("grp", "blk", None), P("grp", "blk"), P("grp", "blk", None))
    return jax.shard_map(
        body, mesh=mesh, in_specs=placed, out_specs=P("grp", "blk"), check_vma=False
    )
```

```python
import functools
import math

import jax
import jax.numpy as jnp
from jax import lax
from jax.experimental import pallas as pl
from jax.experimental.pallas import tpu as pltpu
from jax.sharding import PartitionSpec as P


base_term = 0.05
epsilon = 1e-06
LANES = 128
TAIL = 16
AXES = ("blk", "grp")

VMEM = pl.BlockSpec(memory_space=pltpu.VMEM)
ANY = pl.BlockSpec(memory_space=pl.ANY)


def params(mib):
    return pltpu.CompilerParams(vmem_limit_bytes=mib << 20)


def unit_values(rows):
    values = rows.astype(jnp.float32)
    mean = jnp.mean(values * values, axis=-1, keepdims=True)
    scaling = lax.rsqrt(mean + epsilon) / math.sqrt(rows.shape[-1])
    return (values * scaling).astype(jnp.bfloat16)


def across(left, right):
    return lax.dot_general(
        left, right, (((1,), (1,)), ((), ())), preferred_element_type=jnp.float32
    )


def is_inner(chips):
    me = lax.axis_index("blk")
    return (me % chips) // (chips // 2) != me // chips


def shard_of(k, chips, half):
    owner = half * chips + ((lax.axis_index("blk") % chips) ^ (k // 2))
    return owner ^ ((k % 2) * (chips + chips // 2))


def pack_into(ids, loads, rows_ref, outs, held, pick, cap, strata_dev, half):
    rows, width = rows_ref.shape
    chips = len(outs)
    shards = 2 * chips
    number = lax.broadcasted_iota(jnp.int32, (shards, 1), 0)
    lowest = (shard_of(number, chips, half) * strata_dev).astype(jnp.float32)
    begin = jnp.sum((ids < lowest).astype(jnp.float32), axis=1, keepdims=True)
    start = jnp.minimum(begin, float(rows - cap))
    number = lax.broadcasted_iota(jnp.int32, (shards * strata_dev, 1), 0)
    stratum = shard_of(number // strata_dev, chips, half) * strata_dev + number % strata_dev
    ends = jnp.sum((ids <= stratum.astype(jnp.float32)).astype(jnp.float32), axis=1, keepdims=True)
    slot = lax.broadcasted_iota(jnp.int32, (cap, rows), 0).astype(jnp.float32)
    row = lax.broadcasted_iota(jnp.int32, (cap, rows), 1).astype(jnp.float32)
    ahead = row - slot
    lane = lax.broadcasted_iota(jnp.int32, (1, LANES), 1).astype(jnp.float32)
    for k in range(shards):
        first = start[k : k + 1, :]
        pick[k * cap : (k + 1) * cap, :] = (ahead == first).astype(jnp.bfloat16)
        at = lane + first
        passed = (ends[k * strata_dev : (k + 1) * strata_dev, :] <= at).astype(jnp.float32)
        local = jnp.where(
            at >= begin[k : k + 1, :], jnp.sum(passed, axis=0, keepdims=True), float(strata_dev)
        )
        tail = width // LANES * 2 * cap + (k % 2) * 8
        outs[k // 2][tail : tail + 8, :] = jnp.broadcast_to(local, (8, LANES)).astype(jnp.bfloat16)
    step = rows // max(len(loads), 1)
    for i, load in enumerate(loads):
        load.wait()
        held[i * step : (i + 1) * step, :] = unit_values(rows_ref[i * step : (i + 1) * step, :])
    if not loads:
        held[...] = unit_values(rows_ref[...])
    wide = 2 * LANES
    for c in range(width // wide):
        runs = jnp.dot(
            pick[...], held[:, c * wide : (c + 1) * wide], preferred_element_type=jnp.float32
        ).astype(jnp.bfloat16)
        for d, out in enumerate(outs):
            for part in range(2):
                at = (2 * c + part) * 2 * cap
                out[at : at + 2 * cap, :] = runs[
                    d * 2 * cap : (d + 1) * 2 * cap, part * LANES : (part + 1) * LANES
                ]


def near_kernel(chips, cap, ids_any, cent_ref, rows_any, *rest):
    outs, (extra, rows_ref, ids_ref, held, pick, sems) = rest[:chips], rest[chips:]
    strata_dev, width = cent_ref.shape
    rows = rows_ref.shape[0]
    pieces = 4
    loads = [pltpu.make_async_copy(ids_any, ids_ref, sems.at[pieces])]
    for i in range(pieces):
        at = pl.ds(i * (rows // pieces), rows // pieces)
        loads.append(pltpu.make_async_copy(rows_any.at[at, :], rows_ref.at[at, :], sems.at[i]))
    for load in loads:
        load.start()
    cent = unit_values(cent_ref[...])
    depth = width // LANES * 2 * cap + TAIL
    for c in range(width // LANES):
        at = depth + c * strata_dev
        for out in (outs[0], outs[chips // 2]):
            out[at : at + strata_dev, :] = cent[:, c * LANES : (c + 1) * LANES]
    loads[0].wait()
    ids = ids_ref[...].astype(jnp.float32)
    for c in range(width // LANES):
        at = TAIL + c * strata_dev
        extra[at : at + strata_dev, :] = cent[:, c * LANES : (c + 1) * LANES]
    extra[:TAIL, :] = jnp.concatenate(
        [
            jnp.broadcast_to(ids[:, i * LANES : (i + 1) * LANES], (TAIL // 4, LANES))
            for i in range(rows // LANES)
        ],
        axis=0,
    ).astype(jnp.bfloat16)
    half = lax.axis_index("grp") % 2
    pack_into(ids, loads[1:], rows_ref, outs, held, pick, cap, strata_dev, half)


def far_kernel(chips, cap, strata_dev, extra, rows_ref, *rest):
    inner = is_inner(chips)
    direct, outs, (held, pick) = rest[: chips // 2], rest[chips // 2 : -2], rest[-2:]

    @pl.when(inner)
    def _():
        spread = extra[:TAIL, :].astype(jnp.float32)
        ids = jnp.concatenate([spread[i : i + 1, :] for i in range(0, TAIL, TAIL // 4)], axis=1)
        half = lax.axis_index("blk") // chips
        pack_into(ids, [], rows_ref, outs, held, pick, cap, strata_dev, half)

    @pl.when(jnp.logical_not(inner))
    def _():
        for block, out in zip(direct, outs[chips // 2 :]):
            out[...] = block[: out.shape[0], :]


def unpack(blocks, cap, strata_dev, units, id_col, others=None, use_others=None):
    each = len(blocks) * cap
    width = units.shape[1]
    depth = width // LANES * 2 * cap

    def lay(some):
        for i, block in enumerate(some):
            for r in range(2):
                at = r * each + i * cap
                for c in range(width // LANES):
                    units[at : at + cap, c * LANES : (c + 1) * LANES] = block[
                        (2 * c + r) * cap : (2 * c + r + 1) * cap, :
                    ]

    if others is None:
        lay(blocks)
    else:
        pl.when(use_others)(lambda: lay(others))
        pl.when(jnp.logical_not(use_others))(lambda: lay(blocks))
    id_rows = [[], []]
    for i, block in enumerate(blocks):
        tail = block[depth : depth + TAIL, :].astype(jnp.float32)
        if others is not None:
            other = others[i][depth : depth + TAIL, :].astype(jnp.float32)
            tail = jnp.where(
                jnp.broadcast_to(use_others.astype(jnp.int32), tail.shape) > 0, other, tail
            )
        for r in range(2):
            at = r * each + i * cap
            ids = tail[8 * r : 8 * r + 1, :]
            ids = jnp.where(ids < float(strata_dev), ids, -1.0)
            id_rows[r].append(ids[:, :cap])
            id_col[at : at + cap, :] = jnp.broadcast_to(ids, (LANES, LANES)).T[:cap, :]
    return [jnp.concatenate(rows, axis=1) for rows in id_rows]


def masked_exp(scores, id_col, id_key):
    same = jnp.concatenate([id_col] * (scores.shape[1] // LANES), axis=1) == id_key
    return jnp.where(same, jnp.exp((scores - 1.0) * 4.0), 0.0)


def fold(kernel):
    rows, lanes = kernel.shape
    return jnp.sum(kernel.reshape(rows // 8, 8, lanes), axis=0)


def key_of(id_row):
    return jnp.where(id_row >= 0.0, id_row, -2.0)


def own_centroid(near, id_row):
    which = lax.broadcasted_iota(jnp.int32, near.shape, 0).astype(jnp.float32)
    return jnp.sum(jnp.where(which == id_row, near, 0.0), axis=0, keepdims=True)


def transposed_sum(kernel):
    part = kernel[:, :LANES]
    for c in range(1, kernel.shape[1] // LANES):
        part = part + kernel[:, c * LANES : (c + 1) * LANES]
    return jnp.concatenate(
        [
            jnp.sum(part[i * LANES : (i + 1) * LANES, :].T, axis=0, keepdims=True)
            for i in range(part.shape[0] // LANES)
        ],
        axis=1,
    )


def join(groups, units, id_col, ids, cents=None):
    earlier, new, picked = [[] for _ in groups], [], []
    for r, row in enumerate(ids):
        key = key_of(row)
        each = row.shape[1]
        mine = units[r * each : (r + 1) * each, :]
        left = mine
        if cents is not None:
            strata_dev = cents.shape[0] // 2
            left = jnp.concatenate([mine, cents[r * strata_dev : (r + 1) * strata_dev, :]], axis=0)
        scores = across(left, mine)
        if cents is not None:
            picked.append(own_centroid(scores[each:, :], row))
        sums = fold(masked_exp(scores[:each, :], id_col[r * each : (r + 1) * each, :], key))
        for sums_of, (old_units, old_col, old_density) in zip(earlier, groups):
            size = old_density[r].shape[1]
            at = slice(r * size, (r + 1) * size)
            kernel = masked_exp(across(old_units[at, :], mine), old_col[at, :], key)
            sums = sums + fold(kernel)
            sums_of.append(old_density[r] + transposed_sum(kernel))
        new.append(jnp.sum(sums, axis=0, keepdims=True))
    return earlier, new, picked


def parts_of(value):
    high = value.astype(jnp.bfloat16).astype(jnp.float32)
    middle = (value - high).astype(jnp.bfloat16).astype(jnp.float32)
    return [high, middle, value - high - middle]


def early_kernel(chips, cap, strata_dev, after, *rest):
    blocks, (held, id_col) = rest[:chips], rest[chips:]
    in_a = lax.axis_index("grp") % 2 == lax.axis_index("blk") // chips

    @pl.when(in_a)
    def _():
        width = held.shape[1]
        each = chips * cap
        depth = width // LANES * 2 * cap + TAIL
        ids = unpack(blocks, cap, strata_dev, held, id_col)
        for c in range(width // LANES):
            at = depth + c * strata_dev
            held[2 * each : 2 * each + strata_dev, c * LANES : (c + 1) * LANES] = blocks[0][
                at : at + strata_dev, :
            ]
        _, density, _ = join([], held, id_col, ids)
        rows = [*parts_of(density[0]), *parts_of(density[1]), *ids]
        tail = jnp.concatenate(rows + rows, axis=0).astype(jnp.bfloat16)
        held[2 * each + strata_dev :, :each] = tail


def mid_kernel(chips, cap, group_a, extra, *rest):
    direct, spread, (units, id_col, facts, facts_a, col_a, cents) = (
        rest[: chips // 2],
        rest[chips // 2 : chips],
        rest[chips:],
    )
    inner = is_inner(chips)
    strata_dev, width = cents.shape[0] // 2, cents.shape[1]
    depth = width // LANES * 2 * cap + TAIL
    each = chips * cap

    def place(block, base):
        for c in range(width // LANES):
            at = base + c * strata_dev
            cents[strata_dev:, c * LANES : (c + 1) * LANES] = block[at : at + strata_dev, :]

    cents[:strata_dev, :] = group_a[2 * each : 2 * each + strata_dev, :]
    pl.when(inner)(lambda: place(extra, TAIL))
    pl.when(jnp.logical_not(inner))(lambda: place(direct[0], depth))
    tail = group_a[2 * each + strata_dev :, :each].astype(jnp.float32)
    density_a = []
    for r in range(2):
        density_a.append(
            tail[3 * r : 3 * r + 1, :] + tail[3 * r + 1 : 3 * r + 2, :] + tail[3 * r + 2 : 3 * r + 3, :]
        )
        row = tail[6 + r : 7 + r, :]
        col_a[r * each : (r + 1) * each, :] = upright(row)
        facts_a[2 + r : 3 + r, :] = row
        near = cents[r * strata_dev : (r + 1) * strata_dev, :]
        facts_a[4 + r : 5 + r, :] = own_centroid(
            across(near, group_a[r * each : (r + 1) * each, :]), row
        )
    ids = unpack(direct, cap, strata_dev, units, id_col, spread, inner)
    (old,), density, picked = join([(group_a, col_a, density_a)], units, id_col, ids, cents)
    for r, row in enumerate(ids):
        facts[r : r + 1, :] = density[r]
        facts[2 + r : 3 + r, :] = row
        facts[4 + r : 5 + r, :] = picked[r]
        facts_a[r : r + 1, :] = old[r]


def upright(row):
    return jnp.concatenate(
        [
            jnp.broadcast_to(row[:, i * LANES : (i + 1) * LANES], (LANES, LANES)).T
            for i in range(row.shape[1] // LANES)
        ],
        axis=0,
    )


def late_kernel(order, cap, groups, units_a, col_a, facts_a, units_m, col_m, facts_m, cents, *rest):
    blocks, (out_ref, units, id_col) = rest[:-3], rest[-3:]
    strata_dev = cents.shape[0] // 2
    chips = len(order) // 2
    me, group = lax.axis_index("blk"), lax.axis_index("grp")
    at_work = (me // chips) != (group % 2)
    ids = unpack(blocks, cap, strata_dev, units, id_col)
    old = [
        (some, col, [facts[r : r + 1, :] for r in range(2)])
        for some, col, facts in ((units_a, col_a, facts_a), (units_m, col_m, facts_m))
    ]
    earlier, density, picked_new = join(old, units, id_col, ids, cents)
    total = jnp.zeros((1, 1), jnp.float32)
    weights = []
    for r, row in enumerate(ids):
        states = [
            (facts_a[2 + r : 3 + r, :], facts_a[4 + r : 5 + r, :], earlier[0][r]),
            (facts_m[2 + r : 3 + r, :], facts_m[4 + r : 5 + r, :], earlier[1][r]),
            (row, picked_new[r], density[r]),
        ]
        row, picked, dense = [jnp.concatenate(parts, axis=1) for parts in zip(*states)]
        real = row >= 0.0
        weight = jnp.where(
            real, ((1.0 - picked) + base_term) / jnp.where(real, dense, 1.0), 0.0
        )
        total = total + jnp.sum(weight, axis=1, keepdims=True)
        weights.append(weight)
    out_ref[...] = jnp.broadcast_to(jnp.where(at_work, total, 0.0), out_ref.shape)
    for r in range(2):
        for i in range(2 * chips):
            source = me ^ order[i]
            at = 4 * (source * groups + (group ^ 1)) + r
            out_ref[pl.ds(at, 1), :cap] = weights[r][:, i * cap : (i + 1) * cap]


def finish_kernel(chips, cap, groups, strata_dev, ids_ref, got_ref, out_ref):
    rows = ids_ref.shape[1]
    group = lax.axis_index("grp")
    half = group % 2
    got = got_ref[...]
    row_of = lax.broadcasted_iota(jnp.int32, got.shape, 0) % 4
    total = jnp.sum(jnp.where(row_of == 2, got, 0.0), axis=0, keepdims=True)[:, :1]
    ids = ids_ref[...]
    weight = jnp.zeros((1, rows), jnp.float32)
    for i in range(chips):
        owner = (half * chips + i) * groups + (group ^ 1)
        for r in range(2):
            shard = (half * chips + i) ^ (r * (chips + chips // 2))
            begin = jnp.sum((ids < shard * strata_dev).astype(jnp.int32))
            start = jnp.minimum(begin, rows - cap)
            part = got_ref[pl.ds(4 * owner + r, 1), :]
            part = jnp.broadcast_to(jnp.concatenate([part] * (rows // LANES), axis=1), (8, rows))
            part = pltpu.roll(part, start, axis=1)[:1, :]
            mine = (ids >= shard * strata_dev) & (ids < (shard + 1) * strata_dev)
            weight = jnp.where(mine, part, weight)
    out_ref[...] = weight * (float(rows * 2 * chips * groups) / total)


def body(embeddings, strata, centroids):
    shards, groups = lax.axis_size("blk"), lax.axis_size("grp")
    chips = shards // 2
    rows, width = embeddings.shape[1:]
    strata_dev = centroids.shape[1]
    cap = 2 * rows // shards
    chunks = width // LANES
    depth = chunks * 2 * cap + TAIL
    each = chips * cap
    every = [(b, g) for b in range(shards) for g in range(groups)]
    kind_a = [(b, g) for b, g in every if b // chips == g % 2]
    kind_b = [(b, g) for b, g in every if b // chips != g % 2]
    inner = [(b, g) for b, g in kind_b if b % chips // (chips // 2) != b // chips]
    outer = [(b, g) for b, g in kind_b if (b, g) not in inner]
    side = chips // 2
    flip = chips + side

    def send(array, pairs):
        return lax.ppermute(
            array, AXES, [(b * groups + g, to_b * groups + to_g) for (b, g), (to_b, to_g) in pairs]
        )

    def shape(*dims, dtype=jnp.bfloat16):
        return pltpu.VMEM(dims, dtype)

    held = [pltpu.VMEM((rows, width), jnp.bfloat16), pltpu.VMEM((shards * cap, rows), jnp.bfloat16)]
    order = [0, *reversed(range(1, chips))]
    swap = [((b, g), (b ^ flip, g ^ 1)) for b, g in inner]
    far_rows = send(embeddings[0], swap)
    *near, extra = pl.pallas_call(
        functools.partial(near_kernel, chips, cap),
        out_shape=[
            shape(depth + (chunks * strata_dev if d in (0, side) else 0), LANES) for d in range(chips)
        ]
        + [shape(TAIL + chunks * strata_dev, LANES)],
        in_specs=[ANY, VMEM, ANY],
        out_specs=[VMEM] * (chips + 1),
        scratch_shapes=[
            pltpu.VMEM((rows, width), jnp.bfloat16),
            pltpu.VMEM((1, rows), jnp.int32),
            *held,
            pltpu.SemaphoreType.DMA((5,)),
        ],
        compiler_params=params(44),
        cost_estimate=pl.CostEstimate(flops=0, transcendentals=0, bytes_accessed=0),
        name="near",
    )(strata, centroids[0], embeddings[0])
    blocks_a = [
        near[d] if d == 0 else send(near[d], [((b, g), (b ^ d, g)) for b, g in kind_a])
        for d in order
    ]
    extra = send(extra, swap)
    out = pl.pallas_call(
        functools.partial(far_kernel, chips, cap, strata_dev),
        out_shape=[shape(depth, LANES)] * chips,
        in_specs=[VMEM] * (2 + side),
        out_specs=[VMEM] * chips,
        scratch_shapes=held,
        compiler_params=params(20),
        name="far",
    )(extra, far_rows, *near[:side])
    direct = []
    for e in range(side):
        block, _ = lax.optimization_barrier((near[side + e], out[0]))
        direct.append(send(block, [((b, g), (b ^ (flip + e), g ^ 1)) for b, g in outer]))
    spread = [
        out[e] if e == 0 else send(out[e], [((b, g), (b ^ e, g)) for b, g in inner])
        for e in range(side)
    ]
    last = [
        send(
            out[side + e],
            [((b, g), (b ^ (chips + e), g ^ 1)) for b, g in outer]
            + [((b, g), (b ^ (side + e), g)) for b, g in inner],
        )
        for e in range(side)
    ]
    group_a = pl.pallas_call(
        functools.partial(early_kernel, chips, cap, strata_dev),
        out_shape=shape(2 * each + strata_dev + TAIL, width),
        in_specs=[ANY] + [VMEM] * chips,
        out_specs=VMEM,
        scratch_shapes=[pltpu.VMEM((2 * each, LANES), jnp.float32)],
        compiler_params=params(20),
        name="early",
    )(out[0], *blocks_a)
    group_a = send(group_a, [((b, g), (b, g ^ 1)) for b, g in kind_a])
    units_m, col_m, facts_m, facts_a, col_a, cents = pl.pallas_call(
        functools.partial(mid_kernel, chips, cap),
        out_shape=[
            shape(2 * side * cap, width),
            shape(2 * side * cap, LANES, dtype=jnp.float32),
            shape(8, side * cap, dtype=jnp.float32),
            shape(8, each, dtype=jnp.float32),
            shape(2 * each, LANES, dtype=jnp.float32),
            shape(2 * strata_dev, width),
        ],
        in_specs=[VMEM] * (chips + 2),
        out_specs=[VMEM] * 6,
        compiler_params=params(20),
        name="mid",
    )(group_a, extra, *direct, *spread)
    sent = pl.pallas_call(
        functools.partial(
            late_kernel,
            [*order, *(flip + e for e in range(side)), *(chips + e for e in range(side))],
            cap,
            groups,
        ),
        out_shape=jax.ShapeDtypeStruct((shards * groups * 4, LANES), jnp.float32),
        in_specs=[VMEM] * (7 + side),
        out_specs=VMEM,
        scratch_shapes=[
            pltpu.VMEM((2 * side * cap, width), jnp.bfloat16),
            pltpu.VMEM((2 * side * cap, LANES), jnp.float32),
        ],
        compiler_params=params(20),
        name="late",
    )(group_a, col_a, facts_a, units_m, col_m, facts_m, cents, *last)
    got = lax.all_to_all(
        sent.reshape(shards * groups, 4, LANES), AXES, 0, 0, tiled=True
    ).reshape(shards * groups * 4, LANES)
    return pl.pallas_call(
        functools.partial(finish_kernel, chips, cap, groups, strata_dev),
        out_shape=jax.ShapeDtypeStruct((1, rows), jnp.float32),
        in_specs=[VMEM, VMEM],
        out_specs=VMEM,
        compiler_params=params(8),
        name="finish",
    )(strata, got)


def solution(mesh):
    placed = (P("grp", "blk", None), P("grp", "blk"), P("grp", "blk", None))
    return jax.shard_map(
        body, mesh=mesh, in_specs=placed, out_specs=P("grp", "blk"), check_vma=False
    )
```

```python
import functools
import math

import jax
import jax.numpy as jnp
from jax import lax
from jax.experimental import pallas as pl
from jax.experimental.pallas import tpu as pltpu
from jax.sharding import PartitionSpec as P


base_term = 0.05
epsilon = 1e-06
LANES = 128
TAIL = 16
AXES = ("blk", "grp")

VMEM = pl.BlockSpec(memory_space=pltpu.VMEM)
ANY = pl.BlockSpec(memory_space=pl.ANY)


def params(mib):
    return pltpu.CompilerParams(vmem_limit_bytes=mib << 20)


def unit_values(rows):
    values = rows.astype(jnp.float32)
    mean = jnp.mean(values * values, axis=-1, keepdims=True)
    scaling = lax.rsqrt(mean + epsilon) / math.sqrt(rows.shape[-1])
    return (values * scaling).astype(jnp.bfloat16)


def across(left, right):
    return lax.dot_general(
        left, right, (((1,), (1,)), ((), ())), preferred_element_type=jnp.float32
    )


def is_inner(chips):
    me = lax.axis_index("blk")
    return (me % chips) // (chips // 2) != me // chips


def shard_of(k, chips, half):
    owner = half * chips + ((lax.axis_index("blk") % chips) ^ (k // 2))
    return owner ^ ((k % 2) * (chips + chips // 2))


def pack_into(ids, loads, rows_ref, outs, held, pick, cap, strata_dev, half):
    rows, width = rows_ref.shape
    chips = len(outs)
    shards = 2 * chips
    number = lax.broadcasted_iota(jnp.int32, (shards, 1), 0)
    lowest = (shard_of(number, chips, half) * strata_dev).astype(jnp.float32)
    begin = jnp.sum((ids < lowest).astype(jnp.float32), axis=1, keepdims=True)
    start = jnp.minimum(begin, float(rows - cap))
    number = lax.broadcasted_iota(jnp.int32, (shards * strata_dev, 1), 0)
    stratum = shard_of(number // strata_dev, chips, half) * strata_dev + number % strata_dev
    ends = jnp.sum((ids <= stratum.astype(jnp.float32)).astype(jnp.float32), axis=1, keepdims=True)
    slot = lax.broadcasted_iota(jnp.int32, (cap, rows), 0).astype(jnp.float32)
    row = lax.broadcasted_iota(jnp.int32, (cap, rows), 1).astype(jnp.float32)
    ahead = row - slot
    lane = lax.broadcasted_iota(jnp.int32, (1, LANES), 1).astype(jnp.float32)
    for k in range(shards):
        first = start[k : k + 1, :]
        pick[k * cap : (k + 1) * cap, :] = (ahead == first).astype(jnp.bfloat16)
        at = lane + first
        passed = (ends[k * strata_dev : (k + 1) * strata_dev, :] <= at).astype(jnp.float32)
        local = jnp.where(
            at >= begin[k : k + 1, :], jnp.sum(passed, axis=0, keepdims=True), float(strata_dev)
        )
        tail = width // LANES * 2 * cap + (k % 2) * 8
        outs[k // 2][tail : tail + 8, :] = jnp.broadcast_to(local, (8, LANES)).astype(jnp.bfloat16)
    step = rows // max(len(loads), 1)
    for i, load in enumerate(loads):
        load.wait()
        held[i * step : (i + 1) * step, :] = unit_values(rows_ref[i * step : (i + 1) * step, :])
    if not loads:
        held[...] = unit_values(rows_ref[...])
    wide = 2 * LANES
    for c in range(width // wide):
        runs = jnp.dot(
            pick[...], held[:, c * wide : (c + 1) * wide], preferred_element_type=jnp.float32
        ).astype(jnp.bfloat16)
        for d, out in enumerate(outs):
            for part in range(2):
                at = (2 * c + part) * 2 * cap
                out[at : at + 2 * cap, :] = runs[
                    d * 2 * cap : (d + 1) * 2 * cap, part * LANES : (part + 1) * LANES
                ]


def near_kernel(chips, cap, ids_any, cent_ref, rows_any, *rest):
    outs, (extra, rows_ref, ids_ref, held, pick, sems) = rest[:chips], rest[chips:]
    strata_dev, width = cent_ref.shape
    rows = rows_ref.shape[0]
    pieces = 4
    loads = [pltpu.make_async_copy(ids_any, ids_ref, sems.at[pieces])]
    for i in range(pieces):
        at = pl.ds(i * (rows // pieces), rows // pieces)
        loads.append(pltpu.make_async_copy(rows_any.at[at, :], rows_ref.at[at, :], sems.at[i]))
    for load in loads:
        load.start()
    cent = unit_values(cent_ref[...])
    depth = width // LANES * 2 * cap + TAIL
    for c in range(width // LANES):
        at = depth + c * strata_dev
        for out in (outs[0], outs[chips // 2]):
            out[at : at + strata_dev, :] = cent[:, c * LANES : (c + 1) * LANES]
    loads[0].wait()
    ids = ids_ref[...].astype(jnp.float32)
    for c in range(width // LANES):
        at = TAIL + c * strata_dev
        extra[at : at + strata_dev, :] = cent[:, c * LANES : (c + 1) * LANES]
    extra[:TAIL, :] = jnp.concatenate(
        [
            jnp.broadcast_to(ids[:, i * LANES : (i + 1) * LANES], (TAIL // 4, LANES))
            for i in range(rows // LANES)
        ],
        axis=0,
    ).astype(jnp.bfloat16)
    half = lax.axis_index("grp") % 2
    pack_into(ids, loads[1:], rows_ref, outs, held, pick, cap, strata_dev, half)


def far_kernel(chips, cap, strata_dev, extra, rows_ref, *rest):
    inner = is_inner(chips)
    direct, outs, (held, pick) = rest[: chips // 2], rest[chips // 2 : -2], rest[-2:]

    @pl.when(inner)
    def _():
        spread = extra[:TAIL, :].astype(jnp.float32)
        ids = jnp.concatenate([spread[i : i + 1, :] for i in range(0, TAIL, TAIL // 4)], axis=1)
        half = lax.axis_index("blk") // chips
        pack_into(ids, [], rows_ref, outs, held, pick, cap, strata_dev, half)

    @pl.when(jnp.logical_not(inner))
    def _():
        for block, out in zip(direct, outs[chips // 2 :]):
            out[...] = block[: out.shape[0], :]


def unpack(blocks, cap, strata_dev, units, id_col, others=None, use_others=None):
    each = len(blocks) * cap
    width = units.shape[1]
    depth = width // LANES * 2 * cap

    def lay(some):
        for i, block in enumerate(some):
            for r in range(2):
                at = r * each + i * cap
                for c in range(width // LANES):
                    units[at : at + cap, c * LANES : (c + 1) * LANES] = block[
                        (2 * c + r) * cap : (2 * c + r + 1) * cap, :
                    ]

    if others is None:
        lay(blocks)
    else:
        pl.when(use_others)(lambda: lay(others))
        pl.when(jnp.logical_not(use_others))(lambda: lay(blocks))
    id_rows = [[], []]
    for i, block in enumerate(blocks):
        tail = block[depth : depth + TAIL, :].astype(jnp.float32)
        if others is not None:
            other = others[i][depth : depth + TAIL, :].astype(jnp.float32)
            tail = jnp.where(
                jnp.broadcast_to(use_others.astype(jnp.int32), tail.shape) > 0, other, tail
            )
        for r in range(2):
            at = r * each + i * cap
            ids = tail[8 * r : 8 * r + 1, :]
            ids = jnp.where(ids < float(strata_dev), ids, -1.0)
            id_rows[r].append(ids[:, :cap])
            id_col[at : at + cap, :] = jnp.broadcast_to(ids, (LANES, LANES)).T[:cap, :]
    return [jnp.concatenate(rows, axis=1) for rows in id_rows]


def masked_exp(scores, id_col, id_key):
    same = jnp.concatenate([id_col] * (scores.shape[1] // LANES), axis=1) == id_key
    return jnp.where(same, jnp.exp((scores - 1.0) * 4.0), 0.0)


def fold(kernel):
    rows, lanes = kernel.shape
    return jnp.sum(kernel.reshape(rows // 8, 8, lanes), axis=0)


def key_of(id_row):
    return jnp.where(id_row >= 0.0, id_row, -2.0)


def own_centroid(near, id_row):
    which = lax.broadcasted_iota(jnp.int32, near.shape, 0).astype(jnp.float32)
    return jnp.sum(jnp.where(which == id_row, near, 0.0), axis=0, keepdims=True)


def transposed_sum(kernel):
    part = kernel[:, :LANES]
    for c in range(1, kernel.shape[1] // LANES):
        part = part + kernel[:, c * LANES : (c + 1) * LANES]
    return jnp.concatenate(
        [
            jnp.sum(part[i * LANES : (i + 1) * LANES, :].T, axis=0, keepdims=True)
            for i in range(part.shape[0] // LANES)
        ],
        axis=1,
    )


def join(groups, units, id_col, ids, cents=None):
    earlier, new, picked = [[] for _ in groups], [], []
    for r, row in enumerate(ids):
        key = key_of(row)
        each = row.shape[1]
        mine = units[r * each : (r + 1) * each, :]
        left = mine
        if cents is not None:
            strata_dev = cents.shape[0] // 2
            left = jnp.concatenate([mine, cents[r * strata_dev : (r + 1) * strata_dev, :]], axis=0)
        scores = across(left, mine)
        if cents is not None:
            picked.append(own_centroid(scores[each:, :], row))
        sums = fold(masked_exp(scores[:each, :], id_col[r * each : (r + 1) * each, :], key))
        for sums_of, (old_units, old_col, old_density) in zip(earlier, groups):
            size = old_density[r].shape[1]
            at = slice(r * size, (r + 1) * size)
            kernel = masked_exp(across(old_units[at, :], mine), old_col[at, :], key)
            sums = sums + fold(kernel)
            sums_of.append(old_density[r] + transposed_sum(kernel))
        new.append(jnp.sum(sums, axis=0, keepdims=True))
    return earlier, new, picked


def parts_of(value):
    high = value.astype(jnp.bfloat16).astype(jnp.float32)
    middle = (value - high).astype(jnp.bfloat16).astype(jnp.float32)
    return [high, middle, value - high - middle]


def early_kernel(chips, cap, strata_dev, after, *rest):
    blocks, (held, id_col) = rest[:chips], rest[chips:]
    in_a = lax.axis_index("grp") % 2 == lax.axis_index("blk") // chips

    @pl.when(in_a)
    def _():
        width = held.shape[1]
        each = chips * cap
        depth = width // LANES * 2 * cap + TAIL
        ids = unpack(blocks, cap, strata_dev, held, id_col)
        for c in range(width // LANES):
            at = depth + c * strata_dev
            held[2 * each : 2 * each + strata_dev, c * LANES : (c + 1) * LANES] = blocks[0][
                at : at + strata_dev, :
            ]
        _, density, _ = join([], held, id_col, ids)
        rows = [*parts_of(density[0]), *parts_of(density[1]), *ids]
        tail = jnp.concatenate(rows + rows, axis=0).astype(jnp.bfloat16)
        held[2 * each + strata_dev :, :each] = tail


def mid_kernel(chips, cap, group_a, extra, *rest):
    direct, spread, (units, id_col, facts, facts_a, col_a, cents) = (
        rest[: chips // 2],
        rest[chips // 2 : chips],
        rest[chips:],
    )
    inner = is_inner(chips)
    strata_dev, width = cents.shape[0] // 2, cents.shape[1]
    depth = width // LANES * 2 * cap + TAIL
    each = chips * cap

    def place(block, base):
        for c in range(width // LANES):
            at = base + c * strata_dev
            cents[strata_dev:, c * LANES : (c + 1) * LANES] = block[at : at + strata_dev, :]

    cents[:strata_dev, :] = group_a[2 * each : 2 * each + strata_dev, :]
    pl.when(inner)(lambda: place(extra, TAIL))
    pl.when(jnp.logical_not(inner))(lambda: place(direct[0], depth))
    tail = group_a[2 * each + strata_dev :, :each].astype(jnp.float32)
    density_a = []
    for r in range(2):
        density_a.append(
            tail[3 * r : 3 * r + 1, :] + tail[3 * r + 1 : 3 * r + 2, :] + tail[3 * r + 2 : 3 * r + 3, :]
        )
        row = tail[6 + r : 7 + r, :]
        col_a[r * each : (r + 1) * each, :] = upright(row)
        facts_a[2 + r : 3 + r, :] = row
        near = cents[r * strata_dev : (r + 1) * strata_dev, :]
        facts_a[4 + r : 5 + r, :] = own_centroid(
            across(near, group_a[r * each : (r + 1) * each, :]), row
        )
    ids = unpack(direct, cap, strata_dev, units, id_col, spread, inner)
    (old,), density, picked = join([(group_a, col_a, density_a)], units, id_col, ids, cents)
    for r, row in enumerate(ids):
        facts[r : r + 1, :] = density[r]
        facts[2 + r : 3 + r, :] = row
        facts[4 + r : 5 + r, :] = picked[r]
        facts_a[r : r + 1, :] = old[r]


def upright(row):
    return jnp.concatenate(
        [
            jnp.broadcast_to(row[:, i * LANES : (i + 1) * LANES], (LANES, LANES)).T
            for i in range(row.shape[1] // LANES)
        ],
        axis=0,
    )


def late_kernel(order, cap, groups, units_a, col_a, facts_a, units_m, col_m, facts_m, cents, *rest):
    blocks, (out_ref, units, id_col) = rest[:-3], rest[-3:]
    strata_dev = cents.shape[0] // 2
    chips = len(order) // 2
    me, group = lax.axis_index("blk"), lax.axis_index("grp")
    at_work = (me // chips) != (group % 2)
    ids = unpack(blocks, cap, strata_dev, units, id_col)
    old = [
        (some, col, [facts[r : r + 1, :] for r in range(2)])
        for some, col, facts in ((units_a, col_a, facts_a), (units_m, col_m, facts_m))
    ]
    earlier, density, picked_new = join(old, units, id_col, ids, cents)
    total = jnp.zeros((1, 1), jnp.float32)
    weights = []
    for r, row in enumerate(ids):
        states = [
            (facts_a[2 + r : 3 + r, :], facts_a[4 + r : 5 + r, :], earlier[0][r]),
            (facts_m[2 + r : 3 + r, :], facts_m[4 + r : 5 + r, :], earlier[1][r]),
            (row, picked_new[r], density[r]),
        ]
        row, picked, dense = [jnp.concatenate(parts, axis=1) for parts in zip(*states)]
        real = row >= 0.0
        weight = jnp.where(
            real, ((1.0 - picked) + base_term) / jnp.where(real, dense, 1.0), 0.0
        )
        total = total + jnp.sum(weight, axis=1, keepdims=True)
        weights.append(weight)
    out_ref[...] = jnp.broadcast_to(jnp.where(at_work, total, 0.0), out_ref.shape)
    for r in range(2):
        for i in range(2 * chips):
            source = me ^ order[i]
            at = 4 * (source * groups + (group ^ 1)) + r
            out_ref[pl.ds(at, 1), :cap] = weights[r][:, i * cap : (i + 1) * cap]


def finish_kernel(chips, cap, groups, strata_dev, ids_ref, got_ref, out_ref):
    rows = ids_ref.shape[1]
    group = lax.axis_index("grp")
    half = group % 2
    got = got_ref[...]
    row_of = lax.broadcasted_iota(jnp.int32, got.shape, 0) % 4
    total = jnp.sum(jnp.where(row_of == 2, got, 0.0), axis=0, keepdims=True)[:, :1]
    ids = ids_ref[...]
    weight = jnp.zeros((1, rows), jnp.float32)
    for i in range(chips):
        owner = (half * chips + i) * groups + (group ^ 1)
        for r in range(2):
            shard = (half * chips + i) ^ (r * (chips + chips // 2))
            begin = jnp.sum((ids < shard * strata_dev).astype(jnp.int32))
            start = jnp.minimum(begin, rows - cap)
            part = got_ref[pl.ds(4 * owner + r, 1), :]
            part = jnp.broadcast_to(jnp.concatenate([part] * (rows // LANES), axis=1), (8, rows))
            part = pltpu.roll(part, start, axis=1)[:1, :]
            mine = (ids >= shard * strata_dev) & (ids < (shard + 1) * strata_dev)
            weight = jnp.where(mine, part, weight)
    out_ref[...] = weight * (float(rows * 2 * chips * groups) / total)


def body(embeddings, strata, centroids):
    shards, groups = lax.axis_size("blk"), lax.axis_size("grp")
    chips = shards // 2
    rows, width = embeddings.shape[1:]
    strata_dev = centroids.shape[1]
    cap = 2 * rows // shards
    chunks = width // LANES
    depth = chunks * 2 * cap + TAIL
    each = chips * cap
    every = [(b, g) for b in range(shards) for g in range(groups)]
    kind_a = [(b, g) for b, g in every if b // chips == g % 2]
    kind_b = [(b, g) for b, g in every if b // chips != g % 2]
    inner = [(b, g) for b, g in kind_b if b % chips // (chips // 2) != b // chips]
    outer = [(b, g) for b, g in kind_b if (b, g) not in inner]
    side = chips // 2
    flip = chips + side

    def send(array, pairs):
        return lax.ppermute(
            array, AXES, [(b * groups + g, to_b * groups + to_g) for (b, g), (to_b, to_g) in pairs]
        )

    def shape(*dims, dtype=jnp.bfloat16):
        return pltpu.VMEM(dims, dtype)

    held = [pltpu.VMEM((rows, width), jnp.bfloat16), pltpu.VMEM((shards * cap, rows), jnp.bfloat16)]
    order = [0, *reversed(range(1, chips))]
    swap = [((b, g), (b ^ flip, g ^ 1)) for b, g in inner]
    far_rows = send(embeddings[0], swap)
    *near, extra = pl.pallas_call(
        functools.partial(near_kernel, chips, cap),
        out_shape=[
            shape(depth + (chunks * strata_dev if d in (0, side) else 0), LANES) for d in range(chips)
        ]
        + [shape(TAIL + chunks * strata_dev, LANES)],
        in_specs=[ANY, VMEM, ANY],
        out_specs=[VMEM] * (chips + 1),
        scratch_shapes=[
            pltpu.VMEM((rows, width), jnp.bfloat16),
            pltpu.VMEM((1, rows), jnp.int32),
            *held,
            pltpu.SemaphoreType.DMA((5,)),
        ],
        compiler_params=params(56),
        cost_estimate=pl.CostEstimate(flops=0, transcendentals=0, bytes_accessed=0),
        name="near",
    )(strata, centroids[0], embeddings[0])
    blocks_a = [
        near[d] if d == 0 else send(near[d], [((b, g), (b ^ d, g)) for b, g in kind_a])
        for d in order
    ]
    extra = send(extra, swap)
    out = pl.pallas_call(
        functools.partial(far_kernel, chips, cap, strata_dev),
        out_shape=[shape(depth, LANES)] * chips,
        in_specs=[VMEM] * (2 + side),
        out_specs=[VMEM] * chips,
        scratch_shapes=held,
        compiler_params=params(20),
        name="far",
    )(extra, far_rows, *near[:side])
    direct = []
    for e in range(side):
        block, _ = lax.optimization_barrier((near[side + e], out[0]))
        direct.append(send(block, [((b, g), (b ^ (flip + e), g ^ 1)) for b, g in outer]))
    spread = [
        out[e] if e == 0 else send(out[e], [((b, g), (b ^ e, g)) for b, g in inner])
        for e in range(side)
    ]
    last = [
        send(
            out[side + e],
            [((b, g), (b ^ (chips + e), g ^ 1)) for b, g in outer]
            + [((b, g), (b ^ (side + e), g)) for b, g in inner],
        )
        for e in range(side)
    ]
    group_a = pl.pallas_call(
        functools.partial(early_kernel, chips, cap, strata_dev),
        out_shape=shape(2 * each + strata_dev + TAIL, width),
        in_specs=[ANY] + [VMEM] * chips,
        out_specs=VMEM,
        scratch_shapes=[pltpu.VMEM((2 * each, LANES), jnp.float32)],
        compiler_params=params(20),
        name="early",
    )(out[0], *blocks_a)
    group_a = send(group_a, [((b, g), (b, g ^ 1)) for b, g in kind_a])
    units_m, col_m, facts_m, facts_a, col_a, cents = pl.pallas_call(
        functools.partial(mid_kernel, chips, cap),
        out_shape=[
            shape(2 * side * cap, width),
            shape(2 * side * cap, LANES, dtype=jnp.float32),
            shape(8, side * cap, dtype=jnp.float32),
            shape(8, each, dtype=jnp.float32),
            shape(2 * each, LANES, dtype=jnp.float32),
            shape(2 * strata_dev, width),
        ],
        in_specs=[VMEM] * (chips + 2),
        out_specs=[VMEM] * 6,
        compiler_params=params(20),
        name="mid",
    )(group_a, extra, *direct, *spread)
    sent = pl.pallas_call(
        functools.partial(
            late_kernel,
            [*order, *(flip + e for e in range(side)), *(chips + e for e in range(side))],
            cap,
            groups,
        ),
        out_shape=jax.ShapeDtypeStruct((shards * groups * 4, LANES), jnp.float32),
        in_specs=[VMEM] * (7 + side),
        out_specs=VMEM,
        scratch_shapes=[
            pltpu.VMEM((2 * side * cap, width), jnp.bfloat16),
            pltpu.VMEM((2 * side * cap, LANES), jnp.float32),
        ],
        compiler_params=params(20),
        name="late",
    )(group_a, col_a, facts_a, units_m, col_m, facts_m, cents, *last)
    got = lax.all_to_all(
        sent.reshape(shards * groups, 4, LANES), AXES, 0, 0, tiled=True
    ).reshape(shards * groups * 4, LANES)
    return pl.pallas_call(
        functools.partial(finish_kernel, chips, cap, groups, strata_dev),
        out_shape=jax.ShapeDtypeStruct((1, rows), jnp.float32),
        in_specs=[VMEM, VMEM],
        out_specs=VMEM,
        compiler_params=params(8),
        name="finish",
    )(strata, got)


def solution(mesh):
    placed = (P("grp", "blk", None), P("grp", "blk"), P("grp", "blk", None))
    return jax.shard_map(
        body, mesh=mesh, in_specs=placed, out_specs=P("grp", "blk"), check_vma=False
    )
```

```python
import functools
import math

import jax
import jax.numpy as jnp
from jax import lax
from jax.experimental import pallas as pl
from jax.experimental.pallas import tpu as pltpu
from jax.sharding import PartitionSpec as P


base_term = 0.05
epsilon = 1e-06
LANES = 128
TAIL = 16
AXES = ("blk", "grp")

VMEM = pl.BlockSpec(memory_space=pltpu.VMEM)
ANY = pl.BlockSpec(memory_space=pl.ANY)


def params(mib):
    return pltpu.CompilerParams(vmem_limit_bytes=mib << 20)


def unit_values(rows):
    values = rows.astype(jnp.float32)
    mean = jnp.mean(values * values, axis=-1, keepdims=True)
    scaling = lax.rsqrt(mean + epsilon) / math.sqrt(rows.shape[-1])
    return (values * scaling).astype(jnp.bfloat16)


def across(left, right):
    return lax.dot_general(
        left, right, (((1,), (1,)), ((), ())), preferred_element_type=jnp.float32
    )


def is_inner(chips):
    me = lax.axis_index("blk")
    return (me % chips) // (chips // 2) != me // chips


def shard_of(k, chips, half):
    owner = half * chips + ((lax.axis_index("blk") % chips) ^ (k // 2))
    return owner ^ ((k % 2) * (chips + chips // 2))


def pack_into(ids, loads, rows_ref, outs, held, pick, cap, strata_dev, half):
    rows, width = rows_ref.shape
    chips = len(outs)
    shards = 2 * chips
    number = lax.broadcasted_iota(jnp.int32, (shards, 1), 0)
    lowest = (shard_of(number, chips, half) * strata_dev).astype(jnp.float32)
    begin = jnp.sum((ids < lowest).astype(jnp.float32), axis=1, keepdims=True)
    start = jnp.minimum(begin, float(rows - cap))
    number = lax.broadcasted_iota(jnp.int32, (shards * strata_dev, 1), 0)
    stratum = shard_of(number // strata_dev, chips, half) * strata_dev + number % strata_dev
    ends = jnp.sum((ids <= stratum.astype(jnp.float32)).astype(jnp.float32), axis=1, keepdims=True)
    slot = lax.broadcasted_iota(jnp.int32, (cap, rows), 0).astype(jnp.float32)
    row = lax.broadcasted_iota(jnp.int32, (cap, rows), 1).astype(jnp.float32)
    ahead = row - slot
    lane = lax.broadcasted_iota(jnp.int32, (1, LANES), 1).astype(jnp.float32)
    for k in range(shards):
        first = start[k : k + 1, :]
        pick[k * cap : (k + 1) * cap, :] = (ahead == first).astype(jnp.bfloat16)
        at = lane + first
        passed = (ends[k * strata_dev : (k + 1) * strata_dev, :] <= at).astype(jnp.float32)
        local = jnp.where(
            at >= begin[k : k + 1, :], jnp.sum(passed, axis=0, keepdims=True), float(strata_dev)
        )
        tail = width // LANES * 2 * cap + (k % 2) * 8
        outs[k // 2][tail : tail + 8, :] = jnp.broadcast_to(local, (8, LANES)).astype(jnp.bfloat16)
    step = rows // max(len(loads), 1)
    for i, load in enumerate(loads):
        load.wait()
        held[i * step : (i + 1) * step, :] = unit_values(rows_ref[i * step : (i + 1) * step, :])
    if not loads:
        held[...] = unit_values(rows_ref[...])
    wide = 2 * LANES
    for c in range(width // wide):
        runs = jnp.dot(
            pick[...], held[:, c * wide : (c + 1) * wide], preferred_element_type=jnp.float32
        ).astype(jnp.bfloat16)
        for d, out in enumerate(outs):
            for part in range(2):
                at = (2 * c + part) * 2 * cap
                out[at : at + 2 * cap, :] = runs[
                    d * 2 * cap : (d + 1) * 2 * cap, part * LANES : (part + 1) * LANES
                ]


def near_kernel(chips, cap, ids_any, cent_ref, rows_any, *rest):
    outs, (extra, rows_ref, ids_ref, held, pick, sems) = rest[:chips], rest[chips:]
    strata_dev, width = cent_ref.shape
    rows = rows_ref.shape[0]
    pieces = 4
    loads = [pltpu.make_async_copy(ids_any, ids_ref, sems.at[pieces])]
    for i in range(pieces):
        at = pl.ds(i * (rows // pieces), rows // pieces)
        loads.append(pltpu.make_async_copy(rows_any.at[at, :], rows_ref.at[at, :], sems.at[i]))
    for load in loads:
        load.start()
    cent = unit_values(cent_ref[...])
    depth = width // LANES * 2 * cap + TAIL
    for c in range(width // LANES):
        at = depth + c * strata_dev
        for out in (outs[0], outs[chips // 2]):
            out[at : at + strata_dev, :] = cent[:, c * LANES : (c + 1) * LANES]
    loads[0].wait()
    ids = ids_ref[...].astype(jnp.float32)
    for c in range(width // LANES):
        at = TAIL + c * strata_dev
        extra[at : at + strata_dev, :] = cent[:, c * LANES : (c + 1) * LANES]
    extra[:TAIL, :] = jnp.concatenate(
        [
            jnp.broadcast_to(ids[:, i * LANES : (i + 1) * LANES], (TAIL // 4, LANES))
            for i in range(rows // LANES)
        ],
        axis=0,
    ).astype(jnp.bfloat16)
    half = lax.axis_index("grp") % 2
    pack_into(ids, loads[1:], rows_ref, outs, held, pick, cap, strata_dev, half)


def far_kernel(chips, cap, strata_dev, extra, rows_ref, *rest):
    in_a = lax.axis_index("grp") % 2 == lax.axis_index("blk") // chips
    packs = jnp.logical_or(in_a, is_inner(chips))
    own, outs, (held, pick) = rest[: chips - 1], rest[chips - 1 : -2], rest[-2:]

    @pl.when(packs)
    def _():
        spread = extra[:TAIL, :].astype(jnp.float32)
        ids = jnp.concatenate([spread[i : i + 1, :] for i in range(0, TAIL, TAIL // 4)], axis=1)
        half = lax.axis_index("blk") // chips
        pack_into(ids, [], rows_ref, outs, held, pick, cap, strata_dev, half)

    @pl.when(jnp.logical_not(packs))
    def _():
        for block, out in zip(own, outs[1:]):
            out[...] = block[: out.shape[0], :]


def unpack(blocks, cap, strata_dev, units, id_col, other=None, use_other=None):
    each = len(blocks) * cap
    width = units.shape[1]
    depth = width // LANES * 2 * cap

    def lay(i, block):
        for r in range(2):
            at = r * each + i * cap
            for c in range(width // LANES):
                units[at : at + cap, c * LANES : (c + 1) * LANES] = block[
                    (2 * c + r) * cap : (2 * c + r + 1) * cap, :
                ]

    id_rows = [[], []]
    for i, block in enumerate(blocks):
        tail = block[depth : depth + TAIL, :].astype(jnp.float32)
        if i == 0 and other is not None:
            pl.when(use_other)(lambda: lay(0, other))
            pl.when(jnp.logical_not(use_other))(lambda: lay(0, blocks[0]))
            tail = jnp.where(
                jnp.broadcast_to(use_other.astype(jnp.int32), tail.shape) > 0,
                other[depth : depth + TAIL, :].astype(jnp.float32),
                tail,
            )
        else:
            lay(i, block)
        for r in range(2):
            at = r * each + i * cap
            ids = tail[8 * r : 8 * r + 1, :]
            ids = jnp.where(ids < float(strata_dev), ids, -1.0)
            id_rows[r].append(ids[:, :cap])
            id_col[at : at + cap, :] = jnp.broadcast_to(ids, (LANES, LANES)).T[:cap, :]
    return [jnp.concatenate(rows, axis=1) for rows in id_rows]


def masked_exp(scores, id_col, id_key):
    same = jnp.concatenate([id_col] * (scores.shape[1] // LANES), axis=1) == id_key
    return jnp.where(same, jnp.exp((scores - 1.0) * 4.0), 0.0)


def fold(kernel):
    rows, lanes = kernel.shape
    return jnp.sum(kernel.reshape(rows // 8, 8, lanes), axis=0)


def key_of(id_row):
    return jnp.where(id_row >= 0.0, id_row, -2.0)


def own_centroid(near, id_row):
    which = lax.broadcasted_iota(jnp.int32, near.shape, 0).astype(jnp.float32)
    return jnp.sum(jnp.where(which == id_row, near, 0.0), axis=0, keepdims=True)


def transposed_sum(kernel):
    part = kernel[:, :LANES]
    for c in range(1, kernel.shape[1] // LANES):
        part = part + kernel[:, c * LANES : (c + 1) * LANES]
    return jnp.concatenate(
        [
            jnp.sum(part[i * LANES : (i + 1) * LANES, :].T, axis=0, keepdims=True)
            for i in range(part.shape[0] // LANES)
        ],
        axis=1,
    )


def join(groups, units, id_col, ids, cents=None):
    earlier, new, picked = [[] for _ in groups], [], []
    for r, row in enumerate(ids):
        key = key_of(row)
        each = row.shape[1]
        mine = units[r * each : (r + 1) * each, :]
        left = mine
        if cents is not None:
            strata_dev = cents.shape[0] // 2
            left = jnp.concatenate([mine, cents[r * strata_dev : (r + 1) * strata_dev, :]], axis=0)
        scores = across(left, mine)
        if cents is not None:
            picked.append(own_centroid(scores[each:, :], row))
        sums = fold(masked_exp(scores[:each, :], id_col[r * each : (r + 1) * each, :], key))
        for sums_of, (old_units, old_col, old_density) in zip(earlier, groups):
            size = old_density[r].shape[1]
            at = slice(r * size, (r + 1) * size)
            kernel = masked_exp(across(old_units[at, :], mine), old_col[at, :], key)
            sums = sums + fold(kernel)
            sums_of.append(old_density[r] + transposed_sum(kernel))
        new.append(jnp.sum(sums, axis=0, keepdims=True))
    return earlier, new, picked


def parts_of(value):
    high = value.astype(jnp.bfloat16).astype(jnp.float32)
    middle = (value - high).astype(jnp.bfloat16).astype(jnp.float32)
    return [high, middle, value - high - middle]


def early_kernel(chips, cap, strata_dev, after, *rest):
    blocks, (held, id_col) = rest[:chips], rest[chips:]
    in_a = lax.axis_index("grp") % 2 == lax.axis_index("blk") // chips

    @pl.when(in_a)
    def _():
        width = held.shape[1]
        each = chips * cap
        depth = width // LANES * 2 * cap + TAIL
        ids = unpack(blocks, cap, strata_dev, held, id_col)
        for c in range(width // LANES):
            at = depth + c * strata_dev
            held[2 * each : 2 * each + strata_dev, c * LANES : (c + 1) * LANES] = blocks[0][
                at : at + strata_dev, :
            ]
        _, density, _ = join([], held, id_col, ids)
        rows = [*parts_of(density[0]), *parts_of(density[1]), *ids]
        tail = jnp.concatenate(rows + rows, axis=0).astype(jnp.bfloat16)
        held[2 * each + strata_dev :, :each] = tail


def mid_kernel(chips, cap, group_a, extra, *rest):
    kept, blocks, (units, id_col, facts, facts_a, col_a, cents) = rest[0], rest[1:-6], rest[-6:]
    inner = is_inner(chips)
    strata_dev, width = cents.shape[0] // 2, cents.shape[1]
    depth = width // LANES * 2 * cap + TAIL
    each = chips * cap

    def place(block, base):
        for c in range(width // LANES):
            at = base + c * strata_dev
            cents[strata_dev:, c * LANES : (c + 1) * LANES] = block[at : at + strata_dev, :]

    cents[:strata_dev, :] = group_a[2 * each : 2 * each + strata_dev, :]
    pl.when(inner)(lambda: place(extra, TAIL))
    pl.when(jnp.logical_not(inner))(lambda: place(blocks[0], depth))
    tail = group_a[2 * each + strata_dev :, :each].astype(jnp.float32)
    density_a = []
    for r in range(2):
        density_a.append(
            tail[3 * r : 3 * r + 1, :] + tail[3 * r + 1 : 3 * r + 2, :] + tail[3 * r + 2 : 3 * r + 3, :]
        )
        row = tail[6 + r : 7 + r, :]
        col_a[r * each : (r + 1) * each, :] = upright(row)
        facts_a[2 + r : 3 + r, :] = row
        near = cents[r * strata_dev : (r + 1) * strata_dev, :]
        facts_a[4 + r : 5 + r, :] = own_centroid(
            across(near, group_a[r * each : (r + 1) * each, :]), row
        )
    ids = unpack(blocks, cap, strata_dev, units, id_col, kept, inner)
    (old,), density, picked = join([(group_a, col_a, density_a)], units, id_col, ids, cents)
    for r, row in enumerate(ids):
        facts[r : r + 1, :] = density[r]
        facts[2 + r : 3 + r, :] = row
        facts[4 + r : 5 + r, :] = picked[r]
        facts_a[r : r + 1, :] = old[r]


def upright(row):
    return jnp.concatenate(
        [
            jnp.broadcast_to(row[:, i * LANES : (i + 1) * LANES], (LANES, LANES)).T
            for i in range(row.shape[1] // LANES)
        ],
        axis=0,
    )


def late_kernel(order, cap, groups, units_a, col_a, facts_a, units_m, col_m, facts_m, cents, *rest):
    blocks, (out_ref, units, id_col) = rest[:-3], rest[-3:]
    strata_dev = cents.shape[0] // 2
    chips = len(order) // 2
    me, group = lax.axis_index("blk"), lax.axis_index("grp")
    at_work = (me // chips) != (group % 2)
    ids = unpack(blocks, cap, strata_dev, units, id_col)
    old = [
        (some, col, [facts[r : r + 1, :] for r in range(2)])
        for some, col, facts in ((units_a, col_a, facts_a), (units_m, col_m, facts_m))
    ]
    earlier, density, picked_new = join(old, units, id_col, ids, cents)
    total = jnp.zeros((1, 1), jnp.float32)
    weights = []
    for r, row in enumerate(ids):
        states = [
            (facts_a[2 + r : 3 + r, :], facts_a[4 + r : 5 + r, :], earlier[0][r]),
            (facts_m[2 + r : 3 + r, :], facts_m[4 + r : 5 + r, :], earlier[1][r]),
            (row, picked_new[r], density[r]),
        ]
        row, picked, dense = [jnp.concatenate(parts, axis=1) for parts in zip(*states)]
        real = row >= 0.0
        weight = jnp.where(
            real, ((1.0 - picked) + base_term) / jnp.where(real, dense, 1.0), 0.0
        )
        total = total + jnp.sum(weight, axis=1, keepdims=True)
        weights.append(weight)
    out_ref[...] = jnp.broadcast_to(jnp.where(at_work, total, 0.0), out_ref.shape)
    for r in range(2):
        for i in range(2 * chips):
            source = me ^ order[i]
            at = 4 * (source * groups + (group ^ 1)) + r
            out_ref[pl.ds(at, 1), :cap] = weights[r][:, i * cap : (i + 1) * cap]


def finish_kernel(chips, cap, groups, strata_dev, ids_ref, got_ref, out_ref):
    rows = ids_ref.shape[1]
    group = lax.axis_index("grp")
    half = group % 2
    got = got_ref[...]
    row_of = lax.broadcasted_iota(jnp.int32, got.shape, 0) % 4
    total = jnp.sum(jnp.where(row_of == 2, got, 0.0), axis=0, keepdims=True)[:, :1]
    ids = ids_ref[...]
    weight = jnp.zeros((1, rows), jnp.float32)
    for i in range(chips):
        owner = (half * chips + i) * groups + (group ^ 1)
        for r in range(2):
            shard = (half * chips + i) ^ (r * (chips + chips // 2))
            begin = jnp.sum((ids < shard * strata_dev).astype(jnp.int32))
            start = jnp.minimum(begin, rows - cap)
            part = got_ref[pl.ds(4 * owner + r, 1), :]
            part = jnp.broadcast_to(jnp.concatenate([part] * (rows // LANES), axis=1), (8, rows))
            part = pltpu.roll(part, start, axis=1)[:1, :]
            mine = (ids >= shard * strata_dev) & (ids < (shard + 1) * strata_dev)
            weight = jnp.where(mine, part, weight)
    out_ref[...] = weight * (float(rows * 2 * chips * groups) / total)


def body(embeddings, strata, centroids):
    shards, groups = lax.axis_size("blk"), lax.axis_size("grp")
    chips = shards // 2
    rows, width = embeddings.shape[1:]
    strata_dev = centroids.shape[1]
    cap = 2 * rows // shards
    chunks = width // LANES
    depth = chunks * 2 * cap + TAIL
    each = chips * cap
    every = [(b, g) for b in range(shards) for g in range(groups)]
    kind_a = [(b, g) for b, g in every if b // chips == g % 2]
    kind_b = [(b, g) for b, g in every if b // chips != g % 2]
    inner = [(b, g) for b, g in kind_b if b % chips // (chips // 2) != b // chips]
    outer = [(b, g) for b, g in kind_b if (b, g) not in inner]
    side = chips // 2
    flip = chips + side

    def send(array, pairs):
        return lax.ppermute(
            array, AXES, [(b * groups + g, to_b * groups + to_g) for (b, g), (to_b, to_g) in pairs]
        )

    def shape(*dims, dtype=jnp.bfloat16):
        return pltpu.VMEM(dims, dtype)

    held = [pltpu.VMEM((rows, width), jnp.bfloat16), pltpu.VMEM((shards * cap, rows), jnp.bfloat16)]
    swap = [((b, g), (b ^ flip, g ^ 1)) for b, g in inner]
    swap += [((b, g), (b ^ side, g)) for b, g in kind_a]
    far_rows = send(embeddings[0], swap)
    *near, extra = pl.pallas_call(
        functools.partial(near_kernel, chips, cap),
        out_shape=[
            shape(depth + (chunks * strata_dev if d in (0, side) else 0), LANES) for d in range(chips)
        ]
        + [shape(TAIL + chunks * strata_dev, LANES)],
        in_specs=[ANY, VMEM, ANY],
        out_specs=[VMEM] * (chips + 1),
        scratch_shapes=[
            pltpu.VMEM((rows, width), jnp.bfloat16),
            pltpu.VMEM((1, rows), jnp.int32),
            *held,
            pltpu.SemaphoreType.DMA((5,)),
        ],
        compiler_params=params(56),
        cost_estimate=pl.CostEstimate(flops=0, transcendentals=0, bytes_accessed=0),
        name="near",
    )(strata, centroids[0], embeddings[0])
    blocks_a = [
        near[e] if e == 0 else send(near[e], [((b, g), (b ^ e, g)) for b, g in kind_a])
        for e in range(side)
    ]
    extra = send(extra, swap)
    out = pl.pallas_call(
        functools.partial(far_kernel, chips, cap, strata_dev),
        out_shape=[shape(depth, LANES)] * chips,
        in_specs=[VMEM] * (chips + 1),
        out_specs=[VMEM] * chips,
        scratch_shapes=held,
        compiler_params=params(20),
        name="far",
    )(extra, far_rows, *near[side + 1 :], *near[:side])
    block, _ = lax.optimization_barrier((near[side], out[0]))
    first = [send(block, [((b, g), (b ^ flip, g ^ 1)) for b, g in outer])]
    for e in range(1, side):
        first.append(
            send(
                out[e],
                [((b, g), (b ^ (flip + e), g ^ 1)) for b, g in outer]
                + [((b, g), (b ^ e, g)) for b, g in inner],
            )
        )
    last = [
        send(
            out[side + e],
            [((b, g), (b ^ (chips + e), g ^ 1)) for b, g in outer]
            + [((b, g), (b ^ (side + e), g)) for b, g in inner],
        )
        for e in range(side)
    ]
    blocks_a.append(out[0])
    for e in range(1, side):
        blocks_a.append(send(out[e], [((b, g), (b ^ e, g)) for b, g in kind_a]))
    group_a = pl.pallas_call(
        functools.partial(early_kernel, chips, cap, strata_dev),
        out_shape=shape(2 * each + strata_dev + TAIL, width),
        in_specs=[ANY] + [VMEM] * chips,
        out_specs=VMEM,
        scratch_shapes=[pltpu.VMEM((2 * each, LANES), jnp.float32)],
        compiler_params=params(20),
        name="early",
    )(out[0], *blocks_a)
    group_a = send(group_a, [((b, g), (b, g ^ 1)) for b, g in kind_a])
    units_m, col_m, facts_m, facts_a, col_a, cents = pl.pallas_call(
        functools.partial(mid_kernel, chips, cap),
        out_shape=[
            shape(2 * side * cap, width),
            shape(2 * side * cap, LANES, dtype=jnp.float32),
            shape(8, side * cap, dtype=jnp.float32),
            shape(8, each, dtype=jnp.float32),
            shape(2 * each, LANES, dtype=jnp.float32),
            shape(2 * strata_dev, width),
        ],
        in_specs=[VMEM] * (side + 3),
        out_specs=[VMEM] * 6,
        compiler_params=params(20),
        name="mid",
    )(group_a, extra, out[0], *first)
    sent = pl.pallas_call(
        functools.partial(
            late_kernel,
            [*range(chips), *(flip + e for e in range(side)), *(chips + e for e in range(side))],
            cap,
            groups,
        ),
        out_shape=jax.ShapeDtypeStruct((shards * groups * 4, LANES), jnp.float32),
        in_specs=[VMEM] * (7 + side),
        out_specs=VMEM,
        scratch_shapes=[
            pltpu.VMEM((2 * side * cap, width), jnp.bfloat16),
            pltpu.VMEM((2 * side * cap, LANES), jnp.float32),
        ],
        compiler_params=params(20),
        name="late",
    )(group_a, col_a, facts_a, units_m, col_m, facts_m, cents, *last)
    got = lax.all_to_all(
        sent.reshape(shards * groups, 4, LANES), AXES, 0, 0, tiled=True
    ).reshape(shards * groups * 4, LANES)
    return pl.pallas_call(
        functools.partial(finish_kernel, chips, cap, groups, strata_dev),
        out_shape=jax.ShapeDtypeStruct((1, rows), jnp.float32),
        in_specs=[VMEM, VMEM],
        out_specs=VMEM,
        compiler_params=params(8),
        name="finish",
    )(strata, got)


def solution(mesh):
    placed = (P("grp", "blk", None), P("grp", "blk"), P("grp", "blk", None))
    return jax.shard_map(
        body, mesh=mesh, in_specs=placed, out_specs=P("grp", "blk"), check_vma=False
    )
```

```python
import functools
import math

import jax
import jax.numpy as jnp
from jax import lax
from jax.experimental import pallas as pl
from jax.experimental.pallas import tpu as pltpu
from jax.sharding import PartitionSpec as P


base_term = 0.05
epsilon = 1e-06
LANES = 128
TAIL = 16
AXES = ("blk", "grp")

VMEM = pl.BlockSpec(memory_space=pltpu.VMEM)
ANY = pl.BlockSpec(memory_space=pl.ANY)


def params(mib):
    return pltpu.CompilerParams(vmem_limit_bytes=mib << 20)


def unit_values(rows):
    values = rows.astype(jnp.float32)
    mean = jnp.mean(values * values, axis=-1, keepdims=True)
    scaling = lax.rsqrt(mean + epsilon) / math.sqrt(rows.shape[-1])
    return (values * scaling).astype(jnp.bfloat16)


def across(left, right):
    return lax.dot_general(
        left, right, (((1,), (1,)), ((), ())), preferred_element_type=jnp.float32
    )


def is_inner(chips):
    me = lax.axis_index("blk")
    return (me % chips) // (chips // 2) != me // chips


def shard_of(k, chips, half):
    owner = half * chips + ((lax.axis_index("blk") % chips) ^ (k // 2))
    return owner ^ ((k % 2) * (chips + chips // 2))


def pack_into(ids, loads, rows_ref, outs, held, pick, cap, strata_dev, half):
    rows, width = rows_ref.shape
    chips = len(outs)
    shards = 2 * chips
    number = lax.broadcasted_iota(jnp.int32, (shards, 1), 0)
    lowest = (shard_of(number, chips, half) * strata_dev).astype(jnp.float32)
    begin = jnp.sum((ids < lowest).astype(jnp.float32), axis=1, keepdims=True)
    start = jnp.minimum(begin, float(rows - cap))
    number = lax.broadcasted_iota(jnp.int32, (shards * strata_dev, 1), 0)
    stratum = shard_of(number // strata_dev, chips, half) * strata_dev + number % strata_dev
    ends = jnp.sum((ids <= stratum.astype(jnp.float32)).astype(jnp.float32), axis=1, keepdims=True)
    slot = lax.broadcasted_iota(jnp.int32, (cap, rows), 0).astype(jnp.float32)
    row = lax.broadcasted_iota(jnp.int32, (cap, rows), 1).astype(jnp.float32)
    ahead = row - slot
    lane = lax.broadcasted_iota(jnp.int32, (1, LANES), 1).astype(jnp.float32)
    for k in range(shards):
        first = start[k : k + 1, :]
        pick[k * cap : (k + 1) * cap, :] = (ahead == first).astype(jnp.bfloat16)
        at = lane + first
        passed = (ends[k * strata_dev : (k + 1) * strata_dev, :] <= at).astype(jnp.float32)
        local = jnp.where(
            at >= begin[k : k + 1, :], jnp.sum(passed, axis=0, keepdims=True), float(strata_dev)
        )
        tail = width // LANES * 2 * cap + (k % 2) * 8
        outs[k // 2][tail : tail + 8, :] = jnp.broadcast_to(local, (8, LANES)).astype(jnp.bfloat16)
    step = rows // max(len(loads), 1)
    for i, load in enumerate(loads):
        load.wait()
        held[i * step : (i + 1) * step, :] = unit_values(rows_ref[i * step : (i + 1) * step, :])
    if not loads:
        held[...] = unit_values(rows_ref[...])
    wide = 2 * LANES
    for c in range(width // wide):
        runs = jnp.dot(
            pick[...], held[:, c * wide : (c + 1) * wide], preferred_element_type=jnp.float32
        ).astype(jnp.bfloat16)
        for d, out in enumerate(outs):
            for part in range(2):
                at = (2 * c + part) * 2 * cap
                out[at : at + 2 * cap, :] = runs[
                    d * 2 * cap : (d + 1) * 2 * cap, part * LANES : (part + 1) * LANES
                ]


def near_kernel(chips, cap, ids_any, cent_ref, rows_any, *rest):
    outs, (extra, rows_ref, ids_ref, held, pick, sems) = rest[:chips], rest[chips:]
    strata_dev, width = cent_ref.shape
    rows = rows_ref.shape[0]
    pieces = 4
    loads = [pltpu.make_async_copy(ids_any, ids_ref, sems.at[pieces])]
    for i in range(pieces):
        at = pl.ds(i * (rows // pieces), rows // pieces)
        loads.append(pltpu.make_async_copy(rows_any.at[at, :], rows_ref.at[at, :], sems.at[i]))
    for load in loads:
        load.start()
    cent = unit_values(cent_ref[...])
    depth = width // LANES * 2 * cap + TAIL
    for c in range(width // LANES):
        at = depth + c * strata_dev
        for out in (outs[0], outs[chips // 2]):
            out[at : at + strata_dev, :] = cent[:, c * LANES : (c + 1) * LANES]
    loads[0].wait()
    ids = ids_ref[...].astype(jnp.float32)
    for c in range(width // LANES):
        at = TAIL + c * strata_dev
        extra[at : at + strata_dev, :] = cent[:, c * LANES : (c + 1) * LANES]
    extra[:TAIL, :] = jnp.concatenate(
        [
            jnp.broadcast_to(ids[:, i * LANES : (i + 1) * LANES], (TAIL // 4, LANES))
            for i in range(rows // LANES)
        ],
        axis=0,
    ).astype(jnp.bfloat16)
    half = lax.axis_index("grp") % 2
    pack_into(ids, loads[1:], rows_ref, outs, held, pick, cap, strata_dev, half)


def far_kernel(chips, cap, strata_dev, extra, rows_ref, *rest):
    in_a = lax.axis_index("grp") % 2 == lax.axis_index("blk") // chips
    packs = jnp.logical_or(in_a, is_inner(chips))
    own, outs, (held, pick) = rest[: chips - 1], rest[chips - 1 : -2], rest[-2:]

    @pl.when(packs)
    def _():
        spread = extra[:TAIL, :].astype(jnp.float32)
        ids = jnp.concatenate([spread[i : i + 1, :] for i in range(0, TAIL, TAIL // 4)], axis=1)
        half = lax.axis_index("blk") // chips
        pack_into(ids, [], rows_ref, outs, held, pick, cap, strata_dev, half)

    @pl.when(jnp.logical_not(packs))
    def _():
        for block, out in zip(own, outs[1:]):
            out[...] = block[: out.shape[0], :]


def unpack(blocks, cap, strata_dev, units, id_col, other=None, use_other=None):
    each = len(blocks) * cap
    width = units.shape[1]
    depth = width // LANES * 2 * cap

    def lay(i, block):
        for r in range(2):
            at = r * each + i * cap
            for c in range(width // LANES):
                units[at : at + cap, c * LANES : (c + 1) * LANES] = block[
                    (2 * c + r) * cap : (2 * c + r + 1) * cap, :
                ]

    id_rows = [[], []]
    for i, block in enumerate(blocks):
        tail = block[depth : depth + TAIL, :].astype(jnp.float32)
        if i == 0 and other is not None:
            pl.when(use_other)(lambda: lay(0, other))
            pl.when(jnp.logical_not(use_other))(lambda: lay(0, blocks[0]))
            tail = jnp.where(
                jnp.broadcast_to(use_other.astype(jnp.int32), tail.shape) > 0,
                other[depth : depth + TAIL, :].astype(jnp.float32),
                tail,
            )
        else:
            lay(i, block)
        for r in range(2):
            at = r * each + i * cap
            ids = tail[8 * r : 8 * r + 1, :]
            ids = jnp.where(ids < float(strata_dev), ids, -1.0)
            id_rows[r].append(ids[:, :cap])
            id_col[at : at + cap, :] = jnp.broadcast_to(ids, (LANES, LANES)).T[:cap, :]
    return [jnp.concatenate(rows, axis=1) for rows in id_rows]


def masked_exp(scores, id_col, id_key):
    same = jnp.concatenate([id_col] * (scores.shape[1] // LANES), axis=1) == id_key
    return jnp.where(same, jnp.exp((scores - 1.0) * 4.0), 0.0)


def fold(kernel):
    rows, lanes = kernel.shape
    return jnp.sum(kernel.reshape(rows // 8, 8, lanes), axis=0)


def key_of(id_row):
    return jnp.where(id_row >= 0.0, id_row, -2.0)


def own_centroid(near, id_row):
    which = lax.broadcasted_iota(jnp.int32, near.shape, 0).astype(jnp.float32)
    return jnp.sum(jnp.where(which == id_row, near, 0.0), axis=0, keepdims=True)


def transposed_sum(kernel):
    part = kernel[:, :LANES]
    for c in range(1, kernel.shape[1] // LANES):
        part = part + kernel[:, c * LANES : (c + 1) * LANES]
    return jnp.concatenate(
        [
            jnp.sum(part[i * LANES : (i + 1) * LANES, :].T, axis=0, keepdims=True)
            for i in range(part.shape[0] // LANES)
        ],
        axis=1,
    )


def join(groups, units, id_col, ids, cents=None):
    earlier, new, picked = [[] for _ in groups], [], []
    for r, row in enumerate(ids):
        key = key_of(row)
        each = row.shape[1]
        mine = units[r * each : (r + 1) * each, :]
        left = mine
        if cents is not None:
            strata_dev = cents.shape[0] // 2
            left = jnp.concatenate([mine, cents[r * strata_dev : (r + 1) * strata_dev, :]], axis=0)
        scores = across(left, mine)
        if cents is not None:
            picked.append(own_centroid(scores[each:, :], row))
        sums = fold(masked_exp(scores[:each, :], id_col[r * each : (r + 1) * each, :], key))
        for sums_of, (old_units, old_col, old_density) in zip(earlier, groups):
            size = old_density[r].shape[1]
            at = slice(r * size, (r + 1) * size)
            kernel = masked_exp(across(old_units[at, :], mine), old_col[at, :], key)
            sums = sums + fold(kernel)
            sums_of.append(old_density[r] + transposed_sum(kernel))
        new.append(jnp.sum(sums, axis=0, keepdims=True))
    return earlier, new, picked


def parts_of(value):
    high = value.astype(jnp.bfloat16).astype(jnp.float32)
    middle = (value - high).astype(jnp.bfloat16).astype(jnp.float32)
    return [high, middle, value - high - middle]


def in_a(chips):
    return lax.axis_index("grp") % 2 == lax.axis_index("blk") // chips


def first_kernel(chips, cap, strata_dev, after, *rest):
    blocks, (held, id_col, facts) = rest[:-3], rest[-3:]

    @pl.when(in_a(chips))
    def _():
        width = held.shape[1]
        size = len(blocks) * cap
        depth = width // LANES * 2 * cap + TAIL
        ids = unpack(blocks, cap, strata_dev, held, id_col)
        for c in range(width // LANES):
            at = depth + c * strata_dev
            held[2 * size :, c * LANES : (c + 1) * LANES] = blocks[0][at : at + strata_dev, :]
        _, density, _ = join([], held, id_col, ids)
        for r, row in enumerate(ids):
            facts[r : r + 1, :] = density[r]
            facts[2 + r : 3 + r, :] = row


def second_kernel(chips, cap, strata_dev, old_units, old_col, old_facts, *rest):
    blocks, (held, id_col) = rest[:-2], rest[-2:]

    @pl.when(in_a(chips))
    def _():
        size = len(blocks) * cap
        ids = unpack(blocks, cap, strata_dev, held, id_col)
        old = [old_facts[r : r + 1, :] for r in range(2)]
        (earlier,), density, _ = join([(old_units, old_col, old)], held, id_col, ids)
        rows = []
        for r in range(2):
            rows += parts_of(jnp.concatenate([earlier[r], density[r]], axis=1))
        for r in range(2):
            rows.append(jnp.concatenate([old_facts[2 + r : 3 + r, :], ids[r]], axis=1))
        held[2 * size :, : chips * cap] = jnp.concatenate(rows + rows, axis=0).astype(jnp.bfloat16)


def mid_kernel(chips, cap, first_a, second_a, extra, *rest):
    kept, blocks, outs = rest[0], rest[1:-7], rest[-7:]
    units, id_col, facts, facts_a, col_first, col_second, cents = outs
    inner = is_inner(chips)
    strata_dev, width = cents.shape[0] // 2, cents.shape[1]
    depth = width // LANES * 2 * cap + TAIL
    each, size = chips * cap, chips // 2 * cap

    def place(block, base):
        for c in range(width // LANES):
            at = base + c * strata_dev
            cents[strata_dev:, c * LANES : (c + 1) * LANES] = block[at : at + strata_dev, :]

    cents[:strata_dev, :] = first_a[2 * size :, :]
    pl.when(inner)(lambda: place(extra, TAIL))
    pl.when(jnp.logical_not(inner))(lambda: place(blocks[0], depth))
    tail = second_a[2 * size :, :each].astype(jnp.float32)
    groups = [(first_a, col_first, []), (second_a, col_second, [])]
    for r in range(2):
        density = tail[3 * r : 3 * r + 1, :] + tail[3 * r + 1 : 3 * r + 2, :]
        density = density + tail[3 * r + 2 : 3 * r + 3, :]
        facts_a[2 + r : 3 + r, :] = tail[6 + r : 7 + r, :]
        near = cents[r * strata_dev : (r + 1) * strata_dev, :]
        at = slice(r * size, (r + 1) * size)
        for i, (some, col, densities) in enumerate(groups):
            lanes = slice(i * size, (i + 1) * size)
            row = tail[6 + r : 7 + r, lanes]
            col[at, :] = upright(row)
            densities.append(density[:, lanes])
            facts_a[4 + r : 5 + r, lanes] = own_centroid(across(near, some[at, :]), row)
    ids = unpack(blocks, cap, strata_dev, units, id_col, kept, inner)
    old, density, picked = join(groups, units, id_col, ids, cents)
    for r, row in enumerate(ids):
        facts[r : r + 1, :] = density[r]
        facts[2 + r : 3 + r, :] = row
        facts[4 + r : 5 + r, :] = picked[r]
        for i in range(2):
            facts_a[r : r + 1, i * size : (i + 1) * size] = old[i][r]


def upright(row):
    return jnp.concatenate(
        [
            jnp.broadcast_to(row[:, i * LANES : (i + 1) * LANES], (LANES, LANES)).T
            for i in range(row.shape[1] // LANES)
        ],
        axis=0,
    )


def late_kernel(
    order, cap, groups, first_a, second_a, col_first, col_second, facts_a, units_m, col_m, facts_m, cents, *rest
):
    blocks, (out_ref, units, id_col) = rest[:-3], rest[-3:]
    strata_dev = cents.shape[0] // 2
    chips = len(order) // 2
    me, group = lax.axis_index("blk"), lax.axis_index("grp")
    at_work = (me // chips) != (group % 2)
    ids = unpack(blocks, cap, strata_dev, units, id_col)
    size = chips // 2 * cap
    old = [
        (some, col, [facts_a[r : r + 1, i * size : (i + 1) * size] for r in range(2)])
        for i, (some, col) in enumerate(((first_a, col_first), (second_a, col_second)))
    ]
    old.append((units_m, col_m, [facts_m[r : r + 1, :] for r in range(2)]))
    earlier, density, picked_new = join(old, units, id_col, ids, cents)
    total = jnp.zeros((1, 1), jnp.float32)
    weights = []
    for r, row in enumerate(ids):
        states = [
            (
                facts_a[2 + r : 3 + r, :],
                facts_a[4 + r : 5 + r, :],
                jnp.concatenate([earlier[0][r], earlier[1][r]], axis=1),
            ),
            (facts_m[2 + r : 3 + r, :], facts_m[4 + r : 5 + r, :], earlier[2][r]),
            (row, picked_new[r], density[r]),
        ]
        row, picked, dense = [jnp.concatenate(parts, axis=1) for parts in zip(*states)]
        real = row >= 0.0
        weight = jnp.where(
            real, ((1.0 - picked) + base_term) / jnp.where(real, dense, 1.0), 0.0
        )
        total = total + jnp.sum(weight, axis=1, keepdims=True)
        weights.append(weight)
    out_ref[...] = jnp.broadcast_to(jnp.where(at_work, total, 0.0), out_ref.shape)
    for r in range(2):
        for i in range(2 * chips):
            source = me ^ order[i]
            at = 4 * (source * groups + (group ^ 1)) + r
            out_ref[pl.ds(at, 1), :cap] = weights[r][:, i * cap : (i + 1) * cap]


def finish_kernel(chips, cap, groups, strata_dev, ids_ref, got_ref, out_ref):
    rows = ids_ref.shape[1]
    group = lax.axis_index("grp")
    half = group % 2
    got = got_ref[...]
    row_of = lax.broadcasted_iota(jnp.int32, got.shape, 0) % 4
    total = jnp.sum(jnp.where(row_of == 2, got, 0.0), axis=0, keepdims=True)[:, :1]
    ids = ids_ref[...]
    weight = jnp.zeros((1, rows), jnp.float32)
    for i in range(chips):
        owner = (half * chips + i) * groups + (group ^ 1)
        for r in range(2):
            shard = (half * chips + i) ^ (r * (chips + chips // 2))
            begin = jnp.sum((ids < shard * strata_dev).astype(jnp.int32))
            start = jnp.minimum(begin, rows - cap)
            part = got_ref[pl.ds(4 * owner + r, 1), :]
            part = jnp.broadcast_to(jnp.concatenate([part] * (rows // LANES), axis=1), (8, rows))
            part = pltpu.roll(part, start, axis=1)[:1, :]
            mine = (ids >= shard * strata_dev) & (ids < (shard + 1) * strata_dev)
            weight = jnp.where(mine, part, weight)
    out_ref[...] = weight * (float(rows * 2 * chips * groups) / total)


def body(embeddings, strata, centroids):
    shards, groups = lax.axis_size("blk"), lax.axis_size("grp")
    chips = shards // 2
    rows, width = embeddings.shape[1:]
    strata_dev = centroids.shape[1]
    cap = 2 * rows // shards
    chunks = width // LANES
    depth = chunks * 2 * cap + TAIL
    each = chips * cap
    every = [(b, g) for b in range(shards) for g in range(groups)]
    kind_a = [(b, g) for b, g in every if b // chips == g % 2]
    kind_b = [(b, g) for b, g in every if b // chips != g % 2]
    inner = [(b, g) for b, g in kind_b if b % chips // (chips // 2) != b // chips]
    outer = [(b, g) for b, g in kind_b if (b, g) not in inner]
    side = chips // 2
    flip = chips + side

    def send(array, pairs):
        return lax.ppermute(
            array, AXES, [(b * groups + g, to_b * groups + to_g) for (b, g), (to_b, to_g) in pairs]
        )

    def shape(*dims, dtype=jnp.bfloat16):
        return pltpu.VMEM(dims, dtype)

    held = [pltpu.VMEM((rows, width), jnp.bfloat16), pltpu.VMEM((shards * cap, rows), jnp.bfloat16)]
    swap = [((b, g), (b ^ flip, g ^ 1)) for b, g in inner]
    swap += [((b, g), (b ^ side, g)) for b, g in kind_a]
    far_rows = send(embeddings[0], swap)
    *near, extra = pl.pallas_call(
        functools.partial(near_kernel, chips, cap),
        out_shape=[
            shape(depth + (chunks * strata_dev if d in (0, side) else 0), LANES) for d in range(chips)
        ]
        + [shape(TAIL + chunks * strata_dev, LANES)],
        in_specs=[ANY, VMEM, ANY],
        out_specs=[VMEM] * (chips + 1),
        scratch_shapes=[
            pltpu.VMEM((rows, width), jnp.bfloat16),
            pltpu.VMEM((1, rows), jnp.int32),
            *held,
            pltpu.SemaphoreType.DMA((5,)),
        ],
        compiler_params=params(56),
        cost_estimate=pl.CostEstimate(flops=0, transcendentals=0, bytes_accessed=0),
        name="near",
    )(strata, centroids[0], embeddings[0])
    blocks_a = [
        near[e] if e == 0 else send(near[e], [((b, g), (b ^ e, g)) for b, g in kind_a])
        for e in range(side)
    ]
    extra = send(extra, swap)
    out = pl.pallas_call(
        functools.partial(far_kernel, chips, cap, strata_dev),
        out_shape=[shape(depth, LANES)] * chips,
        in_specs=[VMEM] * (chips + 1),
        out_specs=[VMEM] * chips,
        scratch_shapes=held,
        compiler_params=params(20),
        name="far",
    )(extra, far_rows, *near[side + 1 :], *near[:side])
    block, _ = lax.optimization_barrier((near[side], out[0]))
    first = [send(block, [((b, g), (b ^ flip, g ^ 1)) for b, g in outer])]
    for e in range(1, side):
        first.append(
            send(
                out[e],
                [((b, g), (b ^ (flip + e), g ^ 1)) for b, g in outer]
                + [((b, g), (b ^ e, g)) for b, g in inner],
            )
        )
    blocks_a.append(out[0])
    for e in range(1, side):
        blocks_a.append(send(out[e], [((b, g), (b ^ e, g)) for b, g in kind_a]))
    size = side * cap
    first_a, first_col, first_facts = pl.pallas_call(
        functools.partial(first_kernel, chips, cap, strata_dev),
        out_shape=[
            shape(2 * size + strata_dev, width),
            shape(2 * size, LANES, dtype=jnp.float32),
            shape(8, size, dtype=jnp.float32),
        ],
        in_specs=[ANY] + [VMEM] * side,
        out_specs=[VMEM] * 3,
        compiler_params=params(20),
        name="first",
    )(out[0], *blocks_a[:side])
    second_a = pl.pallas_call(
        functools.partial(second_kernel, chips, cap, strata_dev),
        out_shape=shape(2 * size + TAIL, width),
        in_specs=[VMEM] * (3 + side),
        out_specs=VMEM,
        scratch_shapes=[pltpu.VMEM((2 * size, LANES), jnp.float32)],
        compiler_params=params(20),
        name="second",
    )(first_a, first_col, first_facts, *blocks_a[side:])
    over = [((b, g), (b, g ^ 1)) for b, g in kind_a]
    first_a, second_a = send(first_a, over), send(second_a, over)
    last = []
    for e in range(side):
        block = out[side + e]
        if e == side - 1:
            block, _ = lax.optimization_barrier((block, first_a))
        last.append(
            send(
                block,
                [((b, g), (b ^ (chips + e), g ^ 1)) for b, g in outer]
                + [((b, g), (b ^ (side + e), g)) for b, g in inner],
            )
        )
    units_m, col_m, facts_m, facts_a, col_first, col_second, cents = pl.pallas_call(
        functools.partial(mid_kernel, chips, cap),
        out_shape=[
            shape(2 * side * cap, width),
            shape(2 * side * cap, LANES, dtype=jnp.float32),
            shape(8, side * cap, dtype=jnp.float32),
            shape(8, each, dtype=jnp.float32),
            shape(2 * size, LANES, dtype=jnp.float32),
            shape(2 * size, LANES, dtype=jnp.float32),
            shape(2 * strata_dev, width),
        ],
        in_specs=[VMEM] * (side + 4),
        out_specs=[VMEM] * 7,
        compiler_params=params(20),
        name="mid",
    )(first_a, second_a, extra, out[0], *first)
    sent = pl.pallas_call(
        functools.partial(
            late_kernel,
            [*range(chips), *(flip + e for e in range(side)), *(chips + e for e in range(side))],
            cap,
            groups,
        ),
        out_shape=jax.ShapeDtypeStruct((shards * groups * 4, LANES), jnp.float32),
        in_specs=[VMEM] * (9 + side),
        out_specs=VMEM,
        scratch_shapes=[
            pltpu.VMEM((2 * side * cap, width), jnp.bfloat16),
            pltpu.VMEM((2 * side * cap, LANES), jnp.float32),
        ],
        compiler_params=params(20),
        name="late",
    )(first_a, second_a, col_first, col_second, facts_a, units_m, col_m, facts_m, cents, *last)
    got = lax.all_to_all(
        sent.reshape(shards * groups, 4, LANES), AXES, 0, 0, tiled=True
    ).reshape(shards * groups * 4, LANES)
    return pl.pallas_call(
        functools.partial(finish_kernel, chips, cap, groups, strata_dev),
        out_shape=jax.ShapeDtypeStruct((1, rows), jnp.float32),
        in_specs=[VMEM, VMEM],
        out_specs=VMEM,
        compiler_params=params(8),
        name="finish",
    )(strata, got)


def solution(mesh):
    placed = (P("grp", "blk", None), P("grp", "blk"), P("grp", "blk", None))
    return jax.shard_map(
        body, mesh=mesh, in_specs=placed, out_specs=P("grp", "blk"), check_vma=False
    )
```

```python
import functools
import math

import jax
import jax.numpy as jnp
from jax import lax
from jax.experimental import pallas as pl
from jax.experimental.pallas import tpu as pltpu
from jax.sharding import PartitionSpec as P


base_term = 0.05
epsilon = 1e-06
LANES = 128
TAIL = 16
AXES = ("blk", "grp")

VMEM = pl.BlockSpec(memory_space=pltpu.VMEM)
ANY = pl.BlockSpec(memory_space=pl.ANY)


def params(mib):
    return pltpu.CompilerParams(vmem_limit_bytes=mib << 20)


def unit_values(rows):
    values = rows.astype(jnp.float32)
    mean = jnp.mean(values * values, axis=-1, keepdims=True)
    scaling = lax.rsqrt(mean + epsilon) / math.sqrt(rows.shape[-1])
    return (values * scaling).astype(jnp.bfloat16)


def across(left, right):
    return lax.dot_general(
        left, right, (((1,), (1,)), ((), ())), preferred_element_type=jnp.float32
    )


def is_inner(chips):
    me = lax.axis_index("blk")
    return (me % chips) // (chips // 2) != me // chips


def shard_of(k, chips, half):
    owner = half * chips + ((lax.axis_index("blk") % chips) ^ (k // 2))
    return owner ^ ((k % 2) * (chips + chips // 2))


def pack_into(ids, loads, rows_ref, outs, held, pick, cap, strata_dev, half):
    rows, width = rows_ref.shape
    chips = len(outs)
    shards = 2 * chips
    number = lax.broadcasted_iota(jnp.int32, (shards, 1), 0)
    lowest = (shard_of(number, chips, half) * strata_dev).astype(jnp.float32)
    begin = jnp.sum((ids < lowest).astype(jnp.float32), axis=1, keepdims=True)
    start = jnp.minimum(begin, float(rows - cap))
    number = lax.broadcasted_iota(jnp.int32, (shards * strata_dev, 1), 0)
    stratum = shard_of(number // strata_dev, chips, half) * strata_dev + number % strata_dev
    ends = jnp.sum((ids <= stratum.astype(jnp.float32)).astype(jnp.float32), axis=1, keepdims=True)
    slot = lax.broadcasted_iota(jnp.int32, (cap, rows), 0).astype(jnp.float32)
    row = lax.broadcasted_iota(jnp.int32, (cap, rows), 1).astype(jnp.float32)
    ahead = row - slot
    lane = lax.broadcasted_iota(jnp.int32, (1, LANES), 1).astype(jnp.float32)
    for k in range(shards):
        first = start[k : k + 1, :]
        pick[k * cap : (k + 1) * cap, :] = (ahead == first).astype(jnp.bfloat16)
        at = lane + first
        passed = (ends[k * strata_dev : (k + 1) * strata_dev, :] <= at).astype(jnp.float32)
        local = jnp.where(
            at >= begin[k : k + 1, :], jnp.sum(passed, axis=0, keepdims=True), float(strata_dev)
        )
        tail = width // LANES * 2 * cap + (k % 2) * 8
        outs[k // 2][tail : tail + 8, :] = jnp.broadcast_to(local, (8, LANES)).astype(jnp.bfloat16)
    step = rows // max(len(loads), 1)
    for i, load in enumerate(loads):
        load.wait()
        held[i * step : (i + 1) * step, :] = unit_values(rows_ref[i * step : (i + 1) * step, :])
    if not loads:
        held[...] = unit_values(rows_ref[...])
    wide = 2 * LANES
    for c in range(width // wide):
        runs = jnp.dot(
            pick[...], held[:, c * wide : (c + 1) * wide], preferred_element_type=jnp.float32
        ).astype(jnp.bfloat16)
        for d, out in enumerate(outs):
            for part in range(2):
                at = (2 * c + part) * 2 * cap
                out[at : at + 2 * cap, :] = runs[
                    d * 2 * cap : (d + 1) * 2 * cap, part * LANES : (part + 1) * LANES
                ]


def near_kernel(chips, cap, ids_any, cent_ref, rows_any, *rest):
    outs, (extra, rows_ref, ids_ref, held, pick, sems) = rest[:chips], rest[chips:]
    strata_dev, width = cent_ref.shape
    rows = rows_ref.shape[0]
    pieces = 4
    loads = [pltpu.make_async_copy(ids_any, ids_ref, sems.at[pieces])]
    for i in range(pieces):
        at = pl.ds(i * (rows // pieces), rows // pieces)
        loads.append(pltpu.make_async_copy(rows_any.at[at, :], rows_ref.at[at, :], sems.at[i]))
    for load in loads:
        load.start()
    cent = unit_values(cent_ref[...])
    depth = width // LANES * 2 * cap + TAIL
    for c in range(width // LANES):
        at = depth + c * strata_dev
        for out in (outs[0], outs[chips // 2]):
            out[at : at + strata_dev, :] = cent[:, c * LANES : (c + 1) * LANES]
    loads[0].wait()
    ids = ids_ref[...].astype(jnp.float32)
    for c in range(width // LANES):
        at = TAIL + c * strata_dev
        extra[at : at + strata_dev, :] = cent[:, c * LANES : (c + 1) * LANES]
    extra[:TAIL, :] = jnp.concatenate(
        [
            jnp.broadcast_to(ids[:, i * LANES : (i + 1) * LANES], (TAIL // 4, LANES))
            for i in range(rows // LANES)
        ],
        axis=0,
    ).astype(jnp.bfloat16)
    half = lax.axis_index("grp") % 2
    pack_into(ids, loads[1:], rows_ref, outs, held, pick, cap, strata_dev, half)


def far_kernel(chips, cap, strata_dev, extra, rows_ref, *rest):
    in_a = lax.axis_index("grp") % 2 == lax.axis_index("blk") // chips
    packs = jnp.logical_or(in_a, is_inner(chips))
    own, outs, (held, pick) = rest[: chips - 1], rest[chips - 1 : -2], rest[-2:]

    @pl.when(packs)
    def _():
        spread = extra[:TAIL, :].astype(jnp.float32)
        ids = jnp.concatenate([spread[i : i + 1, :] for i in range(0, TAIL, TAIL // 4)], axis=1)
        half = lax.axis_index("blk") // chips
        pack_into(ids, [], rows_ref, outs, held, pick, cap, strata_dev, half)

    @pl.when(jnp.logical_not(packs))
    def _():
        for block, out in zip(own, outs[1:]):
            out[...] = block[: out.shape[0], :]


def unpack(blocks, cap, strata_dev, units, id_col, other=None, use_other=None):
    each = len(blocks) * cap
    width = units.shape[1]
    depth = width // LANES * 2 * cap

    def lay(i, block):
        for r in range(2):
            at = r * each + i * cap
            for c in range(width // LANES):
                units[at : at + cap, c * LANES : (c + 1) * LANES] = block[
                    (2 * c + r) * cap : (2 * c + r + 1) * cap, :
                ]

    id_rows = [[], []]
    for i, block in enumerate(blocks):
        tail = block[depth : depth + TAIL, :].astype(jnp.float32)
        if i == 0 and other is not None:
            pl.when(use_other)(lambda: lay(0, other))
            pl.when(jnp.logical_not(use_other))(lambda: lay(0, blocks[0]))
            tail = jnp.where(
                jnp.broadcast_to(use_other.astype(jnp.int32), tail.shape) > 0,
                other[depth : depth + TAIL, :].astype(jnp.float32),
                tail,
            )
        else:
            lay(i, block)
        for r in range(2):
            at = r * each + i * cap
            ids = tail[8 * r : 8 * r + 1, :]
            ids = jnp.where(ids < float(strata_dev), ids, -1.0)
            id_rows[r].append(ids[:, :cap])
            id_col[at : at + cap, :] = jnp.broadcast_to(ids, (LANES, LANES)).T[:cap, :]
    return [jnp.concatenate(rows, axis=1) for rows in id_rows]


def masked_exp(scores, id_col, id_key):
    same = jnp.concatenate([id_col] * (scores.shape[1] // LANES), axis=1) == id_key
    return jnp.where(same, jnp.exp((scores - 1.0) * 4.0), 0.0)


def fold(kernel):
    rows, lanes = kernel.shape
    return jnp.sum(kernel.reshape(rows // 8, 8, lanes), axis=0)


def key_of(id_row):
    return jnp.where(id_row >= 0.0, id_row, -2.0)


def own_centroid(near, id_row):
    which = lax.broadcasted_iota(jnp.int32, near.shape, 0).astype(jnp.float32)
    return jnp.sum(jnp.where(which == id_row, near, 0.0), axis=0, keepdims=True)


def transposed_sum(kernel):
    part = kernel[:, :LANES]
    for c in range(1, kernel.shape[1] // LANES):
        part = part + kernel[:, c * LANES : (c + 1) * LANES]
    return jnp.concatenate(
        [
            jnp.sum(part[i * LANES : (i + 1) * LANES, :].T, axis=0, keepdims=True)
            for i in range(part.shape[0] // LANES)
        ],
        axis=1,
    )


def join(groups, units, id_col, ids, cents=None):
    earlier, new, picked = [[] for _ in groups], [], []
    for r, row in enumerate(ids):
        key = key_of(row)
        each = row.shape[1]
        mine = units[r * each : (r + 1) * each, :]
        left = mine
        if cents is not None:
            strata_dev = cents.shape[0] // 2
            left = jnp.concatenate([mine, cents[r * strata_dev : (r + 1) * strata_dev, :]], axis=0)
        scores = across(left, mine)
        if cents is not None:
            picked.append(own_centroid(scores[each:, :], row))
        sums = fold(masked_exp(scores[:each, :], id_col[r * each : (r + 1) * each, :], key))
        for sums_of, (old_units, old_col, old_density) in zip(earlier, groups):
            size = old_density[r].shape[1]
            at = slice(r * size, (r + 1) * size)
            kernel = masked_exp(across(old_units[at, :], mine), old_col[at, :], key)
            sums = sums + fold(kernel)
            sums_of.append(old_density[r] + transposed_sum(kernel))
        new.append(jnp.sum(sums, axis=0, keepdims=True))
    return earlier, new, picked


def parts_of(value):
    high = value.astype(jnp.bfloat16).astype(jnp.float32)
    middle = (value - high).astype(jnp.bfloat16).astype(jnp.float32)
    return [high, middle, value - high - middle]


def in_a(chips):
    return lax.axis_index("grp") % 2 == lax.axis_index("blk") // chips


def first_kernel(chips, cap, strata_dev, after, *rest):
    blocks, (held, id_col, facts) = rest[:-3], rest[-3:]

    @pl.when(in_a(chips))
    def _():
        width = held.shape[1]
        size = len(blocks) * cap
        depth = width // LANES * 2 * cap + TAIL
        ids = unpack(blocks, cap, strata_dev, held, id_col)
        for c in range(width // LANES):
            at = depth + c * strata_dev
            held[2 * size :, c * LANES : (c + 1) * LANES] = blocks[0][at : at + strata_dev, :]
        _, density, _ = join([], held, id_col, ids)
        for r, row in enumerate(ids):
            facts[r : r + 1, :] = density[r]
            facts[2 + r : 3 + r, :] = row


def second_kernel(chips, cap, strata_dev, old_units, old_col, old_facts, *rest):
    blocks, (held, id_col) = rest[:-2], rest[-2:]

    @pl.when(in_a(chips))
    def _():
        size = len(blocks) * cap
        ids = unpack(blocks, cap, strata_dev, held, id_col)
        old = [old_facts[r : r + 1, :] for r in range(2)]
        (earlier,), density, _ = join([(old_units, old_col, old)], held, id_col, ids)
        rows = []
        for r in range(2):
            rows += parts_of(jnp.concatenate([earlier[r], density[r]], axis=1))
        for r in range(2):
            rows.append(jnp.concatenate([old_facts[2 + r : 3 + r, :], ids[r]], axis=1))
        held[2 * size :, : chips * cap] = jnp.concatenate(rows + rows, axis=0).astype(jnp.bfloat16)


def mid_kernel(chips, cap, first_a, second_a, extra, *rest):
    kept, blocks, outs = rest[0], rest[1:-7], rest[-7:]
    units, id_col, facts, facts_a, col_first, col_second, cents = outs
    inner = is_inner(chips)
    strata_dev, width = cents.shape[0] // 2, cents.shape[1]
    depth = width // LANES * 2 * cap + TAIL
    each, size = chips * cap, chips // 2 * cap

    def place(block, base):
        for c in range(width // LANES):
            at = base + c * strata_dev
            cents[strata_dev:, c * LANES : (c + 1) * LANES] = block[at : at + strata_dev, :]

    cents[:strata_dev, :] = first_a[2 * size :, :]
    pl.when(inner)(lambda: place(extra, TAIL))
    pl.when(jnp.logical_not(inner))(lambda: place(blocks[0], depth))
    tail = second_a[2 * size :, :each].astype(jnp.float32)
    groups = [(first_a, col_first, []), (second_a, col_second, [])]
    for r in range(2):
        density = tail[3 * r : 3 * r + 1, :] + tail[3 * r + 1 : 3 * r + 2, :]
        density = density + tail[3 * r + 2 : 3 * r + 3, :]
        facts_a[2 + r : 3 + r, :] = tail[6 + r : 7 + r, :]
        near = cents[r * strata_dev : (r + 1) * strata_dev, :]
        at = slice(r * size, (r + 1) * size)
        for i, (some, col, densities) in enumerate(groups):
            lanes = slice(i * size, (i + 1) * size)
            row = tail[6 + r : 7 + r, lanes]
            col[at, :] = upright(row)
            densities.append(density[:, lanes])
            facts_a[4 + r : 5 + r, lanes] = own_centroid(across(near, some[at, :]), row)
    ids = unpack(blocks, cap, strata_dev, units, id_col, kept, inner)
    old, density, picked = join(groups, units, id_col, ids, cents)
    for r, row in enumerate(ids):
        facts[r : r + 1, :] = density[r]
        facts[2 + r : 3 + r, :] = row
        facts[4 + r : 5 + r, :] = picked[r]
        for i in range(2):
            facts_a[r : r + 1, i * size : (i + 1) * size] = old[i][r]


def upright(row):
    return jnp.concatenate(
        [
            jnp.broadcast_to(row[:, i * LANES : (i + 1) * LANES], (LANES, LANES)).T
            for i in range(row.shape[1] // LANES)
        ],
        axis=0,
    )


def more_kernel(cap, first_a, second_a, col_first, col_second, facts_a, units_m, col_m, facts_m, cents, *rest):
    blocks, (units, id_col, facts, facts_a_out, facts_m_out) = rest[:-5], rest[-5:]
    size = first_a.shape[0] // 2 - cents.shape[0] // 4
    old = [
        (some, col, [facts_a[r : r + 1, i * size : (i + 1) * size] for r in range(2)])
        for i, (some, col) in enumerate(((first_a, col_first), (second_a, col_second)))
    ]
    old.append((units_m, col_m, [facts_m[r : r + 1, :] for r in range(2)]))
    ids = unpack(blocks, cap, cents.shape[0] // 2, units, id_col)
    earlier, density, picked = join(old, units, id_col, ids, cents)
    facts_a_out[...] = facts_a[...]
    facts_m_out[...] = facts_m[...]
    for r, row in enumerate(ids):
        facts[r : r + 1, :] = density[r]
        facts[2 + r : 3 + r, :] = row
        facts[4 + r : 5 + r, :] = picked[r]
        facts_a_out[r : r + 1, :size] = earlier[0][r]
        facts_a_out[r : r + 1, size:] = earlier[1][r]
        facts_m_out[r : r + 1, :] = earlier[2][r]


def late_kernel(
    order, cap, groups, first_a, second_a, col_first, col_second, facts_a, units_m, col_m, facts_m, units_q, col_q, facts_q, cents, *rest
):
    blocks, (out_ref, units, id_col) = rest[:-3], rest[-3:]
    strata_dev = cents.shape[0] // 2
    chips = len(order) // 2
    me, group = lax.axis_index("blk"), lax.axis_index("grp")
    at_work = (me // chips) != (group % 2)
    ids = unpack(blocks, cap, strata_dev, units, id_col)
    size = chips // 2 * cap
    old = [
        (some, col, [facts_a[r : r + 1, i * size : (i + 1) * size] for r in range(2)])
        for i, (some, col) in enumerate(((first_a, col_first), (second_a, col_second)))
    ]
    old.append((units_m, col_m, [facts_m[r : r + 1, :] for r in range(2)]))
    old.append((units_q, col_q, [facts_q[r : r + 1, :] for r in range(2)]))
    earlier, density, picked_new = join(old, units, id_col, ids, cents)
    total = jnp.zeros((1, 1), jnp.float32)
    weights = []
    for r, row in enumerate(ids):
        states = [
            (
                facts_a[2 + r : 3 + r, :],
                facts_a[4 + r : 5 + r, :],
                jnp.concatenate([earlier[0][r], earlier[1][r]], axis=1),
            ),
            (facts_m[2 + r : 3 + r, :], facts_m[4 + r : 5 + r, :], earlier[2][r]),
            (facts_q[2 + r : 3 + r, :], facts_q[4 + r : 5 + r, :], earlier[3][r]),
            (row, picked_new[r], density[r]),
        ]
        row, picked, dense = [jnp.concatenate(parts, axis=1) for parts in zip(*states)]
        real = row >= 0.0
        weight = jnp.where(
            real, ((1.0 - picked) + base_term) / jnp.where(real, dense, 1.0), 0.0
        )
        total = total + jnp.sum(weight, axis=1, keepdims=True)
        weights.append(weight)
    out_ref[...] = jnp.broadcast_to(jnp.where(at_work, total, 0.0), out_ref.shape)
    for r in range(2):
        for i in range(2 * chips):
            source = me ^ order[i]
            at = 4 * (source * groups + (group ^ 1)) + r
            out_ref[pl.ds(at, 1), :cap] = weights[r][:, i * cap : (i + 1) * cap]


def finish_kernel(chips, cap, groups, strata_dev, ids_ref, got_ref, out_ref):
    rows = ids_ref.shape[1]
    group = lax.axis_index("grp")
    half = group % 2
    got = got_ref[...]
    row_of = lax.broadcasted_iota(jnp.int32, got.shape, 0) % 4
    total = jnp.sum(jnp.where(row_of == 2, got, 0.0), axis=0, keepdims=True)[:, :1]
    ids = ids_ref[...]
    weight = jnp.zeros((1, rows), jnp.float32)
    for i in range(chips):
        owner = (half * chips + i) * groups + (group ^ 1)
        for r in range(2):
            shard = (half * chips + i) ^ (r * (chips + chips // 2))
            begin = jnp.sum((ids < shard * strata_dev).astype(jnp.int32))
            start = jnp.minimum(begin, rows - cap)
            part = got_ref[pl.ds(4 * owner + r, 1), :]
            part = jnp.broadcast_to(jnp.concatenate([part] * (rows // LANES), axis=1), (8, rows))
            part = pltpu.roll(part, start, axis=1)[:1, :]
            mine = (ids >= shard * strata_dev) & (ids < (shard + 1) * strata_dev)
            weight = jnp.where(mine, part, weight)
    out_ref[...] = weight * (float(rows * 2 * chips * groups) / total)


def body(embeddings, strata, centroids):
    shards, groups = lax.axis_size("blk"), lax.axis_size("grp")
    chips = shards // 2
    rows, width = embeddings.shape[1:]
    strata_dev = centroids.shape[1]
    cap = 2 * rows // shards
    chunks = width // LANES
    depth = chunks * 2 * cap + TAIL
    each = chips * cap
    every = [(b, g) for b in range(shards) for g in range(groups)]
    kind_a = [(b, g) for b, g in every if b // chips == g % 2]
    kind_b = [(b, g) for b, g in every if b // chips != g % 2]
    inner = [(b, g) for b, g in kind_b if b % chips // (chips // 2) != b // chips]
    outer = [(b, g) for b, g in kind_b if (b, g) not in inner]
    side = chips // 2
    flip = chips + side

    def send(array, pairs):
        return lax.ppermute(
            array, AXES, [(b * groups + g, to_b * groups + to_g) for (b, g), (to_b, to_g) in pairs]
        )

    def shape(*dims, dtype=jnp.bfloat16):
        return pltpu.VMEM(dims, dtype)

    held = [pltpu.VMEM((rows, width), jnp.bfloat16), pltpu.VMEM((shards * cap, rows), jnp.bfloat16)]
    swap = [((b, g), (b ^ flip, g ^ 1)) for b, g in inner]
    swap += [((b, g), (b ^ side, g)) for b, g in kind_a]
    far_rows = send(embeddings[0], swap)
    *near, extra = pl.pallas_call(
        functools.partial(near_kernel, chips, cap),
        out_shape=[
            shape(depth + (chunks * strata_dev if d in (0, side) else 0), LANES) for d in range(chips)
        ]
        + [shape(TAIL + chunks * strata_dev, LANES)],
        in_specs=[ANY, VMEM, ANY],
        out_specs=[VMEM] * (chips + 1),
        scratch_shapes=[
            pltpu.VMEM((rows, width), jnp.bfloat16),
            pltpu.VMEM((1, rows), jnp.int32),
            *held,
            pltpu.SemaphoreType.DMA((5,)),
        ],
        compiler_params=params(56),
        cost_estimate=pl.CostEstimate(flops=0, transcendentals=0, bytes_accessed=0),
        name="near",
    )(strata, centroids[0], embeddings[0])
    blocks_a = [
        near[e] if e == 0 else send(near[e], [((b, g), (b ^ e, g)) for b, g in kind_a])
        for e in range(side)
    ]
    extra = send(extra, swap)
    out = pl.pallas_call(
        functools.partial(far_kernel, chips, cap, strata_dev),
        out_shape=[shape(depth, LANES)] * chips,
        in_specs=[VMEM] * (chips + 1),
        out_specs=[VMEM] * chips,
        scratch_shapes=held,
        compiler_params=params(20),
        name="far",
    )(extra, far_rows, *near[side + 1 :], *near[:side])
    block, _ = lax.optimization_barrier((near[side], out[0]))
    first = [send(block, [((b, g), (b ^ flip, g ^ 1)) for b, g in outer])]
    for e in range(1, side):
        first.append(
            send(
                out[e],
                [((b, g), (b ^ (flip + e), g ^ 1)) for b, g in outer]
                + [((b, g), (b ^ e, g)) for b, g in inner],
            )
        )
    blocks_a.append(out[0])
    for e in range(1, side):
        blocks_a.append(send(out[e], [((b, g), (b ^ e, g)) for b, g in kind_a]))
    size = side * cap
    first_a, first_col, first_facts = pl.pallas_call(
        functools.partial(first_kernel, chips, cap, strata_dev),
        out_shape=[
            shape(2 * size + strata_dev, width),
            shape(2 * size, LANES, dtype=jnp.float32),
            shape(8, size, dtype=jnp.float32),
        ],
        in_specs=[ANY] + [VMEM] * side,
        out_specs=[VMEM] * 3,
        compiler_params=params(20),
        name="first",
    )(out[0], *blocks_a[:side])
    second_a = pl.pallas_call(
        functools.partial(second_kernel, chips, cap, strata_dev),
        out_shape=shape(2 * size + TAIL, width),
        in_specs=[VMEM] * (3 + side),
        out_specs=VMEM,
        scratch_shapes=[pltpu.VMEM((2 * size, LANES), jnp.float32)],
        compiler_params=params(20),
        name="second",
    )(first_a, first_col, first_facts, *blocks_a[side:])
    over = [((b, g), (b, g ^ 1)) for b, g in kind_a]
    first_a, second_a = send(first_a, over), send(second_a, over)
    last = []
    for e in range(side):
        block = out[side + e]
        if e == side - 1:
            block, _ = lax.optimization_barrier((block, first_a))
        last.append(
            send(
                block,
                [((b, g), (b ^ (chips + e), g ^ 1)) for b, g in outer]
                + [((b, g), (b ^ (side + e), g)) for b, g in inner],
            )
        )
    units_m, col_m, facts_m, facts_a, col_first, col_second, cents = pl.pallas_call(
        functools.partial(mid_kernel, chips, cap),
        out_shape=[
            shape(2 * side * cap, width),
            shape(2 * side * cap, LANES, dtype=jnp.float32),
            shape(8, side * cap, dtype=jnp.float32),
            shape(8, each, dtype=jnp.float32),
            shape(2 * size, LANES, dtype=jnp.float32),
            shape(2 * size, LANES, dtype=jnp.float32),
            shape(2 * strata_dev, width),
        ],
        in_specs=[VMEM] * (side + 4),
        out_specs=[VMEM] * 7,
        compiler_params=params(20),
        name="mid",
    )(first_a, second_a, extra, out[0], *first)
    final = LANES // cap
    some = side - final
    known = (first_a, second_a, col_first, col_second)
    units_q, col_q, facts_q, facts_a, facts_m = pl.pallas_call(
        functools.partial(more_kernel, cap),
        out_shape=[
            shape(2 * some * cap, width),
            shape(2 * some * cap, LANES, dtype=jnp.float32),
            shape(8, some * cap, dtype=jnp.float32),
            shape(8, each, dtype=jnp.float32),
            shape(8, size, dtype=jnp.float32),
        ],
        in_specs=[VMEM] * (9 + some),
        out_specs=[VMEM] * 5,
        compiler_params=params(20),
        name="more",
    )(*known, facts_a, units_m, col_m, facts_m, cents, *last[:some])
    sent = pl.pallas_call(
        functools.partial(
            late_kernel,
            [*range(chips), *(flip + e for e in range(side)), *(chips + e for e in range(side))],
            cap,
            groups,
        ),
        out_shape=jax.ShapeDtypeStruct((shards * groups * 4, LANES), jnp.float32),
        in_specs=[VMEM] * (12 + final),
        out_specs=VMEM,
        scratch_shapes=[
            pltpu.VMEM((2 * final * cap, width), jnp.bfloat16),
            pltpu.VMEM((2 * final * cap, LANES), jnp.float32),
        ],
        compiler_params=params(20),
        name="late",
    )(*known, facts_a, units_m, col_m, facts_m, units_q, col_q, facts_q, cents, *last[some:])
    got = lax.all_to_all(
        sent.reshape(shards * groups, 4, LANES), AXES, 0, 0, tiled=True
    ).reshape(shards * groups * 4, LANES)
    return pl.pallas_call(
        functools.partial(finish_kernel, chips, cap, groups, strata_dev),
        out_shape=jax.ShapeDtypeStruct((1, rows), jnp.float32),
        in_specs=[VMEM, VMEM],
        out_specs=VMEM,
        compiler_params=params(8),
        name="finish",
    )(strata, got)


def solution(mesh):
    placed = (P("grp", "blk", None), P("grp", "blk"), P("grp", "blk", None))
    return jax.shard_map(
        body, mesh=mesh, in_specs=placed, out_specs=P("grp", "blk"), check_vma=False
    )
```
